32 devices in a mesh: dp: 4 (over y, x), fsdp: 8 (over z, core).
Axes of the slice: x: 2, y: 2, z: 4, core: 2. Of those that a mesh axis runs over, the one named last changes fastest.
Arguments:
- tokens: bfloat16 [32768, 768], P(('dp', 'fsdp')), may hold values from -6 to 6
- cotangent: bfloat16 [32768, 768], P(('dp', 'fsdp')), may hold values from -6 to 6
- doc_lengths: int32 [64, 8], P(('dp', 'fsdp')), may hold values from 1 to 160, 512 in all within a row
- w_query: bfloat16 [768, 768], P('fsdp'), may hold values from -0.21875 to 0.21875
- w_key: bfloat16 [768, 768], P('fsdp'), may hold values from -0.21875 to 0.21875
- w_value: bfloat16 [768, 768], P('fsdp'), may hold values from -0.21875 to 0.21875
- w_out: bfloat16 [768, 768], P('fsdp'), may hold values from -0.625 to 0.625
- w_up: bfloat16 [768, 3072], P('fsdp'), may hold values from -0.21875 to 0.21875
- w_down: bfloat16 [3072, 768], P('fsdp'), may hold values from -0.109375 to 0.109375
- pre_gain: bfloat16 [768], P('fsdp'), may hold values from 0.25 to 1.75
- pre_shift: bfloat16 [768], P('fsdp'), may hold values from -1.5 to 1.5
- bias_query: bfloat16 [768], P('fsdp'), may hold values from -2.5 to 2.5
- bias_value: bfloat16 [768], P('fsdp'), may hold values from -2.5 to 2.5
- bias_out: bfloat16 [768], P('fsdp'), may hold values from -2.5 to 2.5
- mid_gain: bfloat16 [768], P('fsdp'), may hold values from 0.25 to 1.75
- mid_shift: bfloat16 [768], P('fsdp'), may hold values from -1.5 to 1.5
- bias_up: bfloat16 [3072], P('fsdp'), may hold values from -2.5 to 2.5
- bias_down: bfloat16 [768], P('fsdp'), may hold values from -1.5 to 1.5
Outputs:
- layer_out: bfloat16 [32768, 768], P(('dp', 'fsdp'))
- input_grad: bfloat16 [32768, 768], P(('dp', 'fsdp'))
- w_query_grad: float32 [768, 768], P('fsdp')
- w_key_grad: float32 [768, 768], P('fsdp')
- w_value_grad: float32 [768, 768], P('fsdp')
- w_out_grad: float32 [768, 768], P('fsdp')
- w_up_grad: float32 [768, 3072], P('fsdp')
- w_down_grad: float32 [3072, 768], P('fsdp')
- pre_gain_grad: float32 [768], P('fsdp')
- pre_shift_grad: float32 [768], P('fsdp')
- bias_query_grad: float32 [768], P('fsdp')
- bias_value_grad: float32 [768], P('fsdp')
- bias_out_grad: float32 [768], P('fsdp')
- mid_gain_grad: float32 [768], P('fsdp')
- mid_shift_grad: float32 [768], P('fsdp')
- bias_up_grad: float32 [3072], P('fsdp')
- bias_down_grad: float32 [768], P('fsdp')
The draws below stay inside these ranges and needn't reach their ends.
Inputs may be any that keep to these rules, and one draw needn't show every extreme that they name: `doc_lengths`: each row sums to 512; the largest entry of every row is exactly 160.
All inputs are finite; a program needn't handle non-finite values.
Results may differ from the reference program's by a relative error of at most 0.015.
Values may be sent and summed in bfloat16 or wider, within the bound.
No kernel may reach another device: no remote copies, remote signals or barrier semaphores. Data moves between devices by JAX's collectives and lax.ppermute only.
A program may use at most 256 MiB of HBM per device.

```python
import math
import jax
import jax.numpy as jnp
import numpy as np
from jax import lax

D = 768
H = 12
HD = 64
FF = 3072
SEQ = 512
DOCS = 8
MOST = 160
SEQS = 64
TOKENS = 32768


def block_scale(own_key, shape, shards, least, top_value):
    def one(dim, parts):
        draws = jax.random.uniform(jax.random.fold_in(jax.random.fold_in(own_key, 6), dim), (parts,), jnp.float32, least / len(shards), top_value / len(shards))
        return jnp.repeat(jnp.exp(draws), shape[dim] // parts).reshape((-1,) + (1,) * (len(shape) - dim - 1))

    factor_of = one(*shards[0])
    for cut in shards[1:]:
        factor_of = factor_of * one(*cut)
    return factor_of


def split_up(count, total, bound, slope):
    loads = [(1 << 20) // math.isqrt(grade ** slope) + 1 for grade in range(2, count + 1)]
    spare, counts = total - bound - (count - 1), [1] * (count - 1)
    while spare > 0:
        free = [i for i in range(count - 1) if counts[i] < bound]
        whole, budget = sum([loads[i] for i in free]), spare
        for i in free:
            extra = min(bound - counts[i], max(1, budget * loads[i] // whole), spare)
            counts[i] = counts[i] + extra
            spare = spare - extra
    return np.array([bound] + counts)


def uneven_parts(key, count, total, bound, skew):
    if count == 2:
        one = jax.random.randint(key, (), max(1, total - bound), min(bound, total - 1) + 1)
        return jnp.stack([one, total - one])
    tallies = jnp.asarray(split_up(count, total, bound, skew), jnp.int32)
    twos = (count - 1) // 2
    giver, taker = tallies[1:1 + 2 * twos:2], tallies[2:2 + 2 * twos:2]
    room = jnp.minimum(giver - 1, bound - taker)
    shifted = jax.random.randint(jax.random.fold_in(key, 1), (twos,), 0, 1 << 20) % (room + 1)
    tallies = tallies.at[1:1 + 2 * twos:2].set(giver - shifted).at[2:2 + 2 * twos:2].set(taker + shifted)
    return tallies[jax.random.permutation(jax.random.fold_in(key, 2), count)]


def normal_values(key, shape, width, most, pieces=(), kind=jnp.bfloat16):
    gain = block_scale(key, shape, pieces, -0.22, 0.18) if pieces else 1.0
    array = jax.random.normal(key, shape, jnp.float32) * width * gain
    return jnp.minimum(jnp.maximum(array, -most), most).astype(kind)


def setup_inputs(seed: int = 0) -> dict:
    key_of = jax.random.split(jax.random.key(seed), 19)
    return {
        "tokens": normal_values(key_of[0], (TOKENS, D), 1.0, 6.0, ((0, 32),)),
        "cotangent": normal_values(key_of[1], (TOKENS, D), 1.0, 6.0, ((0, 32),)),
        "doc_lengths": jax.vmap(lambda own: uneven_parts(own, DOCS, SEQ, MOST, 2))(jax.random.split(key_of[2], SEQS)).reshape((SEQS, DOCS)).astype(jnp.int32),
        "w_query": normal_values(key_of[3], (D, D), D ** -0.5, 0.21875, ((0, 8),)),
        "w_key": normal_values(key_of[4], (D, D), D ** -0.5, 0.21875, ((0, 8),)),
        "w_value": normal_values(key_of[5], (D, D), D ** -0.5, 0.21875, ((0, 8),)),
        "w_out": normal_values(key_of[6], (D, D), (D // 8) ** -0.5, 0.625, ((0, 8),)),
        "w_up": normal_values(key_of[7], (D, FF), D ** -0.5, 0.21875, ((0, 8),)),
        "w_down": normal_values(key_of[8], (FF, D), FF ** -0.5, 0.109375, ((0, 8),)),
        "pre_gain": jnp.clip(1.0 + 0.15 * jax.random.normal(key_of[9], (D,), jnp.float32), 0.25, 1.75).astype(jnp.bfloat16),
        "pre_shift": normal_values(key_of[10], (D,), 0.3, 1.5, ((0, 8),)),
        "bias_query": normal_values(key_of[11], (D,), 0.5, 2.5, ((0, 8),)),
        "bias_value": normal_values(key_of[12], (D,), 0.5, 2.5, ((0, 8),)),
        "bias_out": normal_values(key_of[13], (D,), 0.5, 2.5, ((0, 8),)),
        "mid_gain": jnp.clip(1.0 + 0.15 * jax.random.normal(key_of[14], (D,), jnp.float32), 0.25, 1.75).astype(jnp.bfloat16),
        "mid_shift": normal_values(key_of[15], (D,), 0.3, 1.5, ((0, 8),)),
        "bias_up": normal_values(key_of[16], (FF,), 0.5, 2.5, ((0, 8),)),
        "bias_down": normal_values(key_of[17], (D,), 0.3, 1.5, ((0, 8),)),
    }


@jax.custom_vjp
def low(v):
    return lax.optimization_barrier(v.astype(jnp.bfloat16)).astype(jnp.float32)

@jax.custom_vjp
def low_back(v):
    return v

def low_keep(v):
    return (low(v), None)

def low_pass(kept, grad):
    return (grad,)

def back_keep(v):
    return (v, None)

def back_low(kept, grad):
    return (low(grad),)
low.defvjp(low_keep, low_pass)
low_back.defvjp(back_keep, back_low)
epsilon = 1e-05
masked_score = -1000000000.0

def project(left, weight):
    return jnp.dot(left, weight, precision=lax.Precision.HIGHEST)

def normalize(values_in, gain_vec, shift_vec):
    row_mean = lax.optimization_barrier(jnp.mean(values_in, axis=-1, keepdims=True))
    centred = values_in - row_mean
    inverse = lax.rsqrt(lax.optimization_barrier(jnp.mean(centred * centred, axis=-1, keepdims=True)) + epsilon)
    return centred * inverse * gain_vec + shift_vec

def segment_ids(lengths, seq_len):
    ends = jnp.cumsum(lengths, axis=-1).astype(jnp.int32)
    places = jnp.arange(seq_len, dtype=jnp.int32)
    return lax.optimization_barrier(jnp.sum((places[None, :, None] >= ends[:, None, :]).astype(jnp.int32), axis=-1)).astype(jnp.int32)

def attend(inputs):
    queries, key_block, value_block, doc_ids = inputs
    head_shape = (SEQ, H, HD)
    scores = jnp.einsum('qhd,khd->hqk', queries.reshape(head_shape), key_block.reshape(head_shape), precision=lax.Precision.HIGHEST)
    scores = low_back(scores * HD ** (-0.5))
    same_doc = (doc_ids[:, None] == doc_ids[None, :])[None]
    soft_probs = low(jax.nn.softmax(jnp.where(same_doc, scores, masked_score), axis=-1))
    attended = jnp.einsum('hqk,khd->qhd', soft_probs, value_block.reshape(head_shape), precision=lax.Precision.HIGHEST)
    return attended.reshape(SEQ, H * HD)

def block_forward(layer_in, params, doc_ids):
    w_query, w_key, w_value, w_out, w_up, w_down, pre_gain, pre_shift, bias_query, bias_value, bias_out, mid_gain, mid_shift, bias_up, bias_down = params
    seq_count = doc_ids.shape[0]
    first = low(normalize(layer_in, pre_gain, pre_shift))
    queries = low(low_back(project(first, w_query) + bias_query))
    key_rows = low(low_back(project(first, w_key)))
    value_rows = low(low_back(project(first, w_value) + bias_value))
    per_seq = (seq_count, SEQ, D)
    attended = lax.map(jax.checkpoint(attend), (queries.reshape(per_seq), key_rows.reshape(per_seq), value_rows.reshape(per_seq), doc_ids))
    attended = low(low_back(attended.reshape(seq_count * SEQ, D)))
    middle = layer_in + low_back(project(attended, w_out) + bias_out)
    second = low(normalize(middle, mid_gain, mid_shift))
    hidden = low_back(project(second, w_up) + bias_up)
    active = low(jax.nn.gelu(hidden, approximate=False))
    return middle + low_back(project(active, w_down) + bias_down)

def reference(tokens, cotangent, doc_lengths, w_query, w_key, w_value, w_out, w_up, w_down, pre_gain, pre_shift, bias_query, bias_value, bias_out, mid_gain, mid_shift, bias_up, bias_down):
    params = tuple((piece.astype(jnp.float32) for piece in (w_query, w_key, w_value, w_out, w_up, w_down, pre_gain, pre_shift, bias_query, bias_value, bias_out, mid_gain, mid_shift, bias_up, bias_down)))
    per_group = 8
    group_count = SEQS // per_group
    doc_ids = segment_ids(doc_lengths, SEQ).reshape(group_count, per_group, SEQ)
    token_groups = tokens.astype(jnp.float32).reshape(group_count, per_group * SEQ, D)
    grad_groups = cotangent.astype(jnp.float32).reshape(group_count, per_group * SEQ, D)

    def group_step(totals, inputs):
        group_rows, group_grad, group_ids = inputs

        def forward(rows_in, params_in):
            return block_forward(rows_in, params_in, group_ids)
        result, pull = jax.vjp(forward, group_rows, params)
        rows_grad, params_grad = pull(group_grad)
        return (tuple((total_now + part for total_now, part in zip(totals, params_grad))), (result, rows_grad))
    zeros = tuple((jnp.zeros(piece.shape, jnp.float32) for piece in params))
    totals, (results, rows_grads) = lax.scan(group_step, zeros, (token_groups, grad_groups, doc_ids))
    factor = TOKENS ** (-0.5)
    layer_out = results.reshape(TOKENS, D).astype(jnp.bfloat16)
    input_grad = rows_grads.reshape(TOKENS, D).astype(jnp.bfloat16)
    return (layer_out, input_grad, totals[0] * factor, totals[1] * factor, totals[2] * factor, totals[3] * factor, totals[4] * factor, totals[5] * factor, totals[6] * factor, totals[7] * factor, totals[8] * factor, totals[9] * factor, totals[10] * factor, totals[11] * factor, totals[12] * factor, totals[13] * factor, totals[14] * factor)
```

```python
import jax
import jax.numpy as jnp
from jax import lax
from jax.experimental import pallas as pl
from jax.experimental.pallas import tpu as pltpu
from jax.sharding import PartitionSpec as P

H = 12
HD = 64
SEQ = 512
MOST = 160
BQ = 256
BAND = 416
epsilon = 1e-05
bf16 = jnp.bfloat16
f32 = jnp.float32


def nn(a, b):
    return jnp.dot(a, b, preferred_element_type=f32)


def nt(a, b):
    return lax.dot_general(a, b, (((1,), (1,)), ((), ())), preferred_element_type=f32)


def tn(a, b):
    return lax.dot_general(a, b, (((0,), (0,)), ((), ())), preferred_element_type=f32)


def params(n, mb=56):
    return pltpu.CompilerParams(
        dimension_semantics=("arbitrary",) * n, vmem_limit_bytes=mb * 1024 * 1024
    )


def cost(flops, nbytes, trans=0):
    return pl.CostEstimate(flops=int(flops), bytes_accessed=int(nbytes), transcendentals=int(trans))


def moments(v):
    mean = jnp.mean(v, axis=-1, keepdims=True)
    c = v - mean
    inv = lax.rsqrt(jnp.mean(c * c, axis=-1, keepdims=True) + epsilon)
    return c * inv, inv


def qkv_kernel(x_ref, w_ref, b_ref, o_ref):
    b = b_ref[0]
    for r in range(x_ref.shape[0] // 256):
        rows = pl.ds(r * 256, 256)
        o_ref[0, rows, :] = (nn(x_ref[rows, :], w_ref[0]) + b).astype(bf16)


def qkv_call(first, w, bias):
    rows, d = first.shape
    return pl.pallas_call(
        qkv_kernel,
        grid=(3,),
        in_specs=[
            pl.BlockSpec((rows, d), lambda i: (0, 0)),
            pl.BlockSpec((1, d, d), lambda i: (i, 0, 0)),
            pl.BlockSpec((1, 1, d), lambda i: (i, 0, 0)),
        ],
        out_specs=pl.BlockSpec((1, rows, d), lambda i: (i, 0, 0)),
        out_shape=jax.ShapeDtypeStruct((3, rows, d), bf16),
        compiler_params=params(1),
        cost_estimate=cost(6 * rows * d * d, 2 * (rows * d * 4 + 3 * d * d)),
        name="qkv",
    )(first, w, bias)


def spans(b):
    return b * BQ, b * (SEQ - BAND)


def attn_fwd_kernel(q_ref, k_ref, v_ref, dr_ref, dc_ref, o_ref, p_ref, bias):
    @pl.when(pl.program_id(1) == 0)
    def _():
        for b in range(2):
            q0, k0 = spans(b)
            same = dc_ref[0, k0 : k0 + BAND, :] == dr_ref[0, :, q0 : q0 + BQ]
            bias[b] = jnp.where(same, 0.0, -3e38)

    low = lax.broadcasted_iota(jnp.int32, (1, 128), 1) < HD
    for b in range(2):
        q0, k0 = spans(b)
        qb = q_ref[0, q0 : q0 + BQ, :] * bf16(HD**-0.5)
        kb = k_ref[0, k0 : k0 + BAND, :]
        vb = v_ref[0, k0 : k0 + BAND, :]
        acc = None
        for hh in range(2):
            mine = low if hh == 0 else jnp.logical_not(low)
            s = nt(kb, jnp.where(mine, qb, bf16(0))) + bias[b]
            e = jnp.exp(s - jnp.max(s, axis=0, keepdims=True))
            p = (e * (1.0 / jnp.sum(e, axis=0, keepdims=True))).astype(bf16)
            p_ref[hh, b] = p
            part = tn(jnp.where(mine, vb, bf16(0)), p)
            acc = part if acc is None else acc + part
        o_ref[q0 : q0 + BQ, :] = acc.T.astype(bf16)


def attn_fwd_call(qkv, doc):
    rows = qkv.shape[1]
    d = qkv.shape[2]
    seqs = rows // SEQ
    hp = d // 128

    def part(i):
        return pl.BlockSpec((1, SEQ, 128), lambda s, h: (i, s, h))

    return pl.pallas_call(
        attn_fwd_kernel,
        grid=(seqs, hp),
        in_specs=[
            part(0),
            part(1),
            part(2),
            pl.BlockSpec((1, 1, SEQ), lambda s, h: (s, 0, 0)),
            pl.BlockSpec((1, SEQ, 1), lambda s, h: (s, 0, 0)),
        ],
        out_specs=[
            pl.BlockSpec((SEQ, 128), lambda s, h: (s, h)),
            pl.BlockSpec((2, 2, BAND, BQ), lambda s, h: (s * hp + h, 0, 0, 0)),
        ],
        out_shape=[
            jax.ShapeDtypeStruct((rows, d), bf16),
            jax.ShapeDtypeStruct((seqs * H, 2, BAND, BQ), bf16),
        ],
        scratch_shapes=[pltpu.VMEM((2, BAND, BQ), f32)],
        compiler_params=params(2),
        cost_estimate=cost(
            seqs * H * 2 * BAND * BQ * 2 * 256, 2 * 4 * rows * d + 4 * seqs * H * BAND * BQ
        ),
        name="attend",
    )(qkv, qkv, qkv, doc[:, None, :], doc[:, :, None])


def attn_bwd_kernel(q_ref, k_ref, v_ref, do_ref, p_ref, o_ref):
    low = lax.broadcasted_iota(jnp.int32, (1, 128), 1) < HD
    scale = bf16(HD**-0.5)
    over = SEQ - BAND
    tails = []
    for b in range(2):
        q0, k0 = spans(b)
        qb = q_ref[0, q0 : q0 + BQ, :] * scale
        dob = do_ref[q0 : q0 + BQ, :]
        kb = k_ref[0, k0 : k0 + BAND, :] * scale
        vb = v_ref[0, k0 : k0 + BAND, :]
        dq = dk = dv = None
        for hh in range(2):
            mine = low if hh == 0 else jnp.logical_not(low)
            p = p_ref[hh, b]
            dom = jnp.where(mine, dob, bf16(0))
            dp = nt(vb, dom)
            pf = p.astype(f32)
            inner = jnp.sum(pf * dp, axis=0, keepdims=True)
            ds = (pf * (dp - inner)).astype(bf16)
            a = nn(p, dom)
            c = nn(ds, jnp.where(mine, qb, bf16(0)))
            g = tn(jnp.where(mine, kb, bf16(0)), ds)
            dv = a if dv is None else dv + a
            dk = c if dk is None else dk + c
            dq = g if dq is None else dq + g
        o_ref[0, q0 : q0 + BQ, :] = dq.T.astype(bf16)
        tails.append((dk, dv))
    for i, (first_part, second_part) in enumerate(zip(*tails)):
        o_ref[i + 1, :over, :] = first_part[:over].astype(bf16)
        o_ref[i + 1, over:BAND, :] = (first_part[over:] + second_part[: BAND - over]).astype(bf16)
        o_ref[i + 1, BAND:, :] = second_part[BAND - over :].astype(bf16)


def attn_bwd_call(qkv, dattn, probs):
    rows = qkv.shape[1]
    d = qkv.shape[2]
    seqs = rows // SEQ
    hp = d // 128

    def part(i):
        return pl.BlockSpec((1, SEQ, 128), lambda s, h: (i, s, h))

    return pl.pallas_call(
        attn_bwd_kernel,
        grid=(seqs, hp),
        in_specs=[
            part(0),
            part(1),
            part(2),
            pl.BlockSpec((SEQ, 128), lambda s, h: (s, h)),
            pl.BlockSpec((2, 2, BAND, BQ), lambda s, h: (s * hp + h, 0, 0, 0)),
        ],
        out_specs=pl.BlockSpec((3, SEQ, 128), lambda s, h: (0, s, h)),
        out_shape=jax.ShapeDtypeStruct((3, rows, d), bf16),
        compiler_params=params(2),
        cost_estimate=cost(
            seqs * H * 2 * BAND * BQ * 2 * 256 * 2, 2 * 7 * rows * d + 4 * seqs * H * BAND * BQ
        ),
        name="attend_back",
    )(qkv, qkv, qkv, dattn, probs)


def out_kernel(a_ref, w_ref, t_ref, bo_ref, g_ref, s_ref, bd_ref, mid_ref, sec_ref, acc_ref):
    mid = t_ref[...].astype(f32) + nn(a_ref[...], w_ref[0]) + bo_ref[...]
    mid_ref[...] = mid
    acc_ref[...] = mid + bd_ref[...]
    sc, _ = moments(mid)
    sec_ref[...] = (sc * g_ref[...] + s_ref[...]).astype(bf16)


def out_call(attended, wo, tokens, bo, gain, shift, bdown):
    rows, d = tokens.shape
    blk = pl.BlockSpec((256, d), lambda i: (i, 0))
    vec = pl.BlockSpec((1, d), lambda i: (0, 0))
    return pl.pallas_call(
        out_kernel,
        grid=(rows // 256,),
        in_specs=[blk, pl.BlockSpec((1, d, d), lambda i: (3, 0, 0)), blk, vec, vec, vec, vec],
        out_specs=[blk, blk, blk],
        out_shape=[
            jax.ShapeDtypeStruct((rows, d), f32),
            jax.ShapeDtypeStruct((rows, d), bf16),
            jax.ShapeDtypeStruct((rows, d), f32),
        ],
        compiler_params=params(1),
        cost_estimate=cost(2 * rows * d * d, rows * d * 14 + 2 * d * d),
        name="project",
    )(attended, wo, tokens, bo, gain, shift, bdown)


def ffn_kernel(
    x_ref, g_ref, w_ref, b_ref, acc_in, sg_in,
    gw_ref, gb_ref, acc_ref, sg_ref, act, hg,
):
    j = pl.program_id(0)
    rows, d = x_ref.shape
    ff = w_ref.shape[1]
    chunk = 256

    @pl.when(j == 0)
    def _():
        acc_ref[...] = acc_in[...]
        sg_ref[...] = sg_in[...]

    wu = w_ref.at[0]
    wd = w_ref.at[1]
    total = jnp.zeros((1, ff), f32)
    for r in range(rows // chunk):
        at = pl.ds(r * chunk, chunk)
        h = nn(x_ref[at, :], wu[...]) + b_ref[0]
        ag = nt(g_ref[at, :], wd[...])
        phi = 0.5 + 0.5 * lax.erf(h * (0.5**0.5))
        a = (h * phi).astype(bf16)
        act[at, :] = a
        dens = jnp.exp(-0.5 * (h * h)) * 0.3989422804014327
        hgv = (ag * (phi + h * dens)).astype(bf16)
        hg[at, :] = hgv
        total += jnp.sum(hgv.astype(f32), axis=0, keepdims=True)
        acc_ref[at, :] += nn(a, wd[...])
        sg_ref[at, :] += nt(hgv, wu[...])
    gb_ref[0] = total
    gw_ref[0] = tn(x_ref[...], hg[...]).astype(bf16)
    gw_ref[1] = tn(act[...], g_ref[...]).astype(bf16)


def ffn_call(second, dgrad, w, bu, acc, sg):
    rows, d = second.shape
    n = w.shape[0] // 2
    full = pl.BlockSpec((rows, d), lambda j: (0, 0))
    pair = pl.BlockSpec((2, d, d), lambda j: (j, 0, 0))
    vec = pl.BlockSpec((1, 1, d), lambda j: (j, 0, 0))
    return pl.pallas_call(
        ffn_kernel,
        grid=(n,),
        in_specs=[full, full, pair, vec, full, full],
        out_specs=[pair, vec, full, full],
        out_shape=[
            jax.ShapeDtypeStruct((2 * n, d, d), bf16),
            jax.ShapeDtypeStruct((n, 1, d), f32),
            jax.ShapeDtypeStruct((rows, d), f32),
            jax.ShapeDtypeStruct((rows, d), f32),
        ],
        scratch_shapes=[pltpu.VMEM((rows, d), bf16), pltpu.VMEM((rows, d), bf16)],
        input_output_aliases={4: 2, 5: 3},
        compiler_params=params(1),
        cost_estimate=cost(12 * n * rows * d * d, 20 * rows * d + 8 * n * d * d),
        name="feed",
    )(second, dgrad, w, bu, acc, sg)


def norm_back(grad, sc, inv, gain):
    t = grad * gain
    return inv * (
        t - jnp.mean(t, axis=-1, keepdims=True) - sc * jnp.mean(t * sc, axis=-1, keepdims=True)
    )


def mid_kernel(
    sg_ref, mid_ref, dy_ref, a_ref, w_ref, g_ref, acc_ref,
    mg_ref, ag_ref, wg_ref, vec_ref, lo_ref, wacc,
):
    i = pl.program_id(0)

    @pl.when(i == 0)
    def _():
        wacc[...] = jnp.zeros_like(wacc)
        vec_ref[...] = jnp.zeros_like(vec_ref)

    lo_ref[...] = acc_ref[...].astype(bf16)
    sc, inv = moments(mid_ref[...])
    sg = sg_ref[...]
    dy = dy_ref[...].astype(f32)
    mg = dy + norm_back(sg, sc, inv, g_ref[...])
    mg_ref[...] = mg
    br = mg.astype(bf16)
    vec_ref[0:1, :] += jnp.sum(sg * sc, axis=0, keepdims=True)
    vec_ref[1:2, :] += jnp.sum(sg, axis=0, keepdims=True)
    vec_ref[2:3, :] += jnp.sum(br.astype(f32), axis=0, keepdims=True)
    vec_ref[3:4, :] += jnp.sum(dy, axis=0, keepdims=True)
    ag_ref[...] = nt(br, w_ref[0]).astype(bf16)
    wacc[...] += tn(a_ref[...], br)

    @pl.when(i == pl.num_programs(0) - 1)
    def _():
        wg_ref[0] = wacc[...].astype(bf16)


def mid_call(sg, mid, dy, attended, wo, gain, acc):
    rows, d = sg.shape
    blk = pl.BlockSpec((256, d), lambda i: (i, 0))
    vec = pl.BlockSpec((1, d), lambda i: (0, 0))
    return pl.pallas_call(
        mid_kernel,
        grid=(rows // 256,),
        in_specs=[blk, blk, blk, blk, pl.BlockSpec((1, d, d), lambda i: (3, 0, 0)), vec, blk],
        out_specs=[
            blk,
            blk,
            pl.BlockSpec((1, d, d), lambda i: (0, 0, 0)),
            pl.BlockSpec((8, d), lambda i: (0, 0)),
            blk,
        ],
        out_shape=[
            jax.ShapeDtypeStruct((rows, d), f32),
            jax.ShapeDtypeStruct((rows, d), bf16),
            jax.ShapeDtypeStruct((1, d, d), bf16),
            jax.ShapeDtypeStruct((8, d), f32),
            jax.ShapeDtypeStruct((rows, d), bf16),
        ],
        scratch_shapes=[pltpu.VMEM((d, d), f32)],
        compiler_params=params(1),
        cost_estimate=cost(4 * rows * d * d, rows * d * 22 + 4 * d * d),
        name="middle_back",
    )(sg, mid, dy, attended, wo, gain, acc)


def wgrad_kernel(x_ref, g_ref, o_ref, b_ref):
    o_ref[0] = tn(x_ref[...], g_ref[0]).astype(bf16)
    b_ref[0] = jnp.sum(g_ref[0].astype(f32), axis=0, keepdims=True)


def wgrad_call(first, grads):
    rows, d = first.shape
    return pl.pallas_call(
        wgrad_kernel,
        grid=(3,),
        in_specs=[
            pl.BlockSpec((rows, d), lambda i: (0, 0)),
            pl.BlockSpec((1, rows, d), lambda i: (i, 0, 0)),
        ],
        out_specs=[
            pl.BlockSpec((1, d, d), lambda i: (i, 0, 0)),
            pl.BlockSpec((1, 1, d), lambda i: (i, 0, 0)),
        ],
        out_shape=[
            jax.ShapeDtypeStruct((3, d, d), bf16),
            jax.ShapeDtypeStruct((3, 1, d), f32),
        ],
        compiler_params=params(1),
        cost_estimate=cost(6 * rows * d * d, 2 * (rows * d * 4 + 3 * d * d)),
        name="weight_back",
    )(first, grads)


def input_kernel(g_ref, w_ref, t_ref, mg_ref, gain_ref, o_ref, vec_ref):
    i = pl.program_id(0)

    @pl.when(i == 0)
    def _():
        vec_ref[...] = jnp.zeros_like(vec_ref)

    fg = nt(g_ref[0], w_ref[0]) + nt(g_ref[1], w_ref[1]) + nt(g_ref[2], w_ref[2])
    sc, inv = moments(t_ref[...].astype(f32))
    o_ref[...] = (mg_ref[...] + norm_back(fg, sc, inv, gain_ref[...])).astype(bf16)
    vec_ref[0:1, :] += jnp.sum(fg * sc, axis=0, keepdims=True)
    vec_ref[1:2, :] += jnp.sum(fg, axis=0, keepdims=True)


def input_call(grads, w, tokens, mg, gain):
    rows, d = tokens.shape
    blk = pl.BlockSpec((256, d), lambda i: (i, 0))
    return pl.pallas_call(
        input_kernel,
        grid=(rows // 256,),
        in_specs=[
            pl.BlockSpec((3, 256, d), lambda i: (0, i, 0)),
            pl.BlockSpec((3, d, d), lambda i: (0, 0, 0)),
            blk,
            blk,
            pl.BlockSpec((1, d), lambda i: (0, 0)),
        ],
        out_specs=[blk, pl.BlockSpec((8, d), lambda i: (0, 0))],
        out_shape=[
            jax.ShapeDtypeStruct((rows, d), bf16),
            jax.ShapeDtypeStruct((8, d), f32),
        ],
        compiler_params=params(1),
        cost_estimate=cost(6 * rows * d * d, rows * d * 14 + 6 * d * d),
        name="input_back",
    )(grads, w, tokens, mg, gain)


CORE = 1
ALONG = (2, 4, 6)
GROUP = (8, 16, 24)


def hop(x, mask):
    return lax.ppermute(x, ("dp", "fsdp"), [(i, i ^ mask) for i in range(32)])


def pick(x, index):
    return lax.dynamic_index_in_dim(x, index, 0, keepdims=False)


def assemble_kernel(place, *refs):
    pieces, out, sem = refs[:-2], refs[-2], refs[-1]
    rows = out.shape[1] // 8
    d, z, c = place[0], place[1], place[2]
    copies = []
    for p in range(2):
        own, rest = pieces[5 * p], pieces[5 * p + 1 : 5 * p + 5]
        s = 2 * z + (c ^ p)
        for b in range(4):
            copies.append((own.at[b], out.at[b, pl.ds(s * rows, rows), :]))
        for m in range(4):
            for k in range(3):
                s = 2 * (z ^ (k + 1)) + (c ^ p)
                copies.append((rest[m].at[k], out.at[d ^ m, pl.ds(s * rows, rows), :]))
    copies = [pltpu.make_async_copy(a, b, sem) for a, b in copies]
    for copy in copies:
        copy.start()
    for copy in copies:
        copy.wait()


def gather_fast(local, place):
    n, rows, d = local.shape
    other = hop(local, CORE)
    mine = pick(local, place[0])
    along = jnp.stack([hop(mine, m) for m in ALONG])
    pieces = [along] + [hop(along, m) for m in GROUP]
    crossed = [hop(piece, CORE) for piece in pieces]
    return pl.pallas_call(
        assemble_kernel,
        grid_spec=pltpu.PrefetchScalarGridSpec(
            num_scalar_prefetch=1,
            grid=(1,),
            in_specs=[pl.BlockSpec(memory_space=pl.ANY)] * 10,
            out_specs=pl.BlockSpec((n, 8 * rows, d), lambda i, place: (0, 0, 0)),
            scratch_shapes=[pltpu.SemaphoreType.DMA],
        ),
        out_shape=jax.ShapeDtypeStruct((n, 8 * rows, d), bf16),
        compiler_params=params(1),
        cost_estimate=cost(0, 32 * n * rows * d),
        name="assemble",
    )(place, local, *pieces, other, *crossed)


def reduce_fast(grad, place):
    n, d = grad.shape[0], grad.shape[2]
    dp, z, c = place[0], place[1], place[2]
    grad = grad.reshape(n, 4, 2, -1, d)
    take = lambda core: lax.dynamic_index_in_dim(grad, core, 2, keepdims=False)
    got = hop(take(1 - c), CORE)
    half = (take(c).astype(f32) + got.astype(f32)).astype(bf16)
    total = pick(half, dp).astype(f32)
    for i, m in enumerate(GROUP):
        total = total + hop(pick(half, dp ^ (i + 1)), m).astype(f32)
    part = total.astype(bf16)
    total = pick(part, z).astype(f32)
    for i, m in enumerate(ALONG):
        total = total + hop(pick(part, z ^ (i + 1)), m).astype(f32)
    own = total.astype(bf16)
    blocks = jnp.stack([own] + [hop(own, m) for m in GROUP])
    return [pick(blocks, dp ^ b) for b in range(4)]


def gather_vectors_fast(local, place):
    s = 2 * place[1] + place[2]
    x = local
    for bit, mask in ((0, 1), (1, 2), (2, 4)):
        y = hop(x, mask)
        x = jnp.where((s >> bit) & 1 == 0, jnp.concatenate([x, y], 0), jnp.concatenate([y, x], 0))
    return x


def reduce_vectors_fast(grad, place):
    x = grad
    for mask in (1, 2, 4, 8, 16):
        x = x + hop(x, mask)
    return pick(x, 2 * place[1] + place[2])


def gather_plain(local, place):
    return lax.all_gather(local, "fsdp", axis=1, tiled=True)


def reduce_plain(grad, place):
    part = lax.psum_scatter(grad.astype(f32), "fsdp", scatter_dimension=1, tiled=True)
    total = lax.psum(part.astype(bf16), "dp")
    return [total[b] for b in range(grad.shape[0])]


def gather_vectors_plain(local, place):
    return lax.all_gather(local, "fsdp", axis=0, tiled=True)


def reduce_vectors_plain(grad, place):
    part = lax.psum_scatter(grad, "fsdp", scatter_dimension=0, tiled=True)
    return lax.psum(part, "dp")[0]


def segment_ids(lengths):
    ends = jnp.cumsum(lengths, axis=-1)
    places = jnp.arange(SEQ, dtype=jnp.int32)
    return jnp.sum((places[None, :, None] >= ends[:, None, :]).astype(jnp.int32), axis=-1)


def body(
    tokens, cotangent, doc_lengths, w_query, w_key, w_value, w_out, w_up, w_down,
    pre_gain, pre_shift, bias_query, bias_value, bias_out, mid_gain, mid_shift, bias_up, bias_down,
):
    shards, groups = lax.axis_size("fsdp"), lax.axis_size("dp")
    fast = shards == 8 and groups == 4
    gather = gather_fast if fast else gather_plain
    reduce = reduce_fast if fast else reduce_plain
    gather_vectors = gather_vectors_fast if fast else gather_vectors_plain
    reduce_vectors = reduce_vectors_fast if fast else reduce_vectors_plain
    rows, d = tokens.shape
    m = d // shards
    parts = w_down.shape[0] // m
    at = lax.axis_index("fsdp")
    place = jnp.stack([lax.axis_index("dp"), at // 2, at % 2]).astype(jnp.int32)
    doc = segment_ids(doc_lengths)

    up_local = w_up.reshape(m, shards, parts, m).transpose(2, 0, 1, 3).reshape(parts, m, d)
    down_local = w_down.reshape(parts, m, d)
    vectors = (pre_gain, pre_shift, bias_query, bias_value, bias_out, mid_gain, mid_shift, bias_down)
    packed = jnp.concatenate(vectors + (bias_up,))[None]
    small = gather_vectors(packed, place)
    gain_one, shift_one, add_query, add_value, add_out, gain_two, shift_two, add_down = (
        small[:, i * m : (i + 1) * m].reshape(1, d).astype(f32) for i in range(8)
    )
    add_up = small[:, 8 * m :].reshape(shards, parts, m).transpose(1, 0, 2).reshape(parts, 1, d)
    add_up = add_up.astype(f32)

    attn_w = gather(jnp.stack([w_query, w_key, w_value, w_out]), place)
    feed_w = [
        gather(jnp.stack([up_local[j], down_local[j], up_local[j + 1], down_local[j + 1]]), place)
        for j in range(0, parts, 2)
    ]

    scaled, _ = moments(tokens.astype(f32))
    first = (scaled * gain_one + shift_one).astype(bf16)
    biases = jnp.stack([add_query, jnp.zeros_like(add_query), add_value])
    qkv = qkv_call(first, attn_w, biases)
    attended, probs = attn_fwd_call(qkv, doc)
    middle, second, acc = out_call(
        attended, attn_w, tokens, add_out, gain_two, shift_two, add_down
    )
    sg = jnp.zeros((rows, d), f32)
    feed_grads = []
    up_bias_grads = []
    for i, w in enumerate(feed_w):
        grads, bias_grads, acc, sg = ffn_call(
            second, cotangent, w, add_up[2 * i : 2 * i + 2], acc, sg
        )
        feed_grads.append(reduce(grads, place))
        up_bias_grads.append(bias_grads)
    mid_grad, attended_grad, out_grad, mid_vec, layer_out = mid_call(
        sg, middle, cotangent, attended, attn_w, gain_two, acc
    )
    grads = attn_bwd_call(qkv, attended_grad, probs)
    proj_grad, proj_bias = wgrad_call(first, grads)
    input_grad, in_vec = input_call(grads, attn_w, tokens, mid_grad, gain_one)
    attn_grads = reduce(jnp.concatenate([proj_grad, out_grad]), place)

    up_bias = jnp.concatenate(up_bias_grads).reshape(parts, shards, m).transpose(1, 0, 2)
    vec = jnp.stack(
        [in_vec[0], in_vec[1], proj_bias[0, 0], proj_bias[2, 0], mid_vec[2], mid_vec[0],
         mid_vec[1], mid_vec[3]]
    )
    vec = vec.reshape(8, shards, m).transpose(1, 0, 2).reshape(shards, 8 * m)
    vec = reduce_vectors(jnp.concatenate([vec, up_bias.reshape(shards, parts * m)], 1), place)

    factor = (groups * shards * rows) ** (-0.5)
    vec = vec * factor
    down_parts = [feed_grads[j // 2][j % 2 * 2 + 1] for j in range(parts)]
    up_parts = [feed_grads[j // 2][j % 2 * 2] for j in range(parts)]
    up_grad = jnp.stack(up_parts).reshape(parts, m, shards, m).transpose(1, 2, 0, 3)
    return (
        layer_out,
        input_grad,
        *(g.astype(f32) * factor for g in attn_grads),
        up_grad.reshape(m, parts * d).astype(f32) * factor,
        jnp.concatenate(down_parts).astype(f32) * factor,
        *(vec[i * m : (i + 1) * m] for i in range(7)),
        vec[8 * m :],
        vec[7 * m : 8 * m],
    )


def solution(mesh):
    both = P(("dp", "fsdp"), None)
    matrix, vector = P("fsdp", None), P("fsdp")
    return jax.shard_map(
        body,
        mesh=mesh,
        in_specs=(both,) * 3 + (matrix,) * 6 + (vector,) * 9,
        out_specs=(both,) * 2 + (matrix,) * 6 + (vector,) * 9,
        check_vma=False,
    )
```

```python
from functools import partial

import jax
import jax.numpy as jnp
from jax import lax
from jax.experimental import pallas as pl
from jax.experimental.pallas import tpu as pltpu
from jax.sharding import PartitionSpec as P

H = 12
HD = 64
SEQ = 512
MOST = 160
BQ = 256
BAND = 416
GAIN_ONE, SHIFT_ONE, QUERY, KEY, VALUE, OUT, GAIN_TWO, SHIFT_TWO, DOWN, UP = range(10)
epsilon = 1e-05
bf16 = jnp.bfloat16
f32 = jnp.float32


def nn(a, b):
    return jnp.dot(a, b, preferred_element_type=f32)


def nt(a, b):
    return lax.dot_general(a, b, (((1,), (1,)), ((), ())), preferred_element_type=f32)


def tn(a, b):
    return lax.dot_general(a, b, (((0,), (0,)), ((), ())), preferred_element_type=f32)


def params(n, mb=56):
    return pltpu.CompilerParams(
        dimension_semantics=("arbitrary",) * n, vmem_limit_bytes=mb * 1024 * 1024
    )


def cost(flops, nbytes, trans=0):
    return pl.CostEstimate(
        flops=int(flops * 50), bytes_accessed=int(nbytes * 50), transcendentals=int(trans)
    )


def moments(v):
    mean = jnp.mean(v, axis=-1, keepdims=True)
    c = v - mean
    inv = lax.rsqrt(jnp.mean(c * c, axis=-1, keepdims=True) + epsilon)
    return c * inv, inv


def piece_copies(place, pieces, out, sems, lead):
    rows = out.shape[1] // 8
    d, z, c = place[0], place[1], place[2]
    copies = []
    for p in range(2):
        own, rest = pieces[5 * p], pieces[5 * p + 1 : 5 * p + 5]
        s = 2 * z + (c ^ p)
        for b in range(4):
            copies.append((own.at[4 * lead + b], out.at[b, pl.ds(s * rows, rows), :]))
        for m in range(4):
            skip = rest[m].shape[0] - 3
            for k in range(3):
                s = 2 * (z ^ (k + 1)) + (c ^ p)
                piece = rest[m].at[k + skip, pl.ds(0, rows), :]
                copies.append((piece, out.at[d ^ m, pl.ds(s * rows, rows), :]))
    return [pltpu.make_async_copy(a, b, sems) for a, b in copies]


def split_blocks(place, full, keep, send, b):
    rows = full.shape[0] // 8
    for k in range(4):
        keep[b, k] = full[pl.ds((2 * k + place[2]) * rows, rows), :].astype(bf16)
        send[b, k] = full[pl.ds((2 * k + 1 - place[2]) * rows, rows), :].astype(bf16)


ANY = pl.BlockSpec(memory_space=pl.ANY)


def qkv_kernel(x_ref, w_ref, b_ref, o_ref):
    b = b_ref[0]
    for r in range(x_ref.shape[0] // 256):
        rows = pl.ds(r * 256, 256)
        o_ref[0, rows, :] = (nn(x_ref[rows, :], w_ref[0]) + b).astype(bf16)


def qkv_call(first, w, table):
    rows, d = first.shape
    return pl.pallas_call(
        qkv_kernel,
        grid=(3,),
        in_specs=[
            pl.BlockSpec((rows, d), lambda i: (0, 0)),
            pl.BlockSpec((1, d, d), lambda i: (i, 0, 0)),
            pl.BlockSpec((1, 1, d), lambda i: (QUERY + i, 0, 0)),
        ],
        out_specs=pl.BlockSpec((1, rows, d), lambda i: (i, 0, 0)),
        out_shape=jax.ShapeDtypeStruct((3, rows, d), bf16),
        compiler_params=params(1),
        cost_estimate=cost(6 * rows * d * d, 2 * (rows * d * 4 + 3 * d * d)),
        name="qkv",
    )(first, w, table)


def qkv_fast_kernel(place, x_ref, b_ref, *refs):
    pieces, o_ref, w_ref, sem = refs[:10], refs[10], refs[11], refs[12]

    @pl.when(pl.program_id(0) == 0)
    def _():
        copies = piece_copies(place, pieces, w_ref, sem, 0)
        for copy in copies:
            copy.start()
        for copy in copies:
            copy.wait()

    i = pl.program_id(0)
    b = b_ref[0]
    for r in range(x_ref.shape[0] // 256):
        rows = pl.ds(r * 256, 256)
        o_ref[0, rows, :] = (nn(x_ref[rows, :], w_ref[i]) + b).astype(bf16)


def qkv_fast_call(place, first, table, pieces):
    rows, d = first.shape
    return pl.pallas_call(
        qkv_fast_kernel,
        grid_spec=pltpu.PrefetchScalarGridSpec(
            num_scalar_prefetch=1,
            grid=(3,),
            in_specs=[
                pl.BlockSpec((rows, d), lambda i, place: (0, 0)),
                pl.BlockSpec((1, 1, d), lambda i, place: (QUERY + i, 0, 0)),
            ]
            + [ANY] * 10,
            out_specs=[
                pl.BlockSpec((1, rows, d), lambda i, place: (i, 0, 0)),
                pl.BlockSpec((4, d, d), lambda i, place: (0, 0, 0)),
            ],
            scratch_shapes=[pltpu.SemaphoreType.DMA],
        ),
        out_shape=[
            jax.ShapeDtypeStruct((3, rows, d), bf16),
            jax.ShapeDtypeStruct((4, d, d), bf16),
        ],
        compiler_params=params(1),
        cost_estimate=cost(6 * rows * d * d, 2 * (rows * d * 4 + 8 * d * d)),
        name="qkv",
    )(place, first, table, *pieces)


def spans(b):
    return b * BQ, b * (SEQ - BAND)


def attn_fwd_kernel(q_ref, k_ref, v_ref, dr_ref, dc_ref, o_ref, p_ref, bias):
    @pl.when(pl.program_id(1) == 0)
    def _():
        for b in range(2):
            q0, k0 = spans(b)
            same = dc_ref[0, k0 : k0 + BAND, :] == dr_ref[0, :, q0 : q0 + BQ]
            bias[b] = jnp.where(same, 0.0, -3e38)

    low = lax.broadcasted_iota(jnp.int32, (1, 128), 1) < HD
    for b in range(2):
        q0, k0 = spans(b)
        qb = q_ref[0, q0 : q0 + BQ, :] * bf16(HD**-0.5)
        kb = k_ref[0, k0 : k0 + BAND, :]
        vb = v_ref[0, k0 : k0 + BAND, :]
        acc = None
        for hh in range(2):
            mine = low if hh == 0 else jnp.logical_not(low)
            s = nt(kb, jnp.where(mine, qb, bf16(0))) + bias[b]
            e = jnp.exp(s - jnp.max(s, axis=0, keepdims=True))
            p = (e * (1.0 / jnp.sum(e, axis=0, keepdims=True))).astype(bf16)
            p_ref[hh, b] = p
            part = tn(jnp.where(mine, vb, bf16(0)), p)
            acc = part if acc is None else acc + part
        o_ref[q0 : q0 + BQ, :] = acc.T.astype(bf16)


def attn_fwd_call(qkv, doc):
    rows = qkv.shape[1]
    d = qkv.shape[2]
    seqs = rows // SEQ
    hp = d // 128

    def part(i):
        return pl.BlockSpec((1, SEQ, 128), lambda s, h: (i, s, h))

    return pl.pallas_call(
        attn_fwd_kernel,
        grid=(seqs, hp),
        in_specs=[
            part(0),
            part(1),
            part(2),
            pl.BlockSpec((1, 1, SEQ), lambda s, h: (s, 0, 0)),
            pl.BlockSpec((1, SEQ, 1), lambda s, h: (s, 0, 0)),
        ],
        out_specs=[
            pl.BlockSpec((SEQ, 128), lambda s, h: (s, h)),
            pl.BlockSpec((2, 2, BAND, BQ), lambda s, h: (s * hp + h, 0, 0, 0)),
        ],
        out_shape=[
            jax.ShapeDtypeStruct((rows, d), bf16),
            jax.ShapeDtypeStruct((seqs * H, 2, BAND, BQ), bf16),
        ],
        scratch_shapes=[pltpu.VMEM((2, BAND, BQ), f32)],
        compiler_params=params(2),
        cost_estimate=cost(
            seqs * H * 2 * BAND * BQ * 2 * 256, 2 * 4 * rows * d + 4 * seqs * H * BAND * BQ
        ),
        name="attend",
    )(qkv, qkv, qkv, doc[:, None, :], doc[:, :, None])


def attn_bwd_kernel(q_ref, k_ref, v_ref, do_ref, p_ref, o_ref):
    low = lax.broadcasted_iota(jnp.int32, (1, 128), 1) < HD
    scale = bf16(HD**-0.5)
    over = SEQ - BAND
    tails = []
    for b in range(2):
        q0, k0 = spans(b)
        qb = q_ref[0, q0 : q0 + BQ, :] * scale
        dob = do_ref[q0 : q0 + BQ, :]
        kb = k_ref[0, k0 : k0 + BAND, :] * scale
        vb = v_ref[0, k0 : k0 + BAND, :]
        dq = dk = dv = None
        for hh in range(2):
            mine = low if hh == 0 else jnp.logical_not(low)
            p = p_ref[hh, b]
            dom = jnp.where(mine, dob, bf16(0))
            dp = nt(vb, dom)
            pf = p.astype(f32)
            inner = jnp.sum(pf * dp, axis=0, keepdims=True)
            ds = (pf * (dp - inner)).astype(bf16)
            a = nn(p, dom)
            c = nn(ds, jnp.where(mine, qb, bf16(0)))
            g = tn(jnp.where(mine, kb, bf16(0)), ds)
            dv = a if dv is None else dv + a
            dk = c if dk is None else dk + c
            dq = g if dq is None else dq + g
        o_ref[0, q0 : q0 + BQ, :] = dq.T.astype(bf16)
        tails.append((dk, dv))
    for i, (first_part, second_part) in enumerate(zip(*tails)):
        o_ref[i + 1, :over, :] = first_part[:over].astype(bf16)
        o_ref[i + 1, over:BAND, :] = (first_part[over:] + second_part[: BAND - over]).astype(bf16)
        o_ref[i + 1, BAND:, :] = second_part[BAND - over :].astype(bf16)


def attn_bwd_call(qkv, dattn, probs):
    rows = qkv.shape[1]
    d = qkv.shape[2]
    seqs = rows // SEQ
    hp = d // 128

    def part(i):
        return pl.BlockSpec((1, SEQ, 128), lambda s, h: (i, s, h))

    return pl.pallas_call(
        attn_bwd_kernel,
        grid=(seqs, hp),
        in_specs=[
            part(0),
            part(1),
            part(2),
            pl.BlockSpec((SEQ, 128), lambda s, h: (s, h)),
            pl.BlockSpec((2, 2, BAND, BQ), lambda s, h: (s * hp + h, 0, 0, 0)),
        ],
        out_specs=pl.BlockSpec((3, SEQ, 128), lambda s, h: (0, s, h)),
        out_shape=jax.ShapeDtypeStruct((3, rows, d), bf16),
        compiler_params=params(2),
        cost_estimate=cost(
            seqs * H * 2 * BAND * BQ * 2 * 256 * 2, 2 * 7 * rows * d + 4 * seqs * H * BAND * BQ
        ),
        name="attend_back",
    )(qkv, qkv, qkv, dattn, probs)


def row_of(i):
    return pl.BlockSpec((1, 1, 768), lambda *_: (i, 0, 0))


def out_kernel(a_ref, w_ref, t_ref, bo_ref, g_ref, s_ref, mid_ref, sec_ref):
    mid = t_ref[...].astype(f32) + nn(a_ref[...], w_ref[0]) + bo_ref[0]
    mid_ref[...] = mid
    sc, _ = moments(mid)
    sec_ref[...] = (sc * g_ref[0] + s_ref[0]).astype(bf16)


def out_call(attended, wo, tokens, table):
    rows, d = tokens.shape
    blk = pl.BlockSpec((256, d), lambda i: (i, 0))
    return pl.pallas_call(
        out_kernel,
        grid=(rows // 256,),
        in_specs=[
            blk, pl.BlockSpec((1, d, d), lambda i: (3, 0, 0)), blk,
            row_of(OUT), row_of(GAIN_TWO), row_of(SHIFT_TWO),
        ],
        out_specs=[blk, blk],
        out_shape=[
            jax.ShapeDtypeStruct((rows, d), f32),
            jax.ShapeDtypeStruct((rows, d), bf16),
        ],
        compiler_params=params(1),
        cost_estimate=cost(2 * rows * d * d, rows * d * 10 + 2 * d * d),
        name="project",
    )(attended, wo, tokens, table, table, table)


def ffn_step(x_ref, g_ref, wu, wd, b, acc_ref, sg_ref, act, hg, gb_ref):
    rows = x_ref.shape[0]
    chunk = 256
    total = jnp.zeros((1, wu.shape[1]), f32)
    for r in range(rows // chunk):
        at = pl.ds(r * chunk, chunk)
        h = nn(x_ref[at, :], wu[...]) + b
        ag = nt(g_ref[at, :], wd[...])
        phi = 0.5 + 0.5 * lax.erf(h * (0.5**0.5))
        a = (h * phi).astype(bf16)
        act[at, :] = a
        dens = jnp.exp(-0.5 * (h * h)) * 0.3989422804014327
        hgv = (ag * (phi + h * dens)).astype(bf16)
        hg[at, :] = hgv
        total += jnp.sum(hgv.astype(f32), axis=0, keepdims=True)
        acc_ref[at, :] += nn(a, wd[...])
        sg_ref[at, :] += nt(hgv, wu[...])
    gb_ref[0] = total


def ffn_start(start, acc_in, bd_ref, sg_in, acc_ref, sg_ref):
    if start:
        acc_ref[...] = acc_in[...] + bd_ref[0]
        sg_ref[...] = jnp.zeros_like(sg_ref)
    else:
        acc_ref[...] = acc_in[...]
        sg_ref[...] = sg_in[...]


def ffn_kernel(start, x_ref, g_ref, w_ref, b_ref, acc_in, bd_ref, *refs):
    sg_in = None if start else refs[0]
    gw_ref, gb_ref, acc_ref, sg_ref, act, hg = refs[0 if start else 1 :]

    @pl.when(pl.program_id(0) == 0)
    def _():
        ffn_start(start, acc_in, bd_ref, sg_in, acc_ref, sg_ref)

    ffn_step(x_ref, g_ref, w_ref.at[0], w_ref.at[1], b_ref[0], acc_ref, sg_ref, act, hg, gb_ref)
    gw_ref[0] = tn(x_ref[...], hg[...]).astype(bf16)
    gw_ref[1] = tn(act[...], g_ref[...]).astype(bf16)


def ffn_call(lead, second, dgrad, w, table, acc, sg):
    rows, d = second.shape
    n = w.shape[0] // 2
    start = sg is None
    full = pl.BlockSpec((rows, d), lambda j: (0, 0))
    pair = pl.BlockSpec((2, d, d), lambda j: (j, 0, 0))
    return pl.pallas_call(
        partial(ffn_kernel, start),
        grid=(n,),
        in_specs=[
            full, full, pair, pl.BlockSpec((1, 1, d), lambda j: (UP + lead * n + j, 0, 0)),
            full, row_of(DOWN),
        ]
        + ([] if start else [full]),
        out_specs=[pair, pl.BlockSpec((1, 1, d), lambda j: (j, 0, 0)), full, full],
        out_shape=[
            jax.ShapeDtypeStruct((2 * n, d, d), bf16),
            jax.ShapeDtypeStruct((n, 1, d), f32),
            jax.ShapeDtypeStruct((rows, d), f32),
            jax.ShapeDtypeStruct((rows, d), f32),
        ],
        scratch_shapes=[pltpu.VMEM((rows, d), bf16)] * 2,
        compiler_params=params(1),
        cost_estimate=cost(12 * n * rows * d * d, 20 * rows * d + 8 * n * d * d),
        name="feed",
    )(second, dgrad, w, table, acc, table, *([] if start else [sg]))


def ffn_fast_kernel(start, lead, place, x_ref, g_ref, b_ref, acc_in, bd_ref, *refs):
    sg_in = None if start else refs[0]
    refs = refs[0 if start else 1 :]
    pieces = refs[:10]
    keep, send, gb_ref, acc_ref, sg_ref, w_ref, act, hg, full, sem = refs[10:]
    j = pl.program_id(0)

    @pl.when(j == 0)
    def _():
        copies = piece_copies(place, pieces, w_ref, sem, lead)
        for copy in copies:
            copy.start()
        ffn_start(start, acc_in, bd_ref, sg_in, acc_ref, sg_ref)
        for copy in copies:
            copy.wait()

    wu, wd = w_ref.at[2 * j], w_ref.at[2 * j + 1]
    ffn_step(x_ref, g_ref, wu, wd, b_ref[0], acc_ref, sg_ref, act, hg, gb_ref)
    full[...] = tn(x_ref[...], hg[...]).astype(bf16)
    split_blocks(place, full, keep, send, 0)
    full[...] = tn(act[...], g_ref[...]).astype(bf16)
    split_blocks(place, full, keep, send, 1)


def ffn_fast_call(lead, place, second, dgrad, table, acc, sg, pieces):
    rows, d = second.shape
    start = sg is None
    m = d // 8
    full = pl.BlockSpec((rows, d), lambda j, place: (0, 0))
    half = pl.BlockSpec((2, 4, m, d), lambda j, place: (j, 0, 0, 0))
    return pl.pallas_call(
        partial(ffn_fast_kernel, start, lead),
        grid_spec=pltpu.PrefetchScalarGridSpec(
            num_scalar_prefetch=1,
            grid=(2,),
            in_specs=[
                full, full, pl.BlockSpec((1, 1, d), lambda j, place: (UP + lead * 2 + j, 0, 0)),
                full, row_of(DOWN),
            ]
            + ([] if start else [full])
            + [ANY] * 10,
            out_specs=[half, half, pl.BlockSpec((1, 1, d), lambda j, place: (j, 0, 0)), full, full],
            scratch_shapes=[pltpu.VMEM((4, d, d), bf16)]
            + [pltpu.VMEM((rows, d), bf16)] * 2
            + [pltpu.VMEM((d, d), bf16), pltpu.SemaphoreType.DMA],
        ),
        out_shape=[
            jax.ShapeDtypeStruct((4, 4, m, d), bf16),
            jax.ShapeDtypeStruct((4, 4, m, d), bf16),
            jax.ShapeDtypeStruct((2, 1, d), f32),
            jax.ShapeDtypeStruct((rows, d), f32),
            jax.ShapeDtypeStruct((rows, d), f32),
        ],
        compiler_params=params(1),
        cost_estimate=cost(24 * rows * d * d, 20 * rows * d + 16 * d * d),
        name="feed",
    )(place, second, dgrad, table, acc, table, *([] if start else [sg]), *pieces)


def norm_back(grad, sc, inv, gain):
    t = grad * gain
    return inv * (
        t - jnp.mean(t, axis=-1, keepdims=True) - sc * jnp.mean(t * sc, axis=-1, keepdims=True)
    )


def mid_kernel(
    place, sg_ref, mid_ref, dy_ref, a_ref, w_ref, g_ref, acc_ref,
    mg_ref, ag_ref, vec_ref, lo_ref, wg_ref, *rest,
):
    i = pl.program_id(0)
    wacc = rest[-1]

    @pl.when(i == 0)
    def _():
        wacc[...] = jnp.zeros_like(wacc)
        vec_ref[...] = jnp.zeros_like(vec_ref)

    lo_ref[...] = acc_ref[...].astype(bf16)
    sc, inv = moments(mid_ref[...])
    sg = sg_ref[...]
    dy = dy_ref[...].astype(f32)
    mg = dy + norm_back(sg, sc, inv, g_ref[0])
    mg_ref[...] = mg
    br = mg.astype(bf16)
    vec_ref[0:1, :] += jnp.sum(sg * sc, axis=0, keepdims=True)
    vec_ref[1:2, :] += jnp.sum(sg, axis=0, keepdims=True)
    vec_ref[2:3, :] += jnp.sum(br.astype(f32), axis=0, keepdims=True)
    vec_ref[3:4, :] += jnp.sum(dy, axis=0, keepdims=True)
    ag_ref[...] = nt(br, w_ref[0]).astype(bf16)
    wacc[...] += tn(a_ref[...], br)

    @pl.when(i == pl.num_programs(0) - 1)
    def _():
        if len(rest) == 1:
            wg_ref[0] = wacc[...].astype(bf16)
        else:
            split_blocks(place, wacc, wg_ref, rest[0], 0)


def mid_call(place, sg, mid, dy, attended, wo, table, acc, split):
    rows, d = sg.shape
    blk = pl.BlockSpec((256, d), lambda i, place: (i, 0))
    grad = (1, 4, d // 8, d) if split else (1, d, d)
    return pl.pallas_call(
        mid_kernel,
        grid_spec=pltpu.PrefetchScalarGridSpec(
            num_scalar_prefetch=1,
            grid=(rows // 256,),
            in_specs=[
                blk, blk, blk, blk, pl.BlockSpec((1, d, d), lambda i, place: (3, 0, 0)),
                row_of(GAIN_TWO), blk,
            ],
            out_specs=[blk, blk, pl.BlockSpec((8, d), lambda i, place: (0, 0)), blk]
            + [pl.BlockSpec(grad, lambda i, place: (0,) * len(grad))] * (2 if split else 1),
            scratch_shapes=[pltpu.VMEM((d, d), f32)],
        ),
        out_shape=[
            jax.ShapeDtypeStruct((rows, d), f32),
            jax.ShapeDtypeStruct((rows, d), bf16),
            jax.ShapeDtypeStruct((8, d), f32),
            jax.ShapeDtypeStruct((rows, d), bf16),
        ]
        + [jax.ShapeDtypeStruct(grad, bf16)] * (2 if split else 1),
        compiler_params=params(1),
        cost_estimate=cost(4 * rows * d * d, rows * d * 22 + 4 * d * d),
        name="middle_back",
    )(place, sg, mid, dy, attended, wo, table, acc)


def wgrad_kernel(x_ref, g_ref, o_ref, b_ref):
    o_ref[0] = tn(x_ref[...], g_ref[0]).astype(bf16)
    b_ref[0] = jnp.sum(g_ref[0].astype(f32), axis=0, keepdims=True)


def wgrad_call(first, grads):
    rows, d = first.shape
    return pl.pallas_call(
        wgrad_kernel,
        grid=(3,),
        in_specs=[
            pl.BlockSpec((rows, d), lambda i: (0, 0)),
            pl.BlockSpec((1, rows, d), lambda i: (i, 0, 0)),
        ],
        out_specs=[
            pl.BlockSpec((1, d, d), lambda i: (i, 0, 0)),
            pl.BlockSpec((1, 1, d), lambda i: (i, 0, 0)),
        ],
        out_shape=[
            jax.ShapeDtypeStruct((3, d, d), bf16),
            jax.ShapeDtypeStruct((3, 1, d), f32),
        ],
        compiler_params=params(1),
        cost_estimate=cost(6 * rows * d * d, 2 * (rows * d * 4 + 3 * d * d)),
        name="weight_back",
    )(first, grads)


def wgrad_fast_kernel(place, x_ref, g_ref, keep, send, b_ref, full):
    full[...] = tn(x_ref[...], g_ref[0])
    b_ref[0] = jnp.sum(g_ref[0].astype(f32), axis=0, keepdims=True)
    split_blocks(place, full, keep, send, 0)


def wgrad_fast_call(place, first, grads):
    rows, d = first.shape
    m = d // 8
    half = pl.BlockSpec((1, 4, m, d), lambda i, place: (i, 0, 0, 0))
    return pl.pallas_call(
        wgrad_fast_kernel,
        grid_spec=pltpu.PrefetchScalarGridSpec(
            num_scalar_prefetch=1,
            grid=(3,),
            in_specs=[
                pl.BlockSpec((rows, d), lambda i, place: (0, 0)),
                pl.BlockSpec((1, rows, d), lambda i, place: (i, 0, 0)),
            ],
            out_specs=[half, half, pl.BlockSpec((1, 1, d), lambda i, place: (i, 0, 0))],
            scratch_shapes=[pltpu.VMEM((d, d), f32)],
        ),
        out_shape=[
            jax.ShapeDtypeStruct((3, 4, m, d), bf16),
            jax.ShapeDtypeStruct((3, 4, m, d), bf16),
            jax.ShapeDtypeStruct((3, 1, d), f32),
        ],
        compiler_params=params(1),
        cost_estimate=cost(6 * rows * d * d, 2 * (rows * d * 4 + 3 * d * d)),
        name="weight_back",
    )(place, first, grads)


def input_kernel(start, g_ref, w_ref, t_ref, mg_ref, gain_ref, *refs):
    o_ref, vec_ref = refs[-2:]

    @pl.when(pl.program_id(0) == 0)
    def _():
        vec_ref[...] = jnp.zeros_like(vec_ref) if start else refs[0][...]

    fg = nt(g_ref[0], w_ref[0]) + nt(g_ref[1], w_ref[1]) + nt(g_ref[2], w_ref[2])
    sc, inv = moments(t_ref[...].astype(f32))
    o_ref[...] = (mg_ref[...] + norm_back(fg, sc, inv, gain_ref[0])).astype(bf16)
    vec_ref[0:1, :] += jnp.sum(fg * sc, axis=0, keepdims=True)
    vec_ref[1:2, :] += jnp.sum(fg, axis=0, keepdims=True)


def input_call(grads, w, tokens, mg, table, part, before=()):
    rows, d = tokens.shape
    steps = rows // 512
    blk = pl.BlockSpec((256, d), lambda i: (part * steps + i, 0))
    vec = pl.BlockSpec((8, d), lambda i: (0, 0))
    start = not before
    return pl.pallas_call(
        partial(input_kernel, start),
        grid=(steps,),
        in_specs=[
            pl.BlockSpec((3, 256, d), lambda i: (0, part * steps + i, 0)),
            pl.BlockSpec((3, d, d), lambda i: (0, 0, 0)),
            blk,
            blk,
            row_of(GAIN_ONE),
        ]
        + ([] if start else [vec, ANY]),
        out_specs=[blk, vec],
        out_shape=[
            jax.ShapeDtypeStruct((rows, d), bf16),
            jax.ShapeDtypeStruct((8, d), f32),
        ],
        input_output_aliases={} if start else {6: 0},
        compiler_params=params(1),
        cost_estimate=cost(3 * rows * d * d, rows * d * 7 + 6 * d * d),
        name="input_back",
    )(grads, w, tokens, mg, table, *([] if start else [before[1], before[0]]))


CORE = 1
ALONG = (2, 4, 6)
GROUP = (8, 16, 24)


def hop(x, mask):
    return lax.ppermute(x, ("dp", "fsdp"), [(i, i ^ mask) for i in range(32)])


def pick(x, index, axis=0):
    return lax.dynamic_index_in_dim(x, index, axis, keepdims=False)


def after(deps, *xs):
    return lax.optimization_barrier((*xs, *deps))[: len(xs)]


def wide(x):
    return x.astype(f32)


def add_core(keep, got):
    return (wide(keep) + wide(got)).astype(bf16)


def quarter(x, index, axis):
    n = x.shape[axis] // 4
    return lax.dynamic_slice_in_dim(x, index * n, n, axis)


def turn(x, bits):
    for axis, bit in enumerate(bits):
        x = jnp.where(bit == 0, x, jnp.flip(x, axis))
    return x


def add_all(first, others):
    total = wide(first)
    for other in others:
        total = total + wide(other)
    return total.astype(bf16)


def segment_ids(lengths):
    ends = jnp.cumsum(lengths, axis=-1)
    places = jnp.arange(SEQ, dtype=jnp.int32)
    return jnp.sum((places[None, :, None] >= ends[:, None, :]).astype(jnp.int32), axis=-1)


def pack_vectors(pre_gain, pre_shift, bias_query, bias_value, bias_out, mid_gain, mid_shift, bias_up, bias_down):
    none = jnp.zeros_like(bias_query)
    return jnp.concatenate(
        [pre_gain, pre_shift, bias_query, none, bias_value, bias_out, mid_gain, mid_shift, bias_down, bias_up]
    )[None]


def make_table(small):
    shards = small.shape[0]
    n = small.shape[1] * shards // 768
    return small.reshape(shards, n, -1).transpose(1, 0, 2).reshape(n, 1, 768).astype(f32)


def order_hidden(w_up, w_down, shards):
    m, d = w_up.shape[0], w_up.shape[0] * shards
    parts = w_down.shape[0] // m
    up = w_up.reshape(m, shards, parts, m).transpose(2, 0, 1, 3).reshape(parts, m, d)
    return jnp.stack([up, w_down.reshape(parts, m, d)], 1).reshape(2 * parts, m, d)


VEC_ROWS = (0, 1, 16, 18, 10, 8, 9)
DOWN_ROW, UP_ROW = 11, 20


def outputs(layer_out, input_grad, attn, feed, vec, factor, shards):
    m, d = attn[0].shape
    parts = len(feed) // 2
    vec = vec * factor
    up = jnp.stack(feed[0::2]).reshape(parts, m, shards, m).transpose(1, 2, 0, 3)
    return (
        layer_out,
        input_grad,
        *(wide(g) * factor for g in attn),
        wide(up.reshape(m, parts * d)) * factor,
        wide(jnp.concatenate(feed[1::2])) * factor,
        *(vec[i] for i in VEC_ROWS),
        vec[UP_ROW:].reshape(-1),
        vec[DOWN_ROW],
    )


def body_fast(tokens, cotangent, doc_lengths, w_query, w_key, w_value, w_out, w_up, w_down, *vectors):
    rows, d = tokens.shape
    dp, at = lax.axis_index("dp"), lax.axis_index("fsdp")
    z, core = at // 2, at % 2
    place = jnp.stack([dp, z, core]).astype(jnp.int32)

    small = pack_vectors(*vectors)
    width = small.shape[1]
    low = jnp.pad(small[0], (0, 8 * d - width)).reshape(8, d)
    attn_own = jnp.stack([w_query, w_key, w_value, w_out])
    attn_mine = jnp.concatenate([pick(attn_own, dp), low])
    attn_z = [attn_mine] + [hop(attn_mine, m) for m in ALONG]
    attn_along = jnp.stack([x[: d // 8] for x in attn_z[1:]])
    attn_chip = jnp.stack(attn_z)
    attn_group = [attn_along] + [hop(attn_along, m) for m in GROUP]
    attn_other = hop(attn_chip, CORE)
    attn_cross = [hop(attn_own, CORE), attn_other] + [hop(x, CORE) for x in attn_group[1:]]
    small = jnp.stack([attn_chip[:, d // 8 :], attn_other[:, d // 8 :]], 1)
    small = small.reshape(2, 2, 2, 8 * d)[..., :width]
    table = make_table(turn(small, (z // 2, z % 2, core)).reshape(8, width))

    feed_own = order_hidden(w_up, w_down, 8)
    feed_mine = jnp.stack([pick(feed_own[:4], dp), pick(feed_own[4:], dp)])
    tokens_late, lengths_late, feed_mine = after([attn_along], tokens, doc_lengths, feed_mine)
    (feed_mine_late,) = after(attn_group[1:], feed_mine)
    feed_along = [hop(feed_mine_late if m == 2 else feed_mine, m) for m in ALONG]
    along_one = jnp.stack([x[0] for x in feed_along])
    along_two = jnp.stack([x[1] for x in feed_along])
    group_one = [along_one] + [hop(along_one, m) for m in GROUP]
    (along_late,) = after(group_one[1:], along_two)
    group_two = [along_two] + [hop(along_late, m) for m in GROUP]
    feed_cross = hop(feed_own, CORE)
    pieces_one = [feed_own, *group_one, feed_cross, *(hop(x, CORE) for x in group_one)]
    pieces_two = [feed_own, *group_two, feed_cross, *(hop(x, CORE) for x in group_two)]

    doc = segment_ids(lengths_late)
    scaled, _ = moments(wide(tokens_late))
    first = (scaled * table[GAIN_ONE] + table[SHIFT_ONE]).astype(bf16)
    qkv, attn_w = qkv_fast_call(place, first, table, [attn_own, *attn_group, *attn_cross])
    attended, probs = attn_fwd_call(qkv, doc)
    (attended_late,) = after(group_one[1:], attended)
    middle, second = out_call(attended_late, attn_w, tokens, table)

    keep_one, send_one, up_bias_one, acc, sg = ffn_fast_call(
        0, place, second, cotangent, table, middle, None, pieces_one
    )
    (send_one,) = after(group_two[1:], send_one)
    got_one = hop(send_one, CORE)
    half = add_core(keep_one, got_one)
    parts_one = [pick(half, dp ^ i) for i in range(4)]
    group_one = [hop(x, m) for x, m in zip(parts_one[1:], GROUP)]
    (sg,) = after([got_one], sg)
    keep_two, send_two, up_bias_two, acc, sg = ffn_fast_call(
        1, place, second, cotangent, table, acc, sg, pieces_two
    )
    got_two = hop(send_two, CORE)
    (sg,) = after(group_one, sg)
    mid_grad, attended_grad, mid_vec, layer_out, keep_out, send_out = mid_call(
        place, sg, middle, cotangent, attended, attn_w, table, acc, True
    )
    sum_one = add_all(parts_one[0], group_one)
    z_one = [hop(pick(sum_one, z ^ (i + 1)), m) for i, m in enumerate(ALONG)]
    got_out = hop(send_out, CORE)
    (attended_grad,) = after([got_two, got_out], attended_grad)
    half = add_core(keep_two, got_two)
    half_out = add_core(keep_out[0], got_out[0])
    parts_two = [
        jnp.concatenate([pick(half, dp ^ i), quarter(half_out, dp ^ i, 1)], 1) for i in range(4)
    ]
    group_two = [hop(x, m) for x, m in zip(parts_two[1:], GROUP)]
    grads = attn_bwd_call(qkv, attended_grad, probs)
    (grads,) = after(group_two + z_one, grads)
    keep_attn, send_attn, proj_bias = wgrad_fast_call(place, first, grads)
    sum_two = add_all(parts_two[0], group_two)
    z_two = [hop(pick(sum_two, z ^ (i + 1)), m) for i, m in enumerate(ALONG)]
    got_attn = hop(send_attn, CORE)
    (grads,) = after(z_two, grads)
    part = input_call(grads, attn_w, tokens, mid_grad, table, 0)
    (grads,) = after([got_attn], grads)
    half = add_core(keep_attn, got_attn)
    parts_attn = [quarter(half, dp ^ i, 2) for i in range(4)]
    group_attn = [hop(x, m) for x, m in zip(parts_attn[1:], GROUP)]
    input_grad, in_vec = input_call(grads, attn_w, tokens, mid_grad, table, 1, part)
    final_feed = jnp.concatenate(
        [add_all(pick(sum_one, z), z_one), add_all(pick(sum_two, z), z_two)]
    )

    in_vec, final_feed, *group_attn = after((), in_vec, final_feed, *group_attn)
    attn_sum = add_all(parts_attn[0], group_attn)
    attn_z = [hop(pick(attn_sum, z ^ (i + 1), 1), m) for i, m in enumerate(ALONG)]
    none = jnp.zeros((1, d), f32)
    vec = jnp.concatenate(
        [in_vec, mid_vec, proj_bias[:, 0], none, up_bias_one[:, 0], up_bias_two[:, 0]]
    )
    vec = vec.reshape(24, 4, 2, d // 8).transpose(2, 1, 0, 3)
    vec = pick(vec, core) + hop(pick(vec, 1 - core), CORE)
    vec_x, vec_y, vec_xy = (hop(vec, m) for m in GROUP)
    vec = (vec + vec_x) + (vec_y + vec_xy)
    final_feed = [final_feed] + [hop(final_feed, m) for m in GROUP]
    *attn_z, vec = after(final_feed[1:], *attn_z, vec)
    final_attn = add_all(pick(attn_sum, z, 1), attn_z)
    final_attn = jnp.stack([final_attn] + [hop(final_attn, m) for m in GROUP])
    vec_z = [hop(pick(vec, z ^ (i + 1)), m) for i, m in enumerate(ALONG)]
    vec = pick(vec, z) + vec_z[0] + vec_z[1] + vec_z[2]
    final_feed = jnp.stack(final_feed)
    n = d // 8
    final_attn = [pick(final_attn, dp ^ b) for b in range(4)]
    final_feed = [pick(final_feed, dp ^ b) for b in range(4)]
    attn = [jnp.concatenate([x[i] for x in final_attn]) for i in range(3)]
    attn.append(jnp.concatenate([x[2 * n :] for x in final_feed]))
    feed = [x[:n] for x in final_feed] + [x[n : 2 * n] for x in final_feed]
    factor = (32 * rows) ** (-0.5)
    return outputs(layer_out, input_grad, attn, feed, vec, factor, 8)


def gather(local):
    return lax.all_gather(local, "fsdp", axis=1, tiled=True)


def reduce(grad):
    part = lax.psum_scatter(wide(grad), "fsdp", scatter_dimension=1, tiled=True)
    total = lax.psum(part.astype(bf16), "dp")
    return [total[b] for b in range(grad.shape[0])]


def body_plain(tokens, cotangent, doc_lengths, w_query, w_key, w_value, w_out, w_up, w_down, *vectors):
    rows = tokens.shape[0]
    shards, groups = lax.axis_size("fsdp"), lax.axis_size("dp")
    table = make_table(lax.all_gather(pack_vectors(*vectors), "fsdp", axis=0, tiled=True))
    attn_w = gather(jnp.stack([w_query, w_key, w_value, w_out]))
    feed_own = order_hidden(w_up, w_down, shards)
    doc = segment_ids(doc_lengths)
    scaled, _ = moments(wide(tokens))
    first = (scaled * table[GAIN_ONE] + table[SHIFT_ONE]).astype(bf16)
    qkv = qkv_call(first, attn_w, table)
    attended, probs = attn_fwd_call(qkv, doc)
    middle, second = out_call(attended, attn_w, tokens, table)
    acc, sg = middle, None
    feed = []
    up_bias = []
    for lead in range(feed_own.shape[0] // 4):
        w = gather(feed_own[4 * lead : 4 * lead + 4])
        grad, bias_grad, acc, sg = ffn_call(lead, second, cotangent, w, table, acc, sg)
        feed += reduce(grad)
        up_bias.append(bias_grad)
    mid_grad, attended_grad, mid_vec, layer_out, out_grad = mid_call(
        jnp.zeros((3,), jnp.int32), sg, middle, cotangent, attended, attn_w, table, acc, False
    )
    grads = attn_bwd_call(qkv, attended_grad, probs)
    proj_grad, proj_bias = wgrad_call(first, grads)
    part = input_call(grads, attn_w, tokens, mid_grad, table, 0)
    input_grad, in_vec = input_call(grads, attn_w, tokens, mid_grad, table, 1, part)
    attn = reduce(jnp.concatenate([proj_grad, out_grad]))
    none = jnp.zeros((1,) + proj_bias.shape[2:], f32)
    vec = jnp.concatenate([in_vec, mid_vec, proj_bias[:, 0], none] + [x[:, 0] for x in up_bias])
    vec = vec.reshape(vec.shape[0], shards, -1).transpose(1, 0, 2)
    vec = lax.psum(lax.psum_scatter(vec, "fsdp", scatter_dimension=0, tiled=True), "dp")[0]
    factor = (groups * shards * rows) ** (-0.5)
    return outputs(layer_out, input_grad, attn, feed, vec, factor, shards)


def solution(mesh):
    both = P(("dp", "fsdp"), None)
    matrix, vector = P("fsdp", None), P("fsdp")
    fast = mesh.shape["dp"] == 4 and mesh.shape["fsdp"] == 8
    return jax.shard_map(
        body_fast if fast else body_plain,
        mesh=mesh,
        in_specs=(both,) * 3 + (matrix,) * 6 + (vector,) * 9,
        out_specs=(both,) * 2 + (matrix,) * 6 + (vector,) * 9,
        check_vma=False,
    )
```

```python
from functools import partial

import jax
import jax.numpy as jnp
from jax import lax
from jax.experimental import pallas as pl
from jax.experimental.pallas import tpu as pltpu
from jax.sharding import PartitionSpec as P

H = 12
HD = 64
SEQ = 512
MOST = 160
BQ = 256
BAND = 416
GAIN_ONE, SHIFT_ONE, QUERY, KEY, VALUE, OUT, GAIN_TWO, SHIFT_TWO, DOWN, UP = range(10)
epsilon = 1e-05
bf16 = jnp.bfloat16
f32 = jnp.float32


def nn(a, b):
    return jnp.dot(a, b, preferred_element_type=f32)


def nt(a, b):
    return lax.dot_general(a, b, (((1,), (1,)), ((), ())), preferred_element_type=f32)


def tn(a, b):
    return lax.dot_general(a, b, (((0,), (0,)), ((), ())), preferred_element_type=f32)


def params(n, mb=56):
    return pltpu.CompilerParams(
        dimension_semantics=("arbitrary",) * n, vmem_limit_bytes=mb * 1024 * 1024
    )


def cost(flops, nbytes, trans=0):
    return pl.CostEstimate(
        flops=int(flops * 50), bytes_accessed=int(nbytes * 50), transcendentals=int(trans)
    )


def moments(v):
    mean = jnp.mean(v, axis=-1, keepdims=True)
    c = v - mean
    inv = lax.rsqrt(jnp.mean(c * c, axis=-1, keepdims=True) + epsilon)
    return c * inv, inv


def shares(place, sides):
    d, z, c = place[0], place[1], place[2]
    for p, (along, near, far) in enumerate(sides):
        core = c ^ p
        parts = ((d, along), (d ^ (1 + core), near), (d ^ (2 - core), far.at[0]), (d ^ 3, far.at[1]))
        for member, view in parts:
            for k in range(3):
                yield member, 2 * (z ^ (k + 1)) + core, view.at[k]


def by_sides(refs):
    return (refs[0], refs[4]), (refs[1:4], refs[5:8])


def start_all(pairs, sem):
    copies = [pltpu.make_async_copy(a, b, sem) for a, b in pairs]
    for copy in copies:
        copy.start()
    return copies


def wait_all(copies):
    for copy in copies:
        copy.wait()


def block_copies(place, refs, out, lead):
    rows = out.shape[1] // 8
    owns, sides = by_sides(refs)
    pairs = []
    for p, own in enumerate(owns):
        s = 2 * place[1] + (place[2] ^ p)
        pairs += [(own.at[4 * lead + b], out.at[b, pl.ds(s * rows, rows), :]) for b in range(4)]
    for member, s, view in shares(place, sides):
        pairs.append((view.at[pl.ds(0, rows), :], out.at[member, pl.ds(s * rows, rows), :]))
    return pairs


def row_copies(place, refs, out, source, skip):
    rows = out.shape[1] // 8
    few = rows // 4
    owns, sides = by_sides(refs)
    pairs = []
    for p, own in enumerate(owns):
        s = 2 * place[1] + (place[2] ^ p)
        for b in range(out.shape[0]):
            pairs.append((own.at[source + b], out.at[b, pl.ds(s * rows, rows), :]))
    for member, s, view in shares(place, sides):
        for b in range(out.shape[0]):
            to = pl.multiple_of(s * rows + member * few, 8)
            pairs.append((view.at[pl.ds(skip + b * few, few), :], out.at[b, pl.ds(to, few), :]))
    return pairs


def split_blocks(place, full, keep, send, b):
    rows = full.shape[0] // 8
    for k in range(4):
        keep[b, k] = full[pl.ds((2 * k + place[2]) * rows, rows), :].astype(bf16)
        send[b, k] = full[pl.ds((2 * k + 1 - place[2]) * rows, rows), :].astype(bf16)


ANY = pl.BlockSpec(memory_space=pl.ANY)


def qkv_kernel(x_ref, w_ref, b_ref, o_ref):
    b = b_ref[0]
    for r in range(x_ref.shape[0] // 256):
        rows = pl.ds(r * 256, 256)
        o_ref[0, rows, :] = (nn(x_ref[rows, :], w_ref[0]) + b).astype(bf16)


def qkv_call(first, w, table):
    rows, d = first.shape
    return pl.pallas_call(
        qkv_kernel,
        grid=(3,),
        in_specs=[
            pl.BlockSpec((rows, d), lambda i: (0, 0)),
            pl.BlockSpec((1, d, d), lambda i: (i, 0, 0)),
            pl.BlockSpec((1, 1, d), lambda i: (QUERY + i, 0, 0)),
        ],
        out_specs=pl.BlockSpec((1, rows, d), lambda i: (i, 0, 0)),
        out_shape=jax.ShapeDtypeStruct((3, rows, d), bf16),
        compiler_params=params(1),
        cost_estimate=cost(6 * rows * d * d, 2 * (rows * d * 4 + 3 * d * d)),
        name="qkv",
    )(first, w, table)


def qkv_fast_kernel(place, x_ref, b_ref, *refs):
    pieces, (o_ref, w_ref, sem) = refs[:8], refs[8:]
    i = pl.program_id(0)

    @pl.when(i == 0)
    def _():
        wait_all(start_all(row_copies(place, pieces, w_ref, 0, 0), sem))

    b = b_ref[0]
    for r in range(x_ref.shape[0] // 256):
        rows = pl.ds(r * 256, 256)
        o_ref[0, rows, :] = (nn(x_ref[rows, :], w_ref[i]) + b).astype(bf16)


def qkv_fast_call(place, first, table, pieces):
    rows, d = first.shape
    return pl.pallas_call(
        qkv_fast_kernel,
        grid_spec=pltpu.PrefetchScalarGridSpec(
            num_scalar_prefetch=1,
            grid=(3,),
            in_specs=[
                pl.BlockSpec((rows, d), lambda i, place: (0, 0)),
                pl.BlockSpec((1, 1, d), lambda i, place: (QUERY + i, 0, 0)),
            ]
            + [ANY] * 8,
            out_specs=[
                pl.BlockSpec((1, rows, d), lambda i, place: (i, 0, 0)),
                pl.BlockSpec((3, d, d), lambda i, place: (0, 0, 0)),
            ],
            scratch_shapes=[pltpu.SemaphoreType.DMA],
        ),
        out_shape=[
            jax.ShapeDtypeStruct((3, rows, d), bf16),
            jax.ShapeDtypeStruct((3, d, d), bf16),
        ],
        compiler_params=params(1),
        cost_estimate=cost(6 * rows * d * d, 2 * (rows * d * 4 + 8 * d * d)),
        name="qkv",
    )(place, first, table, *pieces)


def spans(b):
    return b * BQ, b * (SEQ - BAND)


def attn_fwd_kernel(q_ref, k_ref, v_ref, dr_ref, dc_ref, o_ref, p_ref, bias):
    @pl.when(pl.program_id(1) == 0)
    def _():
        for b in range(2):
            q0, k0 = spans(b)
            same = dc_ref[0, k0 : k0 + BAND, :] == dr_ref[0, :, q0 : q0 + BQ]
            bias[b] = jnp.where(same, 0.0, -3e38)

    low = lax.broadcasted_iota(jnp.int32, (1, 128), 1) < HD
    for b in range(2):
        q0, k0 = spans(b)
        qb = q_ref[0, q0 : q0 + BQ, :] * bf16(HD**-0.5)
        kb = k_ref[0, k0 : k0 + BAND, :]
        vb = v_ref[0, k0 : k0 + BAND, :]
        acc = None
        for hh in range(2):
            mine = low if hh == 0 else jnp.logical_not(low)
            s = nt(kb, jnp.where(mine, qb, bf16(0))) + bias[b]
            e = jnp.exp(s - jnp.max(s, axis=0, keepdims=True))
            p = (e * (1.0 / jnp.sum(e, axis=0, keepdims=True))).astype(bf16)
            p_ref[hh, b] = p
            part = tn(jnp.where(mine, vb, bf16(0)), p)
            acc = part if acc is None else acc + part
        o_ref[q0 : q0 + BQ, :] = acc.T.astype(bf16)


def attn_fwd_call(qkv, doc):
    rows = qkv.shape[1]
    d = qkv.shape[2]
    seqs = rows // SEQ
    hp = d // 128

    def part(i):
        return pl.BlockSpec((1, SEQ, 128), lambda s, h: (i, s, h))

    return pl.pallas_call(
        attn_fwd_kernel,
        grid=(seqs, hp),
        in_specs=[
            part(0),
            part(1),
            part(2),
            pl.BlockSpec((1, 1, SEQ), lambda s, h: (s, 0, 0)),
            pl.BlockSpec((1, SEQ, 1), lambda s, h: (s, 0, 0)),
        ],
        out_specs=[
            pl.BlockSpec((SEQ, 128), lambda s, h: (s, h)),
            pl.BlockSpec((2, 2, BAND, BQ), lambda s, h: (s * hp + h, 0, 0, 0)),
        ],
        out_shape=[
            jax.ShapeDtypeStruct((rows, d), bf16),
            jax.ShapeDtypeStruct((seqs * H, 2, BAND, BQ), bf16),
        ],
        scratch_shapes=[pltpu.VMEM((2, BAND, BQ), f32)],
        compiler_params=params(2),
        cost_estimate=cost(
            seqs * H * 2 * BAND * BQ * 2 * 256, 2 * 4 * rows * d + 4 * seqs * H * BAND * BQ
        ),
        name="attend",
    )(qkv, qkv, qkv, doc[:, None, :], doc[:, :, None])


def attn_bwd_kernel(q_ref, k_ref, v_ref, do_ref, p_ref, o_ref):
    low = lax.broadcasted_iota(jnp.int32, (1, 128), 1) < HD
    scale = bf16(HD**-0.5)
    over = SEQ - BAND
    tails = []
    for b in range(2):
        q0, k0 = spans(b)
        qb = q_ref[0, q0 : q0 + BQ, :] * scale
        dob = do_ref[q0 : q0 + BQ, :]
        kb = k_ref[0, k0 : k0 + BAND, :] * scale
        vb = v_ref[0, k0 : k0 + BAND, :]
        dq = dk = dv = None
        for hh in range(2):
            mine = low if hh == 0 else jnp.logical_not(low)
            p = p_ref[hh, b]
            dom = jnp.where(mine, dob, bf16(0))
            dp = nt(vb, dom)
            pf = p.astype(f32)
            inner = jnp.sum(pf * dp, axis=0, keepdims=True)
            ds = (pf * (dp - inner)).astype(bf16)
            a = nn(p, dom)
            c = nn(ds, jnp.where(mine, qb, bf16(0)))
            g = tn(jnp.where(mine, kb, bf16(0)), ds)
            dv = a if dv is None else dv + a
            dk = c if dk is None else dk + c
            dq = g if dq is None else dq + g
        o_ref[0, q0 : q0 + BQ, :] = dq.T.astype(bf16)
        tails.append((dk, dv))
    for i, (first_part, second_part) in enumerate(zip(*tails)):
        o_ref[i + 1, :over, :] = first_part[:over].astype(bf16)
        o_ref[i + 1, over:BAND, :] = (first_part[over:] + second_part[: BAND - over]).astype(bf16)
        o_ref[i + 1, BAND:, :] = second_part[BAND - over :].astype(bf16)


def attn_bwd_call(qkv, dattn, probs):
    rows = qkv.shape[1]
    d = qkv.shape[2]
    seqs = rows // SEQ
    hp = d // 128

    def part(i):
        return pl.BlockSpec((1, SEQ, 128), lambda s, h: (i, s, h))

    return pl.pallas_call(
        attn_bwd_kernel,
        grid=(seqs, hp),
        in_specs=[
            part(0),
            part(1),
            part(2),
            pl.BlockSpec((SEQ, 128), lambda s, h: (s, h)),
            pl.BlockSpec((2, 2, BAND, BQ), lambda s, h: (s * hp + h, 0, 0, 0)),
        ],
        out_specs=pl.BlockSpec((3, SEQ, 128), lambda s, h: (0, s, h)),
        out_shape=jax.ShapeDtypeStruct((3, rows, d), bf16),
        compiler_params=params(2),
        cost_estimate=cost(
            seqs * H * 2 * BAND * BQ * 2 * 256 * 2, 2 * 7 * rows * d + 4 * seqs * H * BAND * BQ
        ),
        name="attend_back",
    )(qkv, qkv, qkv, dattn, probs)


def row_of(i):
    return pl.BlockSpec((1, 1, 768), lambda *_: (i, 0, 0))


def out_step(a_ref, w, t_ref, bo_ref, g_ref, s_ref, mid_ref, sec_ref):
    mid = t_ref[...].astype(f32) + nn(a_ref[...], w) + bo_ref[0]
    mid_ref[...] = mid
    sc, _ = moments(mid)
    sec_ref[...] = (sc * g_ref[0] + s_ref[0]).astype(bf16)


def out_kernel(a_ref, w_ref, t_ref, bo_ref, g_ref, s_ref, mid_ref, sec_ref):
    out_step(a_ref, w_ref[0], t_ref, bo_ref, g_ref, s_ref, mid_ref, sec_ref)


def out_fast_kernel(place, a_ref, t_ref, bo_ref, g_ref, s_ref, *refs):
    pieces, (mid_ref, sec_ref, w_ref, sem) = refs[:8], refs[8:]

    @pl.when(pl.program_id(0) == 0)
    def _():
        wait_all(start_all(row_copies(place, pieces, w_ref, 8, w_ref.shape[1] // 8), sem))

    out_step(a_ref, w_ref[0], t_ref, bo_ref, g_ref, s_ref, mid_ref, sec_ref)


def out_fast_call(place, attended, tokens, table, pieces):
    rows, d = tokens.shape
    blk = pl.BlockSpec((256, d), lambda i, place: (i, 0))
    return pl.pallas_call(
        out_fast_kernel,
        grid_spec=pltpu.PrefetchScalarGridSpec(
            num_scalar_prefetch=1,
            grid=(rows // 256,),
            in_specs=[blk, blk, row_of(OUT), row_of(GAIN_TWO), row_of(SHIFT_TWO)] + [ANY] * 8,
            out_specs=[blk, blk, pl.BlockSpec((1, d, d), lambda i, place: (0, 0, 0))],
            scratch_shapes=[pltpu.SemaphoreType.DMA],
        ),
        out_shape=[
            jax.ShapeDtypeStruct((rows, d), f32),
            jax.ShapeDtypeStruct((rows, d), bf16),
            jax.ShapeDtypeStruct((1, d, d), bf16),
        ],
        compiler_params=params(1),
        cost_estimate=cost(2 * rows * d * d, rows * d * 10 + 4 * d * d),
        name="project",
    )(place, attended, tokens, table, table, table, *pieces)


def out_call(attended, wo, tokens, table):
    rows, d = tokens.shape
    blk = pl.BlockSpec((256, d), lambda i: (i, 0))
    return pl.pallas_call(
        out_kernel,
        grid=(rows // 256,),
        in_specs=[
            blk, pl.BlockSpec((1, d, d), lambda i: (3, 0, 0)), blk,
            row_of(OUT), row_of(GAIN_TWO), row_of(SHIFT_TWO),
        ],
        out_specs=[blk, blk],
        out_shape=[
            jax.ShapeDtypeStruct((rows, d), f32),
            jax.ShapeDtypeStruct((rows, d), bf16),
        ],
        compiler_params=params(1),
        cost_estimate=cost(2 * rows * d * d, rows * d * 10 + 2 * d * d),
        name="project",
    )(attended, wo, tokens, table, table, table)


def ffn_step(x_ref, g_ref, wu, wd, b, acc_ref, sg_ref, act, hg, gb_ref):
    rows = x_ref.shape[0]
    chunk = 256
    total = jnp.zeros((1, wu.shape[1]), f32)
    for r in range(rows // chunk):
        at = pl.ds(r * chunk, chunk)
        h = nn(x_ref[at, :], wu[...]) + b
        ag = nt(g_ref[at, :], wd[...])
        phi = 0.5 + 0.5 * lax.erf(h * (0.5**0.5))
        a = (h * phi).astype(bf16)
        act[at, :] = a
        dens = jnp.exp(-0.5 * (h * h)) * 0.3989422804014327
        hgv = (ag * (phi + h * dens)).astype(bf16)
        hg[at, :] = hgv
        total += jnp.sum(hgv.astype(f32), axis=0, keepdims=True)
        acc_ref[at, :] += nn(a, wd[...])
        sg_ref[at, :] += nt(hgv, wu[...])
    gb_ref[0] = total


def ffn_start(start, acc_in, bd_ref, sg_in, acc_ref, sg_ref):
    if start:
        acc_ref[...] = acc_in[...] + bd_ref[0]
        sg_ref[...] = jnp.zeros_like(sg_ref)
    else:
        acc_ref[...] = acc_in[...]
        sg_ref[...] = sg_in[...]


def ffn_kernel(start, x_ref, g_ref, w_ref, b_ref, acc_in, bd_ref, *refs):
    sg_in = None if start else refs[0]
    gw_ref, gb_ref, acc_ref, sg_ref, act, hg = refs[0 if start else 1 :]

    @pl.when(pl.program_id(0) == 0)
    def _():
        ffn_start(start, acc_in, bd_ref, sg_in, acc_ref, sg_ref)

    ffn_step(x_ref, g_ref, w_ref.at[0], w_ref.at[1], b_ref[0], acc_ref, sg_ref, act, hg, gb_ref)
    gw_ref[0] = tn(x_ref[...], hg[...]).astype(bf16)
    gw_ref[1] = tn(act[...], g_ref[...]).astype(bf16)


def ffn_call(lead, second, dgrad, w, table, acc, sg):
    rows, d = second.shape
    n = w.shape[0] // 2
    start = sg is None
    full = pl.BlockSpec((rows, d), lambda j: (0, 0))
    pair = pl.BlockSpec((2, d, d), lambda j: (j, 0, 0))
    return pl.pallas_call(
        partial(ffn_kernel, start),
        grid=(n,),
        in_specs=[
            full, full, pair, pl.BlockSpec((1, 1, d), lambda j: (UP + lead * n + j, 0, 0)),
            full, row_of(DOWN),
        ]
        + ([] if start else [full]),
        out_specs=[pair, pl.BlockSpec((1, 1, d), lambda j: (j, 0, 0)), full, full],
        out_shape=[
            jax.ShapeDtypeStruct((2 * n, d, d), bf16),
            jax.ShapeDtypeStruct((n, 1, d), f32),
            jax.ShapeDtypeStruct((rows, d), f32),
            jax.ShapeDtypeStruct((rows, d), f32),
        ],
        scratch_shapes=[pltpu.VMEM((rows, d), bf16)] * 2,
        compiler_params=params(1),
        cost_estimate=cost(12 * n * rows * d * d, 20 * rows * d + 8 * n * d * d),
        name="feed",
    )(second, dgrad, w, table, acc, table, *([] if start else [sg]))


def ffn_fast_kernel(start, lead, place, x_ref, g_ref, b_ref, acc_in, bd_ref, *refs):
    sg_in = None if start else refs[0]
    refs = refs[0 if start else 1 :]
    pieces = refs[:8]
    keep, send, gb_ref, acc_ref, sg_ref, w_ref, act, hg, full, sem = refs[8:]
    j = pl.program_id(0)

    @pl.when(j == 0)
    def _():
        copies = start_all(block_copies(place, pieces, w_ref, lead), sem)
        ffn_start(start, acc_in, bd_ref, sg_in, acc_ref, sg_ref)
        wait_all(copies)

    wu, wd = w_ref.at[2 * j], w_ref.at[2 * j + 1]
    ffn_step(x_ref, g_ref, wu, wd, b_ref[0], acc_ref, sg_ref, act, hg, gb_ref)
    full[...] = tn(x_ref[...], hg[...]).astype(bf16)
    split_blocks(place, full, keep, send, 0)
    full[...] = tn(act[...], g_ref[...]).astype(bf16)
    split_blocks(place, full, keep, send, 1)


def ffn_fast_call(lead, place, second, dgrad, table, acc, sg, pieces):
    rows, d = second.shape
    start = sg is None
    m = d // 8
    full = pl.BlockSpec((rows, d), lambda j, place: (0, 0))
    half = pl.BlockSpec((2, 4, m, d), lambda j, place: (j, 0, 0, 0))
    return pl.pallas_call(
        partial(ffn_fast_kernel, start, lead),
        grid_spec=pltpu.PrefetchScalarGridSpec(
            num_scalar_prefetch=1,
            grid=(2,),
            in_specs=[
                full, full, pl.BlockSpec((1, 1, d), lambda j, place: (UP + lead * 2 + j, 0, 0)),
                full, row_of(DOWN),
            ]
            + ([] if start else [full])
            + [ANY] * 8,
            out_specs=[half, half, pl.BlockSpec((1, 1, d), lambda j, place: (j, 0, 0)), full, full],
            scratch_shapes=[pltpu.VMEM((4, d, d), bf16)]
            + [pltpu.VMEM((rows, d), bf16)] * 2
            + [pltpu.VMEM((d, d), bf16), pltpu.SemaphoreType.DMA],
        ),
        out_shape=[
            jax.ShapeDtypeStruct((4, 4, m, d), bf16),
            jax.ShapeDtypeStruct((4, 4, m, d), bf16),
            jax.ShapeDtypeStruct((2, 1, d), f32),
            jax.ShapeDtypeStruct((rows, d), f32),
            jax.ShapeDtypeStruct((rows, d), f32),
        ],
        compiler_params=params(1),
        cost_estimate=cost(24 * rows * d * d, 20 * rows * d + 16 * d * d),
        name="feed",
    )(place, second, dgrad, table, acc, table, *([] if start else [sg]), *pieces)


def norm_back(grad, sc, inv, gain):
    t = grad * gain
    return inv * (
        t - jnp.mean(t, axis=-1, keepdims=True) - sc * jnp.mean(t * sc, axis=-1, keepdims=True)
    )


def mid_kernel(
    place, sg_ref, mid_ref, dy_ref, a_ref, w_ref, g_ref, acc_ref,
    mg_ref, ag_ref, vec_ref, lo_ref, wg_ref, *rest,
):
    i = pl.program_id(0)
    wacc = rest[-1]

    @pl.when(i == 0)
    def _():
        wacc[...] = jnp.zeros_like(wacc)
        vec_ref[...] = jnp.zeros_like(vec_ref)

    lo_ref[...] = acc_ref[...].astype(bf16)
    sc, inv = moments(mid_ref[...])
    sg = sg_ref[...]
    dy = dy_ref[...].astype(f32)
    mg = dy + norm_back(sg, sc, inv, g_ref[0])
    mg_ref[...] = mg
    br = mg.astype(bf16)
    vec_ref[0:1, :] += jnp.sum(sg * sc, axis=0, keepdims=True)
    vec_ref[1:2, :] += jnp.sum(sg, axis=0, keepdims=True)
    vec_ref[2:3, :] += jnp.sum(br.astype(f32), axis=0, keepdims=True)
    vec_ref[3:4, :] += jnp.sum(dy, axis=0, keepdims=True)
    ag_ref[...] = nt(br, w_ref[0]).astype(bf16)
    wacc[...] += tn(a_ref[...], br)

    @pl.when(i == pl.num_programs(0) - 1)
    def _():
        if len(rest) == 1:
            wg_ref[0] = wacc[...].astype(bf16)
        else:
            split_blocks(place, wacc, wg_ref, rest[0], 0)


def mid_call(place, sg, mid, dy, attended, wo, table, acc, split):
    rows, d = sg.shape
    blk = pl.BlockSpec((256, d), lambda i, place: (i, 0))
    grad = (1, 4, d // 8, d) if split else (1, d, d)
    last = wo.shape[0] - 1
    return pl.pallas_call(
        mid_kernel,
        grid_spec=pltpu.PrefetchScalarGridSpec(
            num_scalar_prefetch=1,
            grid=(rows // 256,),
            in_specs=[
                blk, blk, blk, blk, pl.BlockSpec((1, d, d), lambda i, place: (last, 0, 0)),
                row_of(GAIN_TWO), blk,
            ],
            out_specs=[blk, blk, pl.BlockSpec((8, d), lambda i, place: (0, 0)), blk]
            + [pl.BlockSpec(grad, lambda i, place: (0,) * len(grad))] * (2 if split else 1),
            scratch_shapes=[pltpu.VMEM((d, d), f32)],
        ),
        out_shape=[
            jax.ShapeDtypeStruct((rows, d), f32),
            jax.ShapeDtypeStruct((rows, d), bf16),
            jax.ShapeDtypeStruct((8, d), f32),
            jax.ShapeDtypeStruct((rows, d), bf16),
        ]
        + [jax.ShapeDtypeStruct(grad, bf16)] * (2 if split else 1),
        compiler_params=params(1),
        cost_estimate=cost(4 * rows * d * d, rows * d * 22 + 4 * d * d),
        name="middle_back",
    )(place, sg, mid, dy, attended, wo, table, acc)


def wgrad_kernel(x_ref, g_ref, o_ref, b_ref):
    o_ref[0] = tn(x_ref[...], g_ref[0]).astype(bf16)
    b_ref[0] = jnp.sum(g_ref[0].astype(f32), axis=0, keepdims=True)


def wgrad_call(first, grads):
    rows, d = first.shape
    return pl.pallas_call(
        wgrad_kernel,
        grid=(3,),
        in_specs=[
            pl.BlockSpec((rows, d), lambda i: (0, 0)),
            pl.BlockSpec((1, rows, d), lambda i: (i, 0, 0)),
        ],
        out_specs=[
            pl.BlockSpec((1, d, d), lambda i: (i, 0, 0)),
            pl.BlockSpec((1, 1, d), lambda i: (i, 0, 0)),
        ],
        out_shape=[
            jax.ShapeDtypeStruct((3, d, d), bf16),
            jax.ShapeDtypeStruct((3, 1, d), f32),
        ],
        compiler_params=params(1),
        cost_estimate=cost(6 * rows * d * d, 2 * (rows * d * 4 + 3 * d * d)),
        name="weight_back",
    )(first, grads)


def wgrad_fast_kernel(place, x_ref, g_ref, keep, send, b_ref, full):
    full[...] = tn(x_ref[...], g_ref[0])
    b_ref[0] = jnp.sum(g_ref[0].astype(f32), axis=0, keepdims=True)
    split_blocks(place, full, keep, send, 0)


def wgrad_fast_call(place, first, grads):
    rows, d = first.shape
    m = d // 8
    half = pl.BlockSpec((1, 4, m, d), lambda i, place: (i, 0, 0, 0))
    return pl.pallas_call(
        wgrad_fast_kernel,
        grid_spec=pltpu.PrefetchScalarGridSpec(
            num_scalar_prefetch=1,
            grid=(3,),
            in_specs=[
                pl.BlockSpec((rows, d), lambda i, place: (0, 0)),
                pl.BlockSpec((1, rows, d), lambda i, place: (i, 0, 0)),
            ],
            out_specs=[half, half, pl.BlockSpec((1, 1, d), lambda i, place: (i, 0, 0))],
            scratch_shapes=[pltpu.VMEM((d, d), f32)],
        ),
        out_shape=[
            jax.ShapeDtypeStruct((3, 4, m, d), bf16),
            jax.ShapeDtypeStruct((3, 4, m, d), bf16),
            jax.ShapeDtypeStruct((3, 1, d), f32),
        ],
        compiler_params=params(1),
        cost_estimate=cost(6 * rows * d * d, 2 * (rows * d * 4 + 3 * d * d)),
        name="weight_back",
    )(place, first, grads)


def input_kernel(start, g_ref, w_ref, t_ref, mg_ref, gain_ref, *refs):
    o_ref, vec_ref = refs[-2:]

    @pl.when(pl.program_id(0) == 0)
    def _():
        vec_ref[...] = jnp.zeros_like(vec_ref) if start else refs[0][...]

    fg = nt(g_ref[0], w_ref[0]) + nt(g_ref[1], w_ref[1]) + nt(g_ref[2], w_ref[2])
    sc, inv = moments(t_ref[...].astype(f32))
    o_ref[...] = (mg_ref[...] + norm_back(fg, sc, inv, gain_ref[0])).astype(bf16)
    vec_ref[0:1, :] += jnp.sum(fg * sc, axis=0, keepdims=True)
    vec_ref[1:2, :] += jnp.sum(fg, axis=0, keepdims=True)


def input_call(grads, w, tokens, mg, table, skip, steps, before=()):
    rows, d = tokens.shape
    blk = pl.BlockSpec((256, d), lambda i: (skip + i, 0))
    vec = pl.BlockSpec((8, d), lambda i: (0, 0))
    start = not before
    return pl.pallas_call(
        partial(input_kernel, start),
        grid=(steps,),
        in_specs=[
            pl.BlockSpec((3, 256, d), lambda i: (0, skip + i, 0)),
            pl.BlockSpec((3, d, d), lambda i: (0, 0, 0)),
            blk,
            blk,
            row_of(GAIN_ONE),
        ]
        + ([] if start else [vec, ANY]),
        out_specs=[blk, vec],
        out_shape=[
            jax.ShapeDtypeStruct((rows, d), bf16),
            jax.ShapeDtypeStruct((8, d), f32),
        ],
        input_output_aliases={} if start else {6: 0},
        compiler_params=params(1),
        cost_estimate=cost(1536 * steps * d * d, 256 * steps * d * 14 + 6 * d * d),
        name="input_back",
    )(grads, w, tokens, mg, table, *([] if start else [before[1], before[0]]))


CORE = 1
ALONG = (2, 4, 6)
GROUP = (8, 16, 24)


def hop(x, mask):
    return lax.ppermute(x, ("dp", "fsdp"), [(i, i ^ mask) for i in range(32)])


def group_hop(x, second):
    pairs = [(i, i ^ (GROUP[0] if i % 2 == second else GROUP[1])) for i in range(32)]
    return lax.ppermute(x, ("dp", "fsdp"), pairs)


def pick(x, index, axis=0):
    return lax.dynamic_index_in_dim(x, index, axis, keepdims=False)


def after(deps, *xs):
    return lax.optimization_barrier((*xs, *deps))[: len(xs)]


def wide(x):
    return x.astype(f32)


def add_core(keep, got):
    return (wide(keep) + wide(got)).astype(bf16)


def quarter(x, index, axis):
    n = x.shape[axis] // 4
    return lax.dynamic_slice_in_dim(x, index * n, n, axis)


def add_two(a, b):
    return (wide(a) + wide(b)).astype(bf16)


def turn(x, bits):
    for axis, bit in enumerate(bits):
        x = jnp.where(bit == 0, x, jnp.flip(x, axis))
    return x


def add_all(first, others):
    total = wide(first)
    for other in others:
        total = total + wide(other)
    return total.astype(bf16)


def segment_ids(lengths):
    ends = jnp.cumsum(lengths, axis=-1)
    places = jnp.arange(SEQ, dtype=jnp.int32)
    return jnp.sum((places[None, :, None] >= ends[:, None, :]).astype(jnp.int32), axis=-1)


def pack_vectors(pre_gain, pre_shift, bias_query, bias_value, bias_out, mid_gain, mid_shift, bias_up, bias_down):
    none = jnp.zeros_like(bias_query)
    return jnp.concatenate(
        [pre_gain, pre_shift, bias_query, none, bias_value, bias_out, mid_gain, mid_shift, bias_down, bias_up]
    )[None]


def make_table(small):
    shards = small.shape[0]
    n = small.shape[1] * shards // 768
    return small.reshape(shards, n, -1).transpose(1, 0, 2).reshape(n, 1, 768).astype(f32)


def order_hidden(w_up, w_down, shards):
    m, d = w_up.shape[0], w_up.shape[0] * shards
    parts = w_down.shape[0] // m
    up = w_up.reshape(m, shards, parts, m).transpose(2, 0, 1, 3).reshape(parts, m, d)
    return jnp.stack([up, w_down.reshape(parts, m, d)], 1).reshape(2 * parts, m, d)


VEC_ROWS = (0, 1, 16, 18, 10, 8, 9)
DOWN_ROW, UP_ROW = 11, 20


def outputs(layer_out, input_grad, attn, feed, vec, factor, shards):
    m, d = attn[0].shape
    parts = len(feed) // 2
    vec = vec * factor
    up = jnp.stack(feed[0::2]).reshape(parts, m, shards, m).transpose(1, 2, 0, 3)
    return (
        layer_out,
        input_grad,
        *(wide(g) * factor for g in attn),
        wide(up.reshape(m, parts * d)) * factor,
        wide(jnp.concatenate(feed[1::2])) * factor,
        *(vec[i] for i in VEC_ROWS),
        vec[UP_ROW:].reshape(-1),
        vec[DOWN_ROW],
    )


def body_fast(tokens, cotangent, doc_lengths, w_query, w_key, w_value, w_out, w_up, w_down, *vectors):
    rows, d = tokens.shape
    n = d // 8
    dp, at = lax.axis_index("dp"), lax.axis_index("fsdp")
    z, core = at // 2, at % 2
    place = jnp.stack([dp, z, core]).astype(jnp.int32)
    one, two = 1 + core, 2 - core

    small = pack_vectors(*vectors)
    width = small.shape[1]
    low = jnp.pad(small[0], (0, 8 * d - width)).reshape(8, d)
    quarters = [quarter(w, dp, 0) for w in (w_query, w_key, w_value, w_out)]
    attn_mine = jnp.concatenate(quarters[:3] + [low])
    attn_z = [hop(attn_mine, m) for m in ALONG]
    attn_own = jnp.stack([w_query, w_key, w_value, jnp.pad(low, ((0, n - 8), (0, 0)))])
    attn_own_cross = hop(attn_own, CORE)
    attn_along = jnp.stack(attn_z)
    attn_near = group_hop(attn_along, 0)
    attn_along_cross = hop(attn_along, CORE)
    attn_far = group_hop(jnp.stack([attn_along, attn_near]), 1)
    attn_near_cross = hop(attn_near, CORE)
    attn_far_cross = hop(attn_far, CORE)
    lows = jnp.concatenate(
        [
            jnp.stack([low, attn_own_cross[3, :8]])[None],
            jnp.stack([attn_along[:, n - n // 4 :], attn_along_cross[:, n - n // 4 :]], 1),
        ]
    )
    small = lows.reshape(2, 2, 2, 8 * d)[..., :width]
    table = make_table(turn(small, (z // 2, z % 2, core)).reshape(8, width))

    feed_own = order_hidden(w_up, w_down, 8)
    mine_one = jnp.concatenate([pick(feed_own[:4], dp), quarters[3]])
    mine_two = pick(feed_own[4:], dp)
    feed_own = jnp.concatenate([feed_own, w_out[None]])
    tokens_late, lengths_late, mine_one = after([attn_along], tokens, doc_lengths, mine_one)
    across_one = hop(mine_one, ALONG[1])
    mine_late, across_late = after([attn_near], mine_one, across_one)
    beside_one = hop(jnp.stack([mine_late, across_late]), ALONG[0])
    beside_one, mine_two = after([attn_far], beside_one, mine_two)
    along_one = jnp.stack([beside_one[0], across_one, beside_one[1]])
    near_one = group_hop(along_one, 0)
    across_two = hop(mine_two, ALONG[1])

    doc = segment_ids(lengths_late)
    scaled, _ = moments(wide(tokens_late))
    first = (scaled * table[GAIN_ONE] + table[SHIFT_ONE]).astype(bf16)
    qkv, attn_w = qkv_fast_call(
        place, first, table,
        [attn_own, attn_along, attn_near, attn_far]
        + [attn_own_cross, attn_along_cross, attn_near_cross, attn_far_cross],
    )
    feed_own_late, along_one, near_one, mine_two, across_two = after(
        [qkv], feed_own, along_one, near_one, mine_two, across_two
    )
    (qkv,) = after([near_one, across_two], qkv)
    far_one = group_hop(jnp.stack([along_one, near_one]), 1)
    beside_two = hop(jnp.stack([mine_two, across_two]), ALONG[0])
    feed_cross = hop(feed_own_late, CORE)
    pieces_one = [feed_cross, hop(along_one, CORE), hop(near_one, CORE)]
    attended, probs = attn_fwd_call(qkv, doc)
    far_one, beside_two, attended_late = after([attended], far_one, beside_two, attended)
    (attended_late,) = after([far_one, beside_two], attended_late)
    pieces_one = [feed_own, along_one, near_one, far_one, *pieces_one, hop(far_one, CORE)]
    along_two = jnp.stack([beside_two[0], across_two, beside_two[1]])
    near_two = group_hop(along_two, 0)
    middle, second, wo = out_fast_call(place, attended_late, tokens, table, pieces_one)
    along_two, near_two, second = after([middle], along_two, near_two, second)
    (second,) = after([near_two], second)
    far_two = group_hop(jnp.stack([along_two, near_two]), 1)
    pieces_two = [along_two, near_two, far_two]
    pieces_two = [feed_own, *pieces_two, feed_cross, *(hop(x, CORE) for x in pieces_two)]

    def first_hop(parts):
        return group_hop(jnp.stack([parts(dp ^ one), parts(dp ^ 3)]), 0)

    def fold(parts, got):
        return add_two(parts(dp), got[0]), add_two(parts(dp ^ two), got[1])

    def beside(x):
        return jnp.stack([pick(x, z ^ 1), pick(x, z ^ 3)])

    def across(x, got):
        return add_two(pick(x, z), got[0]), add_two(pick(x, z ^ 2), got[1])

    keep_one, send_one, up_bias_one, acc, sg = ffn_fast_call(
        0, place, second, cotangent, table, middle, None, pieces_one
    )
    (send_one,) = after([far_two], send_one)
    got_one = hop(send_one, CORE)
    parts_one = lambda i: add_two(pick(keep_one, i), pick(got_one, i))
    near_one = first_hop(parts_one)
    (sg,) = after([got_one], sg)
    keep_two, send_two, up_bias_two, acc, sg = ffn_fast_call(
        1, place, second, cotangent, table, acc, sg, pieces_two
    )
    got_two = hop(send_two, CORE)
    (sg,) = after([near_one], sg)
    mine_one, far_one = fold(parts_one, near_one)
    (sg,) = after([far_one], sg)
    far_one = group_hop(far_one, 1)
    mid_grad, attended_grad, mid_vec, layer_out, keep_out, send_out = mid_call(
        place, sg, middle, cotangent, attended, wo, table, acc, True
    )
    got_out = hop(send_out, CORE)
    (attended_grad,) = after([far_one, got_two, got_out], attended_grad)
    sum_one = add_two(mine_one, far_one)
    beside_one = hop(beside(sum_one), ALONG[0])

    def parts_two(i):
        out = add_two(quarter(keep_out[0], i, 1), quarter(got_out[0], i, 1))
        return jnp.concatenate([add_two(pick(keep_two, i), pick(got_two, i)), out], 1)

    near_two = first_hop(parts_two)
    grads = attn_bwd_call(qkv, attended_grad, probs)
    (beside_one,) = after([grads], beside_one)
    mine_one, across_one = across(sum_one, beside_one)
    mine_two, far_two = fold(parts_two, near_two)
    (grads,) = after([across_one, far_two], grads)
    across_one = hop(across_one, ALONG[1])
    far_two = group_hop(far_two, 1)
    keep_attn, send_attn, proj_bias = wgrad_fast_call(place, first, grads)
    got_attn = hop(send_attn, CORE)
    sum_two = add_two(mine_two, far_two)
    beside_two = beside(sum_two)
    (got_attn,) = after([beside_two], got_attn)
    (grads,) = after([beside_two, got_attn], grads)
    beside_two = hop(beside_two, ALONG[0])
    parts_attn = lambda i: add_two(quarter(keep_attn, i, 2), quarter(got_attn, i, 2))
    near_attn = first_hop(parts_attn)
    part = input_call(grads, attn_w, tokens, mid_grad, table, 0, rows // 256 - 1)
    near_attn, beside_two, across_one = after([part[1]], near_attn, beside_two, across_one)
    mine_attn, far_attn = fold(parts_attn, near_attn)
    mine_two, across_two = across(sum_two, beside_two)
    (grads,) = after([across_two, far_attn], grads)
    far_attn = group_hop(far_attn, 1)
    across_two = hop(across_two, ALONG[1])
    input_grad, in_vec = input_call(grads, attn_w, tokens, mid_grad, table, rows // 256 - 1, 1, part)

    across_two, far_attn = after([in_vec], across_two, far_attn)
    final_feed = jnp.concatenate([add_two(mine_one, across_one), add_two(mine_two, across_two)])
    none = jnp.zeros((1, d), f32)
    vec = jnp.concatenate(
        [in_vec, mid_vec, proj_bias[:, 0], none, up_bias_one[:, 0], up_bias_two[:, 0]]
    )
    (vec,) = after((), vec)
    vec = vec.reshape(24, 4, 2, n).transpose(2, 1, 0, 3)
    vec = pick(vec, core) + hop(pick(vec, 1 - core), CORE)
    vec = vec.reshape(4, 24 * n // d, d).astype(bf16)
    few = vec.shape[1]
    attn_sum = add_two(mine_attn, far_attn)
    many = attn_sum.shape[0] * attn_sum.shape[2]
    rest = jnp.concatenate(
        [attn_sum.transpose(1, 0, 2, 3).reshape(4, many, d), vec, jnp.zeros((4, 8 - few, d), bf16)], 1
    )
    mine_rest, across_rest = across(rest, hop(beside(rest), ALONG[0]))
    final_feed = [final_feed] + [hop(final_feed, m) for m in GROUP]
    final_rest = add_two(mine_rest, hop(across_rest, ALONG[1]))
    (final_rest,) = after(final_feed, final_rest)
    final_rest = jnp.stack([final_rest] + [hop(final_rest, m) for m in GROUP])
    vec = jnp.sum(wide(final_rest[:, many : many + few]), axis=0).reshape(24, n)
    final_feed = jnp.stack(final_feed)
    final_attn = [pick(final_rest, dp ^ b)[:many].reshape(3, many // 3, d) for b in range(4)]
    final_feed = [pick(final_feed, dp ^ b) for b in range(4)]
    attn = [jnp.concatenate([x[i] for x in final_attn]) for i in range(3)]
    attn.append(jnp.concatenate([x[2 * n :] for x in final_feed]))
    feed = [x[:n] for x in final_feed] + [x[n : 2 * n] for x in final_feed]
    factor = (32 * rows) ** (-0.5)
    return outputs(layer_out, input_grad, attn, feed, vec, factor, 8)


def gather(local):
    return lax.all_gather(local, "fsdp", axis=1, tiled=True)


def reduce(grad):
    part = lax.psum_scatter(wide(grad), "fsdp", scatter_dimension=1, tiled=True)
    total = lax.psum(part.astype(bf16), "dp")
    return [total[b] for b in range(grad.shape[0])]


def body_plain(tokens, cotangent, doc_lengths, w_query, w_key, w_value, w_out, w_up, w_down, *vectors):
    rows = tokens.shape[0]
    shards, groups = lax.axis_size("fsdp"), lax.axis_size("dp")
    table = make_table(lax.all_gather(pack_vectors(*vectors), "fsdp", axis=0, tiled=True))
    attn_w = gather(jnp.stack([w_query, w_key, w_value, w_out]))
    feed_own = order_hidden(w_up, w_down, shards)
    doc = segment_ids(doc_lengths)
    scaled, _ = moments(wide(tokens))
    first = (scaled * table[GAIN_ONE] + table[SHIFT_ONE]).astype(bf16)
    qkv = qkv_call(first, attn_w, table)
    attended, probs = attn_fwd_call(qkv, doc)
    middle, second = out_call(attended, attn_w, tokens, table)
    acc, sg = middle, None
    feed = []
    up_bias = []
    for lead in range(feed_own.shape[0] // 4):
        w = gather(feed_own[4 * lead : 4 * lead + 4])
        grad, bias_grad, acc, sg = ffn_call(lead, second, cotangent, w, table, acc, sg)
        feed += reduce(grad)
        up_bias.append(bias_grad)
    mid_grad, attended_grad, mid_vec, layer_out, out_grad = mid_call(
        jnp.zeros((3,), jnp.int32), sg, middle, cotangent, attended, attn_w, table, acc, False
    )
    grads = attn_bwd_call(qkv, attended_grad, probs)
    proj_grad, proj_bias = wgrad_call(first, grads)
    input_grad, in_vec = input_call(grads, attn_w, tokens, mid_grad, table, 0, tokens.shape[0] // 256)
    attn = reduce(jnp.concatenate([proj_grad, out_grad]))
    none = jnp.zeros((1,) + proj_bias.shape[2:], f32)
    vec = jnp.concatenate([in_vec, mid_vec, proj_bias[:, 0], none] + [x[:, 0] for x in up_bias])
    vec = vec.reshape(vec.shape[0], shards, -1).transpose(1, 0, 2)
    vec = lax.psum(lax.psum_scatter(vec, "fsdp", scatter_dimension=0, tiled=True), "dp")[0]
    factor = (groups * shards * rows) ** (-0.5)
    return outputs(layer_out, input_grad, attn, feed, vec, factor, shards)


def solution(mesh):
    both = P(("dp", "fsdp"), None)
    matrix, vector = P("fsdp", None), P("fsdp")
    fast = mesh.shape["dp"] == 4 and mesh.shape["fsdp"] == 8
    return jax.shard_map(
        body_fast if fast else body_plain,
        mesh=mesh,
        in_specs=(both,) * 3 + (matrix,) * 6 + (vector,) * 9,
        out_specs=(both,) * 2 + (matrix,) * 6 + (vector,) * 9,
        check_vma=False,
    )
```

```python
from functools import partial

import jax
import jax.numpy as jnp
from jax import lax
from jax.experimental import pallas as pl
from jax.experimental.pallas import tpu as pltpu
from jax.sharding import PartitionSpec as P

H = 12
HD = 64
SEQ = 512
MOST = 160
BQ = 256
BAND = 416
GAIN_ONE, SHIFT_ONE, QUERY, KEY, VALUE, OUT, GAIN_TWO, SHIFT_TWO, DOWN, UP = range(10)
epsilon = 1e-05
bf16 = jnp.bfloat16
f32 = jnp.float32


def nn(a, b):
    return jnp.dot(a, b, preferred_element_type=f32)


def nt(a, b):
    return lax.dot_general(a, b, (((1,), (1,)), ((), ())), preferred_element_type=f32)


def tn(a, b):
    return lax.dot_general(a, b, (((0,), (0,)), ((), ())), preferred_element_type=f32)


def params(n, mb=56):
    return pltpu.CompilerParams(
        dimension_semantics=("arbitrary",) * n, vmem_limit_bytes=mb * 1024 * 1024
    )


def cost(flops, nbytes, trans=0):
    return pl.CostEstimate(
        flops=int(flops * 50), bytes_accessed=int(nbytes * 50), transcendentals=int(trans)
    )


def moments(v):
    mean = jnp.mean(v, axis=-1, keepdims=True)
    c = v - mean
    inv = lax.rsqrt(jnp.mean(c * c, axis=-1, keepdims=True) + epsilon)
    return c * inv, inv


def shares(place, sides):
    d, z, c = place[0], place[1], place[2]
    for p, (along, near, far) in enumerate(sides):
        core = c ^ p
        parts = ((d, along), (d ^ (1 + core), near), (d ^ (2 - core), far.at[0]), (d ^ 3, far.at[1]))
        for member, view in parts:
            for k in range(3):
                yield member, 2 * (z ^ (k + 1)) + core, view.at[k]


def by_sides(refs):
    return (refs[0], refs[4]), (refs[1:4], refs[5:8])


def start_all(pairs, sem):
    copies = [pltpu.make_async_copy(a, b, sem) for a, b in pairs]
    for copy in copies:
        copy.start()
    return copies


def wait_all(copies):
    for copy in copies:
        copy.wait()


def block_copies(place, refs, out, lead):
    rows = out.shape[1] // 8
    owns, sides = by_sides(refs)
    pairs = []
    for p, own in enumerate(owns):
        s = 2 * place[1] + (place[2] ^ p)
        pairs += [(own.at[4 * lead + b], out.at[b, pl.ds(s * rows, rows), :]) for b in range(4)]
    for member, s, view in shares(place, sides):
        pairs.append((view.at[pl.ds(0, rows), :], out.at[member, pl.ds(s * rows, rows), :]))
    return pairs


def row_copies(place, refs, out, source, skip):
    rows = out.shape[1] // 8
    few = rows // 4
    owns, sides = by_sides(refs)
    pairs = []
    for p, own in enumerate(owns):
        s = 2 * place[1] + (place[2] ^ p)
        for b in range(out.shape[0]):
            pairs.append((own.at[source + b], out.at[b, pl.ds(s * rows, rows), :]))
    for member, s, view in shares(place, sides):
        for b in range(out.shape[0]):
            to = pl.multiple_of(s * rows + member * few, 8)
            pairs.append((view.at[pl.ds(skip + b * few, few), :], out.at[b, pl.ds(to, few), :]))
    return pairs


def split_blocks(place, full, keep, send, b):
    rows = full.shape[0] // 8
    for k in range(4):
        keep[b, k] = full[pl.ds((2 * k + place[2]) * rows, rows), :].astype(bf16)
        send[b, k] = full[pl.ds((2 * k + 1 - place[2]) * rows, rows), :].astype(bf16)


ANY = pl.BlockSpec(memory_space=pl.ANY)


def qkv_kernel(x_ref, w_ref, b_ref, o_ref):
    b = b_ref[0]
    for r in range(x_ref.shape[0] // 256):
        rows = pl.ds(r * 256, 256)
        o_ref[0, rows, :] = (nn(x_ref[rows, :], w_ref[0]) + b).astype(bf16)


def qkv_call(first, w, table):
    rows, d = first.shape
    return pl.pallas_call(
        qkv_kernel,
        grid=(3,),
        in_specs=[
            pl.BlockSpec((rows, d), lambda i: (0, 0)),
            pl.BlockSpec((1, d, d), lambda i: (i, 0, 0)),
            pl.BlockSpec((1, 1, d), lambda i: (QUERY + i, 0, 0)),
        ],
        out_specs=pl.BlockSpec((1, rows, d), lambda i: (i, 0, 0)),
        out_shape=jax.ShapeDtypeStruct((3, rows, d), bf16),
        compiler_params=params(1),
        cost_estimate=cost(6 * rows * d * d, 2 * (rows * d * 4 + 3 * d * d)),
        name="qkv",
    )(first, w, table)


def qkv_fast_kernel(place, x_ref, b_ref, *refs):
    pieces, (o_ref, w_ref, sem) = refs[:8], refs[8:]
    i = pl.program_id(0)

    @pl.when(i == 0)
    def _():
        wait_all(start_all(row_copies(place, pieces, w_ref, 0, 0), sem))

    b = b_ref[0]
    for r in range(x_ref.shape[0] // 256):
        rows = pl.ds(r * 256, 256)
        o_ref[0, rows, :] = (nn(x_ref[rows, :], w_ref[i]) + b).astype(bf16)


def qkv_fast_call(place, first, table, pieces):
    rows, d = first.shape
    return pl.pallas_call(
        qkv_fast_kernel,
        grid_spec=pltpu.PrefetchScalarGridSpec(
            num_scalar_prefetch=1,
            grid=(3,),
            in_specs=[
                pl.BlockSpec((rows, d), lambda i, place: (0, 0)),
                pl.BlockSpec((1, 1, d), lambda i, place: (QUERY + i, 0, 0)),
            ]
            + [ANY] * 8,
            out_specs=[
                pl.BlockSpec((1, rows, d), lambda i, place: (i, 0, 0)),
                pl.BlockSpec((3, d, d), lambda i, place: (0, 0, 0)),
            ],
            scratch_shapes=[pltpu.SemaphoreType.DMA],
        ),
        out_shape=[
            jax.ShapeDtypeStruct((3, rows, d), bf16),
            jax.ShapeDtypeStruct((3, d, d), bf16),
        ],
        compiler_params=params(1),
        cost_estimate=cost(6 * rows * d * d, 2 * (rows * d * 4 + 8 * d * d)),
        name="qkv",
    )(place, first, table, *pieces)


def spans(b):
    return b * BQ, b * (SEQ - BAND)


def attn_fwd_kernel(q_ref, k_ref, v_ref, dr_ref, dc_ref, o_ref, p_ref, bias):
    @pl.when(pl.program_id(1) == 0)
    def _():
        for b in range(2):
            q0, k0 = spans(b)
            same = dc_ref[0, k0 : k0 + BAND, :] == dr_ref[0, :, q0 : q0 + BQ]
            bias[b] = jnp.where(same, 0.0, -3e38)

    low = lax.broadcasted_iota(jnp.int32, (1, 128), 1) < HD
    for b in range(2):
        q0, k0 = spans(b)
        qb = q_ref[0, q0 : q0 + BQ, :] * bf16(HD**-0.5)
        kb = k_ref[0, k0 : k0 + BAND, :]
        vb = v_ref[0, k0 : k0 + BAND, :]
        acc = None
        for hh in range(2):
            mine = low if hh == 0 else jnp.logical_not(low)
            s = nt(kb, jnp.where(mine, qb, bf16(0))) + bias[b]
            e = jnp.exp(s - jnp.max(s, axis=0, keepdims=True))
            p = (e * (1.0 / jnp.sum(e, axis=0, keepdims=True))).astype(bf16)
            p_ref[hh, b] = p
            part = tn(jnp.where(mine, vb, bf16(0)), p)
            acc = part if acc is None else acc + part
        o_ref[q0 : q0 + BQ, :] = acc.T.astype(bf16)


def attn_fwd_call(qkv, doc):
    rows = qkv.shape[1]
    d = qkv.shape[2]
    seqs = rows // SEQ
    hp = d // 128

    def part(i):
        return pl.BlockSpec((1, SEQ, 128), lambda s, h: (i, s, h))

    return pl.pallas_call(
        attn_fwd_kernel,
        grid=(seqs, hp),
        in_specs=[
            part(0),
            part(1),
            part(2),
            pl.BlockSpec((1, 1, SEQ), lambda s, h: (s, 0, 0)),
            pl.BlockSpec((1, SEQ, 1), lambda s, h: (s, 0, 0)),
        ],
        out_specs=[
            pl.BlockSpec((SEQ, 128), lambda s, h: (s, h)),
            pl.BlockSpec((2, 2, BAND, BQ), lambda s, h: (s * hp + h, 0, 0, 0)),
        ],
        out_shape=[
            jax.ShapeDtypeStruct((rows, d), bf16),
            jax.ShapeDtypeStruct((seqs * H, 2, BAND, BQ), bf16),
        ],
        scratch_shapes=[pltpu.VMEM((2, BAND, BQ), f32)],
        compiler_params=params(2),
        cost_estimate=cost(
            seqs * H * 2 * BAND * BQ * 2 * 256, 2 * 4 * rows * d + 4 * seqs * H * BAND * BQ
        ),
        name="attend",
    )(qkv, qkv, qkv, doc[:, None, :], doc[:, :, None])


def attn_bwd_kernel(q_ref, k_ref, v_ref, do_ref, p_ref, o_ref):
    low = lax.broadcasted_iota(jnp.int32, (1, 128), 1) < HD
    scale = bf16(HD**-0.5)
    over = SEQ - BAND
    tails = []
    for b in range(2):
        q0, k0 = spans(b)
        qb = q_ref[0, q0 : q0 + BQ, :] * scale
        dob = do_ref[q0 : q0 + BQ, :]
        kb = k_ref[0, k0 : k0 + BAND, :] * scale
        vb = v_ref[0, k0 : k0 + BAND, :]
        dq = dk = dv = None
        for hh in range(2):
            mine = low if hh == 0 else jnp.logical_not(low)
            p = p_ref[hh, b]
            dom = jnp.where(mine, dob, bf16(0))
            dp = nt(vb, dom)
            pf = p.astype(f32)
            inner = jnp.sum(pf * dp, axis=0, keepdims=True)
            ds = (pf * (dp - inner)).astype(bf16)
            a = nn(p, dom)
            c = nn(ds, jnp.where(mine, qb, bf16(0)))
            g = tn(jnp.where(mine, kb, bf16(0)), ds)
            dv = a if dv is None else dv + a
            dk = c if dk is None else dk + c
            dq = g if dq is None else dq + g
        o_ref[0, q0 : q0 + BQ, :] = dq.T.astype(bf16)
        tails.append((dk, dv))
    for i, (first_part, second_part) in enumerate(zip(*tails)):
        o_ref[i + 1, :over, :] = first_part[:over].astype(bf16)
        o_ref[i + 1, over:BAND, :] = (first_part[over:] + second_part[: BAND - over]).astype(bf16)
        o_ref[i + 1, BAND:, :] = second_part[BAND - over :].astype(bf16)


def attn_bwd_call(qkv, dattn, probs):
    rows = qkv.shape[1]
    d = qkv.shape[2]
    seqs = rows // SEQ
    hp = d // 128

    def part(i):
        return pl.BlockSpec((1, SEQ, 128), lambda s, h: (i, s, h))

    return pl.pallas_call(
        attn_bwd_kernel,
        grid=(seqs, hp),
        in_specs=[
            part(0),
            part(1),
            part(2),
            pl.BlockSpec((SEQ, 128), lambda s, h: (s, h)),
            pl.BlockSpec((2, 2, BAND, BQ), lambda s, h: (s * hp + h, 0, 0, 0)),
        ],
        out_specs=pl.BlockSpec((3, SEQ, 128), lambda s, h: (0, s, h)),
        out_shape=jax.ShapeDtypeStruct((3, rows, d), bf16),
        compiler_params=params(2),
        cost_estimate=cost(
            seqs * H * 2 * BAND * BQ * 2 * 256 * 2, 2 * 7 * rows * d + 4 * seqs * H * BAND * BQ
        ),
        name="attend_back",
    )(qkv, qkv, qkv, dattn, probs)


def row_of(i):
    return pl.BlockSpec((1, 1, 768), lambda *_: (i, 0, 0))


def out_step(a_ref, w, t_ref, bo_ref, g_ref, s_ref, mid_ref, sec_ref):
    mid = t_ref[...].astype(f32) + nn(a_ref[...], w) + bo_ref[0]
    mid_ref[...] = mid
    sc, _ = moments(mid)
    sec_ref[...] = (sc * g_ref[0] + s_ref[0]).astype(bf16)


def out_kernel(a_ref, w_ref, t_ref, bo_ref, g_ref, s_ref, mid_ref, sec_ref):
    out_step(a_ref, w_ref[0], t_ref, bo_ref, g_ref, s_ref, mid_ref, sec_ref)


def out_fast_kernel(place, a_ref, t_ref, bo_ref, g_ref, s_ref, *refs):
    pieces, (mid_ref, sec_ref, w_ref, sem) = refs[:8], refs[8:]

    @pl.when(pl.program_id(0) == 0)
    def _():
        wait_all(start_all(row_copies(place, pieces, w_ref, 8, w_ref.shape[1] // 8), sem))

    out_step(a_ref, w_ref[0], t_ref, bo_ref, g_ref, s_ref, mid_ref, sec_ref)


def out_fast_call(place, attended, tokens, table, pieces):
    rows, d = tokens.shape
    blk = pl.BlockSpec((256, d), lambda i, place: (i, 0))
    return pl.pallas_call(
        out_fast_kernel,
        grid_spec=pltpu.PrefetchScalarGridSpec(
            num_scalar_prefetch=1,
            grid=(rows // 256,),
            in_specs=[blk, blk, row_of(OUT), row_of(GAIN_TWO), row_of(SHIFT_TWO)] + [ANY] * 8,
            out_specs=[blk, blk, pl.BlockSpec((1, d, d), lambda i, place: (0, 0, 0))],
            scratch_shapes=[pltpu.SemaphoreType.DMA],
        ),
        out_shape=[
            jax.ShapeDtypeStruct((rows, d), f32),
            jax.ShapeDtypeStruct((rows, d), bf16),
            jax.ShapeDtypeStruct((1, d, d), bf16),
        ],
        compiler_params=params(1),
        cost_estimate=cost(2 * rows * d * d, rows * d * 10 + 4 * d * d),
        name="project",
    )(place, attended, tokens, table, table, table, *pieces)


def out_call(attended, wo, tokens, table):
    rows, d = tokens.shape
    blk = pl.BlockSpec((256, d), lambda i: (i, 0))
    return pl.pallas_call(
        out_kernel,
        grid=(rows // 256,),
        in_specs=[
            blk, pl.BlockSpec((1, d, d), lambda i: (3, 0, 0)), blk,
            row_of(OUT), row_of(GAIN_TWO), row_of(SHIFT_TWO),
        ],
        out_specs=[blk, blk],
        out_shape=[
            jax.ShapeDtypeStruct((rows, d), f32),
            jax.ShapeDtypeStruct((rows, d), bf16),
        ],
        compiler_params=params(1),
        cost_estimate=cost(2 * rows * d * d, rows * d * 10 + 2 * d * d),
        name="project",
    )(attended, wo, tokens, table, table, table)


def ffn_step(x_ref, g_ref, wu, wd, b, acc_ref, sg_ref, act, hg, gb_ref):
    rows = x_ref.shape[0]
    chunk = 256
    total = jnp.zeros((1, wu.shape[1]), f32)
    for r in range(rows // chunk):
        at = pl.ds(r * chunk, chunk)
        h = nn(x_ref[at, :], wu[...]) + b
        ag = nt(g_ref[at, :], wd[...])
        phi = 0.5 + 0.5 * lax.erf(h * (0.5**0.5))
        a = (h * phi).astype(bf16)
        act[at, :] = a
        dens = jnp.exp(-0.5 * (h * h)) * 0.3989422804014327
        hgv = (ag * (phi + h * dens)).astype(bf16)
        hg[at, :] = hgv
        total += jnp.sum(hgv.astype(f32), axis=0, keepdims=True)
        acc_ref[at, :] += nn(a, wd[...])
        sg_ref[at, :] += nt(hgv, wu[...])
    gb_ref[0] = total


def ffn_start(start, acc_in, bd_ref, sg_in, acc_ref, sg_ref):
    if start:
        acc_ref[...] = acc_in[...] + bd_ref[0]
        sg_ref[...] = jnp.zeros_like(sg_ref)
    else:
        acc_ref[...] = acc_in[...]
        sg_ref[...] = sg_in[...]


def ffn_kernel(start, x_ref, g_ref, w_ref, b_ref, acc_in, bd_ref, *refs):
    sg_in = None if start else refs[0]
    gw_ref, gb_ref, acc_ref, sg_ref, act, hg = refs[0 if start else 1 :]

    @pl.when(pl.program_id(0) == 0)
    def _():
        ffn_start(start, acc_in, bd_ref, sg_in, acc_ref, sg_ref)

    ffn_step(x_ref, g_ref, w_ref.at[0], w_ref.at[1], b_ref[0], acc_ref, sg_ref, act, hg, gb_ref)
    gw_ref[0] = tn(x_ref[...], hg[...]).astype(bf16)
    gw_ref[1] = tn(act[...], g_ref[...]).astype(bf16)


def ffn_call(lead, second, dgrad, w, table, acc, sg):
    rows, d = second.shape
    n = w.shape[0] // 2
    start = sg is None
    full = pl.BlockSpec((rows, d), lambda j: (0, 0))
    pair = pl.BlockSpec((2, d, d), lambda j: (j, 0, 0))
    return pl.pallas_call(
        partial(ffn_kernel, start),
        grid=(n,),
        in_specs=[
            full, full, pair, pl.BlockSpec((1, 1, d), lambda j: (UP + lead * n + j, 0, 0)),
            full, row_of(DOWN),
        ]
        + ([] if start else [full]),
        out_specs=[pair, pl.BlockSpec((1, 1, d), lambda j: (j, 0, 0)), full, full],
        out_shape=[
            jax.ShapeDtypeStruct((2 * n, d, d), bf16),
            jax.ShapeDtypeStruct((n, 1, d), f32),
            jax.ShapeDtypeStruct((rows, d), f32),
            jax.ShapeDtypeStruct((rows, d), f32),
        ],
        scratch_shapes=[pltpu.VMEM((rows, d), bf16)] * 2,
        compiler_params=params(1),
        cost_estimate=cost(12 * n * rows * d * d, 20 * rows * d + 8 * n * d * d),
        name="feed",
    )(second, dgrad, w, table, acc, table, *([] if start else [sg]))


def ffn_fast_kernel(start, lead, place, x_ref, g_ref, b_ref, acc_in, bd_ref, *refs):
    sg_in = None if start else refs[0]
    refs = refs[0 if start else 1 :]
    pieces = refs[:8]
    keep, send, gb_ref, acc_ref, sg_ref, w_ref, act, hg, full, sem = refs[8:]
    j = pl.program_id(0)

    @pl.when(j == 0)
    def _():
        copies = start_all(block_copies(place, pieces, w_ref, lead), sem)
        ffn_start(start, acc_in, bd_ref, sg_in, acc_ref, sg_ref)
        wait_all(copies)

    wu, wd = w_ref.at[2 * j], w_ref.at[2 * j + 1]
    ffn_step(x_ref, g_ref, wu, wd, b_ref[0], acc_ref, sg_ref, act, hg, gb_ref)
    full[...] = tn(x_ref[...], hg[...]).astype(bf16)
    split_blocks(place, full, keep, send, 0)
    full[...] = tn(act[...], g_ref[...]).astype(bf16)
    split_blocks(place, full, keep, send, 1)


def ffn_fast_call(lead, place, second, dgrad, table, acc, sg, pieces):
    rows, d = second.shape
    start = sg is None
    m = d // 8
    full = pl.BlockSpec((rows, d), lambda j, place: (0, 0))
    half = pl.BlockSpec((2, 4, m, d), lambda j, place: (j, 0, 0, 0))
    return pl.pallas_call(
        partial(ffn_fast_kernel, start, lead),
        grid_spec=pltpu.PrefetchScalarGridSpec(
            num_scalar_prefetch=1,
            grid=(2,),
            in_specs=[
                full, full, pl.BlockSpec((1, 1, d), lambda j, place: (UP + lead * 2 + j, 0, 0)),
                full, row_of(DOWN),
            ]
            + ([] if start else [full])
            + [ANY] * 8,
            out_specs=[half, half, pl.BlockSpec((1, 1, d), lambda j, place: (j, 0, 0)), full, full],
            scratch_shapes=[pltpu.VMEM((4, d, d), bf16)]
            + [pltpu.VMEM((rows, d), bf16)] * 2
            + [pltpu.VMEM((d, d), bf16), pltpu.SemaphoreType.DMA],
        ),
        out_shape=[
            jax.ShapeDtypeStruct((4, 4, m, d), bf16),
            jax.ShapeDtypeStruct((4, 4, m, d), bf16),
            jax.ShapeDtypeStruct((2, 1, d), f32),
            jax.ShapeDtypeStruct((rows, d), f32),
            jax.ShapeDtypeStruct((rows, d), f32),
        ],
        compiler_params=params(1),
        cost_estimate=cost(24 * rows * d * d, 20 * rows * d + 16 * d * d),
        name="feed",
    )(place, second, dgrad, table, acc, table, *([] if start else [sg]), *pieces)


def norm_back(grad, sc, inv, gain):
    t = grad * gain
    return inv * (
        t - jnp.mean(t, axis=-1, keepdims=True) - sc * jnp.mean(t * sc, axis=-1, keepdims=True)
    )


def mid_kernel(
    place, sg_ref, mid_ref, dy_ref, a_ref, w_ref, g_ref, acc_ref,
    mg_ref, ag_ref, vec_ref, lo_ref, wg_ref, *rest,
):
    i = pl.program_id(0)
    wacc = rest[-1]

    @pl.when(i == 0)
    def _():
        wacc[...] = jnp.zeros_like(wacc)
        vec_ref[...] = jnp.zeros_like(vec_ref)

    lo_ref[...] = acc_ref[...].astype(bf16)
    sc, inv = moments(mid_ref[...])
    sg = sg_ref[...]
    dy = dy_ref[...].astype(f32)
    mg = dy + norm_back(sg, sc, inv, g_ref[0])
    mg_ref[...] = mg
    br = mg.astype(bf16)
    vec_ref[0:1, :] += jnp.sum(sg * sc, axis=0, keepdims=True)
    vec_ref[1:2, :] += jnp.sum(sg, axis=0, keepdims=True)
    vec_ref[2:3, :] += jnp.sum(br.astype(f32), axis=0, keepdims=True)
    vec_ref[3:4, :] += jnp.sum(dy, axis=0, keepdims=True)
    ag_ref[...] = nt(br, w_ref[0]).astype(bf16)
    wacc[...] += tn(a_ref[...], br)

    @pl.when(i == pl.num_programs(0) - 1)
    def _():
        if len(rest) == 1:
            wg_ref[0] = wacc[...].astype(bf16)
        else:
            split_blocks(place, wacc, wg_ref, rest[0], 0)


def mid_call(place, sg, mid, dy, attended, wo, table, acc, split):
    rows, d = sg.shape
    blk = pl.BlockSpec((256, d), lambda i, place: (i, 0))
    grad = (1, 4, d // 8, d) if split else (1, d, d)
    last = wo.shape[0] - 1
    return pl.pallas_call(
        mid_kernel,
        grid_spec=pltpu.PrefetchScalarGridSpec(
            num_scalar_prefetch=1,
            grid=(rows // 256,),
            in_specs=[
                blk, blk, blk, blk, pl.BlockSpec((1, d, d), lambda i, place: (last, 0, 0)),
                row_of(GAIN_TWO), blk,
            ],
            out_specs=[blk, blk, pl.BlockSpec((8, d), lambda i, place: (0, 0)), blk]
            + [pl.BlockSpec(grad, lambda i, place: (0,) * len(grad))] * (2 if split else 1),
            scratch_shapes=[pltpu.VMEM((d, d), f32)],
        ),
        out_shape=[
            jax.ShapeDtypeStruct((rows, d), f32),
            jax.ShapeDtypeStruct((rows, d), bf16),
            jax.ShapeDtypeStruct((8, d), f32),
            jax.ShapeDtypeStruct((rows, d), bf16),
        ]
        + [jax.ShapeDtypeStruct(grad, bf16)] * (2 if split else 1),
        compiler_params=params(1),
        cost_estimate=cost(4 * rows * d * d, rows * d * 22 + 4 * d * d),
        name="middle_back",
    )(place, sg, mid, dy, attended, wo, table, acc)


def wgrad_kernel(x_ref, g_ref, o_ref, b_ref):
    o_ref[0] = tn(x_ref[...], g_ref[0]).astype(bf16)
    b_ref[0] = jnp.sum(g_ref[0].astype(f32), axis=0, keepdims=True)


def wgrad_call(first, grads):
    rows, d = first.shape
    return pl.pallas_call(
        wgrad_kernel,
        grid=(3,),
        in_specs=[
            pl.BlockSpec((rows, d), lambda i: (0, 0)),
            pl.BlockSpec((1, rows, d), lambda i: (i, 0, 0)),
        ],
        out_specs=[
            pl.BlockSpec((1, d, d), lambda i: (i, 0, 0)),
            pl.BlockSpec((1, 1, d), lambda i: (i, 0, 0)),
        ],
        out_shape=[
            jax.ShapeDtypeStruct((3, d, d), bf16),
            jax.ShapeDtypeStruct((3, 1, d), f32),
        ],
        compiler_params=params(1),
        cost_estimate=cost(6 * rows * d * d, 2 * (rows * d * 4 + 3 * d * d)),
        name="weight_back",
    )(first, grads)


def wgrad_fast_kernel(place, x_ref, g_ref, keep, send, b_ref, full):
    full[...] = tn(x_ref[...], g_ref[0])
    b_ref[0] = jnp.sum(g_ref[0].astype(f32), axis=0, keepdims=True)
    split_blocks(place, full, keep, send, 0)


def wgrad_fast_call(place, first, grads):
    rows, d = first.shape
    m = d // 8
    half = pl.BlockSpec((1, 4, m, d), lambda i, place: (i, 0, 0, 0))
    return pl.pallas_call(
        wgrad_fast_kernel,
        grid_spec=pltpu.PrefetchScalarGridSpec(
            num_scalar_prefetch=1,
            grid=(3,),
            in_specs=[
                pl.BlockSpec((rows, d), lambda i, place: (0, 0)),
                pl.BlockSpec((1, rows, d), lambda i, place: (i, 0, 0)),
            ],
            out_specs=[half, half, pl.BlockSpec((1, 1, d), lambda i, place: (i, 0, 0))],
            scratch_shapes=[pltpu.VMEM((d, d), f32)],
        ),
        out_shape=[
            jax.ShapeDtypeStruct((3, 4, m, d), bf16),
            jax.ShapeDtypeStruct((3, 4, m, d), bf16),
            jax.ShapeDtypeStruct((3, 1, d), f32),
        ],
        compiler_params=params(1),
        cost_estimate=cost(6 * rows * d * d, 2 * (rows * d * 4 + 3 * d * d)),
        name="weight_back",
    )(place, first, grads)


def input_kernel(start, g_ref, w_ref, t_ref, mg_ref, gain_ref, *refs):
    o_ref, vec_ref = refs[-2:]

    @pl.when(pl.program_id(0) == 0)
    def _():
        vec_ref[...] = jnp.zeros_like(vec_ref) if start else refs[0][...]

    fg = nt(g_ref[0], w_ref[0]) + nt(g_ref[1], w_ref[1]) + nt(g_ref[2], w_ref[2])
    sc, inv = moments(t_ref[...].astype(f32))
    o_ref[...] = (mg_ref[...] + norm_back(fg, sc, inv, gain_ref[0])).astype(bf16)
    vec_ref[0:1, :] += jnp.sum(fg * sc, axis=0, keepdims=True)
    vec_ref[1:2, :] += jnp.sum(fg, axis=0, keepdims=True)


def input_call(grads, w, tokens, mg, table, skip, steps, before=()):
    rows, d = tokens.shape
    blk = pl.BlockSpec((256, d), lambda i: (skip + i, 0))
    vec = pl.BlockSpec((8, d), lambda i: (0, 0))
    start = not before
    return pl.pallas_call(
        partial(input_kernel, start),
        grid=(steps,),
        in_specs=[
            pl.BlockSpec((3, 256, d), lambda i: (0, skip + i, 0)),
            pl.BlockSpec((3, d, d), lambda i: (0, 0, 0)),
            blk,
            blk,
            row_of(GAIN_ONE),
        ]
        + ([] if start else [vec, ANY]),
        out_specs=[blk, vec],
        out_shape=[
            jax.ShapeDtypeStruct((rows, d), bf16),
            jax.ShapeDtypeStruct((8, d), f32),
        ],
        input_output_aliases={} if start else {6: 0},
        compiler_params=params(1),
        cost_estimate=cost(1536 * steps * d * d, 256 * steps * d * 14 + 6 * d * d),
        name="input_back",
    )(grads, w, tokens, mg, table, *([] if start else [before[1], before[0]]))


CORE = 1
ALONG = (2, 4, 6)
GROUP = (8, 16, 24)


def hop(x, mask):
    return lax.ppermute(x, ("dp", "fsdp"), [(i, i ^ mask) for i in range(32)])


def group_hop(x, second):
    pairs = [(i, i ^ (GROUP[0] if i % 2 == second else GROUP[1])) for i in range(32)]
    return lax.ppermute(x, ("dp", "fsdp"), pairs)


def pick(x, index, axis=0):
    return lax.dynamic_index_in_dim(x, index, axis, keepdims=False)


def after(deps, *xs):
    return lax.optimization_barrier((*xs, *deps))[: len(xs)]


def wide(x):
    return x.astype(f32)


def add_core(keep, got):
    return (wide(keep) + wide(got)).astype(bf16)


def quarter(x, index, axis):
    n = x.shape[axis] // 4
    return lax.dynamic_slice_in_dim(x, index * n, n, axis)


def add_two(a, b):
    return (wide(a) + wide(b)).astype(bf16)


def turn(x, bits):
    for axis, bit in enumerate(bits):
        x = jnp.where(bit == 0, x, jnp.flip(x, axis))
    return x


def add_all(first, others):
    total = wide(first)
    for other in others:
        total = total + wide(other)
    return total.astype(bf16)


def segment_ids(lengths):
    ends = jnp.cumsum(lengths, axis=-1)
    places = jnp.arange(SEQ, dtype=jnp.int32)
    return jnp.sum((places[None, :, None] >= ends[:, None, :]).astype(jnp.int32), axis=-1)


def pack_vectors(pre_gain, pre_shift, bias_query, bias_value, bias_out, mid_gain, mid_shift, bias_up, bias_down):
    none = jnp.zeros_like(bias_query)
    return jnp.concatenate(
        [pre_gain, pre_shift, bias_query, none, bias_value, bias_out, mid_gain, mid_shift, bias_down, bias_up]
    )[None]


def make_table(small):
    shards = small.shape[0]
    n = small.shape[1] * shards // 768
    return small.reshape(shards, n, -1).transpose(1, 0, 2).reshape(n, 1, 768).astype(f32)


def order_hidden(w_up, w_down, shards):
    m, d = w_up.shape[0], w_up.shape[0] * shards
    parts = w_down.shape[0] // m
    up = w_up.reshape(m, shards, parts, m).transpose(2, 0, 1, 3).reshape(parts, m, d)
    return jnp.stack([up, w_down.reshape(parts, m, d)], 1).reshape(2 * parts, m, d)


VEC_ROWS = (0, 1, 16, 18, 10, 8, 9)
DOWN_ROW, UP_ROW = 11, 20


def outputs(layer_out, input_grad, attn, feed, vec, factor, shards):
    m, d = attn[0].shape
    parts = len(feed) // 2
    vec = vec * factor
    up = jnp.stack(feed[0::2]).reshape(parts, m, shards, m).transpose(1, 2, 0, 3)
    return (
        layer_out,
        input_grad,
        *(wide(g) * factor for g in attn),
        wide(up.reshape(m, parts * d)) * factor,
        wide(jnp.concatenate(feed[1::2])) * factor,
        *(vec[i] for i in VEC_ROWS),
        vec[UP_ROW:].reshape(-1),
        vec[DOWN_ROW],
    )


def body_fast(tokens, cotangent, doc_lengths, w_query, w_key, w_value, w_out, w_up, w_down, *vectors):
    rows, d = tokens.shape
    n = d // 8
    dp, at = lax.axis_index("dp"), lax.axis_index("fsdp")
    z, core = at // 2, at % 2
    place = jnp.stack([dp, z, core]).astype(jnp.int32)
    one, two = 1 + core, 2 - core

    quarters = [quarter(w, dp, 0) for w in (w_query, w_key, w_value, w_out)]
    attn_mine = jnp.concatenate(quarters[:3])
    attn_z = [hop(attn_mine, m) for m in ALONG]
    small = pack_vectors(*vectors)
    width = small.shape[1]
    low = jnp.pad(small[0], (0, 8 * d - width)).reshape(8, d)
    low = jnp.concatenate([low, hop(low, CORE)])
    attn_own = jnp.stack([w_query, w_key, w_value])
    attn_own_cross = hop(attn_own, CORE)
    attn_along = jnp.stack(attn_z)
    low_across = hop(low, ALONG[1])
    low_beside = hop(jnp.stack([low, low_across]), ALONG[0])
    low, low_across, low_beside = after([attn_along], low, low_across, low_beside)
    lows = jnp.stack([low, low_beside[0], low_across, low_beside[1]])
    small = lows.reshape(2, 2, 2, 8 * d)[..., :width]
    table = make_table(turn(small, (z // 2, z % 2, core)).reshape(8, width))
    attn_near = group_hop(attn_along, 0)
    attn_along_cross = hop(attn_along, CORE)
    attn_far = group_hop(jnp.stack([attn_along, attn_near]), 1)
    attn_near_cross = hop(attn_near, CORE)
    attn_far_cross = hop(attn_far, CORE)

    tokens_late, lengths_late, w_up, w_down, last = after(
        [attn_along], tokens, doc_lengths, w_up, w_down, quarters[3]
    )
    feed_own = order_hidden(w_up, w_down, 8)
    mine_one = jnp.concatenate([pick(feed_own[:4], dp), last])
    mine_two = pick(feed_own[4:], dp)
    feed_own = jnp.concatenate([feed_own, w_out[None]])
    across_one = hop(mine_one, ALONG[1])
    mine_late, across_late = after([attn_near], mine_one, across_one)
    beside_one = hop(jnp.stack([mine_late, across_late]), ALONG[0])
    beside_one, mine_two = after([attn_far], beside_one, mine_two)
    along_one = jnp.stack([beside_one[0], across_one, beside_one[1]])
    near_one = group_hop(along_one, 0)
    across_two = hop(mine_two, ALONG[1])

    doc = segment_ids(lengths_late)
    scaled, _ = moments(wide(tokens_late))
    first = (scaled * table[GAIN_ONE] + table[SHIFT_ONE]).astype(bf16)
    qkv, attn_w = qkv_fast_call(
        place, first, table,
        [attn_own, attn_along, attn_near, attn_far]
        + [attn_own_cross, attn_along_cross, attn_near_cross, attn_far_cross],
    )
    feed_own_late, along_one, near_one, mine_two, across_two = after(
        [qkv], feed_own, along_one, near_one, mine_two, across_two
    )
    (qkv,) = after([near_one, across_two], qkv)
    far_one = group_hop(jnp.stack([along_one, near_one]), 1)
    beside_two = hop(jnp.stack([mine_two, across_two]), ALONG[0])
    feed_cross = hop(feed_own_late, CORE)
    pieces_one = [feed_cross, hop(along_one, CORE), hop(near_one, CORE)]
    attended, probs = attn_fwd_call(qkv, doc)
    far_one, beside_two, attended_late = after([attended], far_one, beside_two, attended)
    (attended_late,) = after([far_one, beside_two], attended_late)
    pieces_one = [feed_own, along_one, near_one, far_one, *pieces_one, hop(far_one, CORE)]
    along_two = jnp.stack([beside_two[0], across_two, beside_two[1]])
    near_two = group_hop(along_two, 0)
    middle, second, wo = out_fast_call(place, attended_late, tokens, table, pieces_one)
    along_two, near_two, second = after([middle], along_two, near_two, second)
    (second,) = after([near_two], second)
    far_two = group_hop(jnp.stack([along_two, near_two]), 1)
    pieces_two = [along_two, near_two, far_two]
    pieces_two = [feed_own, *pieces_two, feed_cross, *(hop(x, CORE) for x in pieces_two)]

    def first_hop(parts):
        return group_hop(jnp.stack([parts(dp ^ one), parts(dp ^ 3)]), 0)

    def fold(parts, got):
        return add_two(parts(dp), got[0]), add_two(parts(dp ^ two), got[1])

    def beside(x):
        return jnp.stack([pick(x, z ^ 1), pick(x, z ^ 3)])

    def across(x, got):
        return add_two(pick(x, z), got[0]), add_two(pick(x, z ^ 2), got[1])

    keep_one, send_one, up_bias_one, acc, sg = ffn_fast_call(
        0, place, second, cotangent, table, middle, None, pieces_one
    )
    (send_one,) = after([far_two], send_one)
    got_one = hop(send_one, CORE)
    parts_one = lambda i: add_two(pick(keep_one, i), pick(got_one, i))
    near_one = first_hop(parts_one)
    (sg,) = after([got_one], sg)
    keep_two, send_two, up_bias_two, acc, sg = ffn_fast_call(
        1, place, second, cotangent, table, acc, sg, pieces_two
    )
    got_two = hop(send_two, CORE)
    (sg,) = after([near_one], sg)
    mine_one, far_one = fold(parts_one, near_one)
    (sg,) = after([far_one], sg)
    far_one = group_hop(far_one, 1)
    mid_grad, attended_grad, mid_vec, layer_out, keep_out, send_out = mid_call(
        place, sg, middle, cotangent, attended, wo, table, acc, True
    )
    got_out = hop(send_out, CORE)
    (attended_grad,) = after([far_one, got_two, got_out], attended_grad)
    sum_one = add_two(mine_one, far_one)
    beside_one = hop(beside(sum_one), ALONG[0])

    def parts_two(i):
        out = add_two(quarter(keep_out[0], i, 1), quarter(got_out[0], i, 1))
        return jnp.concatenate([add_two(pick(keep_two, i), pick(got_two, i)), out], 1)

    near_two = first_hop(parts_two)
    grads = attn_bwd_call(qkv, attended_grad, probs)
    (beside_one,) = after([grads], beside_one)
    mine_one, across_one = across(sum_one, beside_one)
    mine_two, far_two = fold(parts_two, near_two)
    (grads,) = after([across_one, far_two], grads)
    across_one = hop(across_one, ALONG[1])
    far_two = group_hop(far_two, 1)
    keep_attn, send_attn, proj_bias = wgrad_fast_call(place, first, grads)
    (send_attn,) = after([across_one, far_two], send_attn)
    got_attn = hop(send_attn, CORE)
    sum_two = add_two(mine_two, far_two)
    beside_two = beside(sum_two)
    final_one = add_two(mine_one, across_one)
    got_attn, final_one = after([beside_two], got_attn, final_one)
    parts_attn = lambda i: add_two(quarter(keep_attn, i, 2), quarter(got_attn, i, 2)).reshape(-1, d)
    near_attn = jnp.concatenate([parts_attn(dp ^ one), parts_attn(dp ^ 3), final_one])
    (grads,) = after([beside_two, near_attn], grads)
    beside_two = hop(beside_two, ALONG[0])
    near_attn = group_hop(near_attn, 0)
    input_grad, in_vec = input_call(grads, attn_w, tokens, mid_grad, table, 0, rows // 256)
    many = near_attn.shape[0] - n
    near_attn, beside_two = after([in_vec], near_attn, beside_two)
    near_one = near_attn[many:]
    mine_attn, far_attn = fold(parts_attn, near_attn[:many].reshape(2, many // 2, d))
    mine_two, across_two = across(sum_two, beside_two)
    far_attn = jnp.concatenate([far_attn, final_one, near_one])
    in_vec, *vec = after(
        [far_attn], in_vec, mid_vec, proj_bias[:, 0], up_bias_one[:, 0], up_bias_two[:, 0]
    )
    far_attn = group_hop(far_attn, 1)
    across_two = hop(across_two, ALONG[1])

    in_vec = in_vec[:2] + hop(in_vec[:2], CORE)
    none = jnp.zeros((1, d), f32)
    (vec,) = after((), jnp.concatenate([*vec[:2], none, *vec[2:]]))
    vec = vec.reshape(16, 4, 2, n).transpose(2, 1, 0, 3)
    vec = pick(vec, core) + hop(pick(vec, 1 - core), CORE)
    vec = vec.reshape(4, 16 * n // d, d).astype(bf16)
    many = many // 2
    low = jnp.concatenate(
        [vec, jnp.broadcast_to(in_vec.astype(bf16)[None], (4, 2, d)), jnp.zeros((4, 4, d), bf16)], 1
    )
    far_attn, low = after((), far_attn, low)
    far_one = far_attn[many:].reshape(2, n, d)
    attn_sum = add_two(mine_attn, far_attn[:many])
    many = many // 4
    rest = attn_sum.reshape(3, 4, many // 3, d).transpose(1, 0, 2, 3).reshape(4, many, d)
    rest = jnp.concatenate([rest, low], 1)
    beside_rest = beside(rest)
    (across_two,) = after([beside_rest], across_two)
    beside_rest = hop(beside_rest, ALONG[0])
    final_two = add_two(mine_two, across_two)
    near_two = group_hop(final_two, 0)
    mine_rest, across_rest = across(rest, beside_rest)
    final_two, near_two = after([across_rest], final_two, near_two)
    far_two = group_hop(jnp.stack([final_two, near_two]), 1)
    final_rest = add_two(mine_rest, hop(across_rest, ALONG[1]))
    (final_rest,) = after([far_two], final_rest)
    final_rest = jnp.stack([final_rest] + [hop(final_rest, m) for m in GROUP])
    vec = jnp.sum(wide(final_rest[:, many : many + 4]), axis=0)
    in_vec = lax.dynamic_slice_in_dim(vec[2:], at * n, n, 1)
    vec = jnp.concatenate([in_vec, jnp.zeros((6, n), f32), vec[:2].reshape(16, n)])
    final_one = jnp.stack([final_one, near_one, far_one[0], far_one[1]])
    final_two = jnp.stack([final_two, near_two, far_two[0], far_two[1]])
    order = lambda b: jnp.where(b == one, 1, jnp.where(b == two, 2, b))
    final_attn = [pick(final_rest, dp ^ b)[:many].reshape(3, many // 3, d) for b in range(4)]
    final_one = [pick(final_one, order(dp ^ b)) for b in range(4)]
    final_two = [pick(final_two, order(dp ^ b)) for b in range(4)]
    attn = [jnp.concatenate([x[i] for x in final_attn]) for i in range(3)]
    attn.append(jnp.concatenate([x[n:] for x in final_two]))
    feed = final_one + [x[:n] for x in final_two]
    factor = (32 * rows) ** (-0.5)
    return outputs(layer_out, input_grad, attn, feed, vec, factor, 8)


def gather(local):
    return lax.all_gather(local, "fsdp", axis=1, tiled=True)


def reduce(grad):
    part = lax.psum_scatter(wide(grad), "fsdp", scatter_dimension=1, tiled=True)
    total = lax.psum(part.astype(bf16), "dp")
    return [total[b] for b in range(grad.shape[0])]


def body_plain(tokens, cotangent, doc_lengths, w_query, w_key, w_value, w_out, w_up, w_down, *vectors):
    rows = tokens.shape[0]
    shards, groups = lax.axis_size("fsdp"), lax.axis_size("dp")
    table = make_table(lax.all_gather(pack_vectors(*vectors), "fsdp", axis=0, tiled=True))
    attn_w = gather(jnp.stack([w_query, w_key, w_value, w_out]))
    feed_own = order_hidden(w_up, w_down, shards)
    doc = segment_ids(doc_lengths)
    scaled, _ = moments(wide(tokens))
    first = (scaled * table[GAIN_ONE] + table[SHIFT_ONE]).astype(bf16)
    qkv = qkv_call(first, attn_w, table)
    attended, probs = attn_fwd_call(qkv, doc)
    middle, second = out_call(attended, attn_w, tokens, table)
    acc, sg = middle, None
    feed = []
    up_bias = []
    for lead in range(feed_own.shape[0] // 4):
        w = gather(feed_own[4 * lead : 4 * lead + 4])
        grad, bias_grad, acc, sg = ffn_call(lead, second, cotangent, w, table, acc, sg)
        feed += reduce(grad)
        up_bias.append(bias_grad)
    mid_grad, attended_grad, mid_vec, layer_out, out_grad = mid_call(
        jnp.zeros((3,), jnp.int32), sg, middle, cotangent, attended, attn_w, table, acc, False
    )
    grads = attn_bwd_call(qkv, attended_grad, probs)
    proj_grad, proj_bias = wgrad_call(first, grads)
    input_grad, in_vec = input_call(grads, attn_w, tokens, mid_grad, table, 0, tokens.shape[0] // 256)
    attn = reduce(jnp.concatenate([proj_grad, out_grad]))
    none = jnp.zeros((1,) + proj_bias.shape[2:], f32)
    vec = jnp.concatenate([in_vec, mid_vec, proj_bias[:, 0], none] + [x[:, 0] for x in up_bias])
    vec = vec.reshape(vec.shape[0], shards, -1).transpose(1, 0, 2)
    vec = lax.psum(lax.psum_scatter(vec, "fsdp", scatter_dimension=0, tiled=True), "dp")[0]
    factor = (groups * shards * rows) ** (-0.5)
    return outputs(layer_out, input_grad, attn, feed, vec, factor, shards)


def solution(mesh):
    both = P(("dp", "fsdp"), None)
    matrix, vector = P("fsdp", None), P("fsdp")
    fast = mesh.shape["dp"] == 4 and mesh.shape["fsdp"] == 8
    return jax.shard_map(
        body_fast if fast else body_plain,
        mesh=mesh,
        in_specs=(both,) * 3 + (matrix,) * 6 + (vector,) * 9,
        out_specs=(both,) * 2 + (matrix,) * 6 + (vector,) * 9,
        check_vma=False,
    )
```

```python
from functools import partial

import jax
import jax.numpy as jnp
from jax import lax
from jax.experimental import pallas as pl
from jax.experimental.pallas import tpu as pltpu
from jax.sharding import PartitionSpec as P

H = 12
HD = 64
SEQ = 512
MOST = 160
BQ = 256
BAND = 416
GAIN_ONE, SHIFT_ONE, QUERY, KEY, VALUE, OUT, GAIN_TWO, SHIFT_TWO, DOWN, UP = range(10)
epsilon = 1e-05
bf16 = jnp.bfloat16
f32 = jnp.float32


def nn(a, b):
    return jnp.dot(a, b, preferred_element_type=f32)


def nt(a, b):
    return lax.dot_general(a, b, (((1,), (1,)), ((), ())), preferred_element_type=f32)


def tn(a, b):
    return lax.dot_general(a, b, (((0,), (0,)), ((), ())), preferred_element_type=f32)


def params(n, mb=56):
    return pltpu.CompilerParams(
        dimension_semantics=("arbitrary",) * n, vmem_limit_bytes=mb * 1024 * 1024
    )


def cost(flops, nbytes, trans=0):
    return pl.CostEstimate(
        flops=int(flops * 50), bytes_accessed=int(nbytes * 50), transcendentals=int(trans)
    )


def moments(v):
    mean = jnp.mean(v, axis=-1, keepdims=True)
    c = v - mean
    inv = lax.rsqrt(jnp.mean(c * c, axis=-1, keepdims=True) + epsilon)
    return c * inv, inv


def shares(place, sides):
    d, z, c = place[0], place[1], place[2]
    for p, (along, near, far) in enumerate(sides):
        core = c ^ p
        parts = ((d, along), (d ^ (1 + core), near), (d ^ (2 - core), far.at[0]), (d ^ 3, far.at[1]))
        for member, view in parts:
            for k in range(3):
                yield member, 2 * (z ^ (k + 1)) + core, view.at[k]


def by_sides(refs):
    return (refs[0], refs[4]), (refs[1:4], refs[5:8])


def start_all(pairs, sem):
    copies = [pltpu.make_async_copy(a, b, sem) for a, b in pairs]
    for copy in copies:
        copy.start()
    return copies


def wait_all(copies):
    for copy in copies:
        copy.wait()


def block_copies(place, refs, out, lead):
    rows = out.shape[1] // 8
    owns, sides = by_sides(refs)
    pairs = []
    for p, own in enumerate(owns):
        s = 2 * place[1] + (place[2] ^ p)
        pairs += [(own.at[4 * lead + b], out.at[b, pl.ds(s * rows, rows), :]) for b in range(4)]
    for member, s, view in shares(place, sides):
        pairs.append((view.at[pl.ds(0, rows), :], out.at[member, pl.ds(s * rows, rows), :]))
    return pairs


def row_copies(place, refs, out, source, skip):
    rows = out.shape[1] // 8
    few = rows // 4
    owns, sides = by_sides(refs)
    pairs = []
    for p, own in enumerate(owns):
        s = 2 * place[1] + (place[2] ^ p)
        for b in range(out.shape[0]):
            pairs.append((own.at[source + b], out.at[b, pl.ds(s * rows, rows), :]))
    for member, s, view in shares(place, sides):
        for b in range(out.shape[0]):
            to = pl.multiple_of(s * rows + member * few, 8)
            pairs.append((view.at[pl.ds(skip + b * few, few), :], out.at[b, pl.ds(to, few), :]))
    return pairs


def split_blocks(place, full, keep, send, b):
    rows = full.shape[0] // 8
    for k in range(4):
        keep[b, k] = full[pl.ds((2 * k + place[2]) * rows, rows), :].astype(bf16)
        send[b, k] = full[pl.ds((2 * k + 1 - place[2]) * rows, rows), :].astype(bf16)


ANY = pl.BlockSpec(memory_space=pl.ANY)


def qkv_kernel(x_ref, w_ref, b_ref, o_ref):
    b = b_ref[0]
    for r in range(x_ref.shape[0] // 256):
        rows = pl.ds(r * 256, 256)
        o_ref[0, rows, :] = (nn(x_ref[rows, :], w_ref[0]) + b).astype(bf16)


def qkv_call(first, w, table):
    rows, d = first.shape
    return pl.pallas_call(
        qkv_kernel,
        grid=(3,),
        in_specs=[
            pl.BlockSpec((rows, d), lambda i: (0, 0)),
            pl.BlockSpec((1, d, d), lambda i: (i, 0, 0)),
            pl.BlockSpec((1, 1, d), lambda i: (QUERY + i, 0, 0)),
        ],
        out_specs=pl.BlockSpec((1, rows, d), lambda i: (i, 0, 0)),
        out_shape=jax.ShapeDtypeStruct((3, rows, d), bf16),
        compiler_params=params(1),
        cost_estimate=cost(6 * rows * d * d, 2 * (rows * d * 4 + 3 * d * d)),
        name="qkv",
    )(first, w, table)


def qkv_fast_kernel(place, x_ref, b_ref, *refs):
    pieces, (o_ref, w_ref, sem) = refs[:8], refs[8:]
    i = pl.program_id(0)

    @pl.when(i == 0)
    def _():
        wait_all(start_all(row_copies(place, pieces, w_ref, 0, 0), sem))

    b = b_ref[0]
    for r in range(x_ref.shape[0] // 256):
        rows = pl.ds(r * 256, 256)
        o_ref[0, rows, :] = (nn(x_ref[rows, :], w_ref[i]) + b).astype(bf16)


def qkv_fast_call(place, first, table, pieces):
    rows, d = first.shape
    return pl.pallas_call(
        qkv_fast_kernel,
        grid_spec=pltpu.PrefetchScalarGridSpec(
            num_scalar_prefetch=1,
            grid=(3,),
            in_specs=[
                pl.BlockSpec((rows, d), lambda i, place: (0, 0)),
                pl.BlockSpec((1, 1, d), lambda i, place: (QUERY + i, 0, 0)),
            ]
            + [ANY] * 8,
            out_specs=[
                pl.BlockSpec((1, rows, d), lambda i, place: (i, 0, 0)),
                pl.BlockSpec((3, d, d), lambda i, place: (0, 0, 0)),
            ],
            scratch_shapes=[pltpu.SemaphoreType.DMA],
        ),
        out_shape=[
            jax.ShapeDtypeStruct((3, rows, d), bf16),
            jax.ShapeDtypeStruct((3, d, d), bf16),
        ],
        compiler_params=params(1),
        cost_estimate=cost(6 * rows * d * d, 2 * (rows * d * 4 + 8 * d * d)),
        name="qkv",
    )(place, first, table, *pieces)


def spans(b):
    return b * BQ, b * (SEQ - BAND)


def attn_fwd_kernel(q_ref, k_ref, v_ref, dr_ref, dc_ref, o_ref, p_ref, bias):
    @pl.when(pl.program_id(1) == 0)
    def _():
        for b in range(2):
            q0, k0 = spans(b)
            same = dc_ref[0, k0 : k0 + BAND, :] == dr_ref[0, :, q0 : q0 + BQ]
            bias[b] = jnp.where(same, 0.0, -3e38)

    low = lax.broadcasted_iota(jnp.int32, (1, 128), 1) < HD
    for b in range(2):
        q0, k0 = spans(b)
        qb = q_ref[0, q0 : q0 + BQ, :] * bf16(HD**-0.5)
        kb = k_ref[0, k0 : k0 + BAND, :]
        vb = v_ref[0, k0 : k0 + BAND, :]
        acc = None
        for hh in range(2):
            mine = low if hh == 0 else jnp.logical_not(low)
            s = nt(kb, jnp.where(mine, qb, bf16(0))) + bias[b]
            e = jnp.exp(s - jnp.max(s, axis=0, keepdims=True))
            p = (e * (1.0 / jnp.sum(e, axis=0, keepdims=True))).astype(bf16)
            p_ref[hh, b] = p
            part = tn(jnp.where(mine, vb, bf16(0)), p)
            acc = part if acc is None else acc + part
        o_ref[q0 : q0 + BQ, :] = acc.T.astype(bf16)


def attn_fwd_call(qkv, doc):
    rows = qkv.shape[1]
    d = qkv.shape[2]
    seqs = rows // SEQ
    hp = d // 128

    def part(i):
        return pl.BlockSpec((1, SEQ, 128), lambda s, h: (i, s, h))

    return pl.pallas_call(
        attn_fwd_kernel,
        grid=(seqs, hp),
        in_specs=[
            part(0),
            part(1),
            part(2),
            pl.BlockSpec((1, 1, SEQ), lambda s, h: (s, 0, 0)),
            pl.BlockSpec((1, SEQ, 1), lambda s, h: (s, 0, 0)),
        ],
        out_specs=[
            pl.BlockSpec((SEQ, 128), lambda s, h: (s, h)),
            pl.BlockSpec((2, 2, BAND, BQ), lambda s, h: (s * hp + h, 0, 0, 0)),
        ],
        out_shape=[
            jax.ShapeDtypeStruct((rows, d), bf16),
            jax.ShapeDtypeStruct((seqs * H, 2, BAND, BQ), bf16),
        ],
        scratch_shapes=[pltpu.VMEM((2, BAND, BQ), f32)],
        compiler_params=params(2),
        cost_estimate=cost(
            seqs * H * 2 * BAND * BQ * 2 * 256, 2 * 4 * rows * d + 4 * seqs * H * BAND * BQ
        ),
        name="attend",
    )(qkv, qkv, qkv, doc[:, None, :], doc[:, :, None])


def attn_bwd_kernel(q_ref, k_ref, v_ref, do_ref, p_ref, o_ref):
    low = lax.broadcasted_iota(jnp.int32, (1, 128), 1) < HD
    scale = bf16(HD**-0.5)
    over = SEQ - BAND
    tails = []
    for b in range(2):
        q0, k0 = spans(b)
        qb = q_ref[0, q0 : q0 + BQ, :] * scale
        dob = do_ref[q0 : q0 + BQ, :]
        kb = k_ref[0, k0 : k0 + BAND, :] * scale
        vb = v_ref[0, k0 : k0 + BAND, :]
        dq = dk = dv = None
        for hh in range(2):
            mine = low if hh == 0 else jnp.logical_not(low)
            p = p_ref[hh, b]
            dom = jnp.where(mine, dob, bf16(0))
            dp = nt(vb, dom)
            pf = p.astype(f32)
            inner = jnp.sum(pf * dp, axis=0, keepdims=True)
            ds = (pf * (dp - inner)).astype(bf16)
            a = nn(p, dom)
            c = nn(ds, jnp.where(mine, qb, bf16(0)))
            g = tn(jnp.where(mine, kb, bf16(0)), ds)
            dv = a if dv is None else dv + a
            dk = c if dk is None else dk + c
            dq = g if dq is None else dq + g
        o_ref[0, q0 : q0 + BQ, :] = dq.T.astype(bf16)
        tails.append((dk, dv))
    for i, (first_part, second_part) in enumerate(zip(*tails)):
        o_ref[i + 1, :over, :] = first_part[:over].astype(bf16)
        o_ref[i + 1, over:BAND, :] = (first_part[over:] + second_part[: BAND - over]).astype(bf16)
        o_ref[i + 1, BAND:, :] = second_part[BAND - over :].astype(bf16)


def attn_bwd_call(qkv, dattn, probs):
    rows = qkv.shape[1]
    d = qkv.shape[2]
    seqs = rows // SEQ
    hp = d // 128

    def part(i):
        return pl.BlockSpec((1, SEQ, 128), lambda s, h: (i, s, h))

    return pl.pallas_call(
        attn_bwd_kernel,
        grid=(seqs, hp),
        in_specs=[
            part(0),
            part(1),
            part(2),
            pl.BlockSpec((SEQ, 128), lambda s, h: (s, h)),
            pl.BlockSpec((2, 2, BAND, BQ), lambda s, h: (s * hp + h, 0, 0, 0)),
        ],
        out_specs=pl.BlockSpec((3, SEQ, 128), lambda s, h: (0, s, h)),
        out_shape=jax.ShapeDtypeStruct((3, rows, d), bf16),
        compiler_params=params(2),
        cost_estimate=cost(
            seqs * H * 2 * BAND * BQ * 2 * 256 * 2, 2 * 7 * rows * d + 4 * seqs * H * BAND * BQ
        ),
        name="attend_back",
    )(qkv, qkv, qkv, dattn, probs)


def row_of(i):
    return pl.BlockSpec((1, 1, 768), lambda *_: (i, 0, 0))


def out_step(a_ref, w, t_ref, bo_ref, g_ref, s_ref, mid_ref, sec_ref):
    mid = t_ref[...].astype(f32) + nn(a_ref[...], w) + bo_ref[0]
    mid_ref[...] = mid
    sc, _ = moments(mid)
    sec_ref[...] = (sc * g_ref[0] + s_ref[0]).astype(bf16)


def out_kernel(a_ref, w_ref, t_ref, bo_ref, g_ref, s_ref, mid_ref, sec_ref):
    out_step(a_ref, w_ref[0], t_ref, bo_ref, g_ref, s_ref, mid_ref, sec_ref)


def out_fast_kernel(place, a_ref, t_ref, bo_ref, g_ref, s_ref, *refs):
    pieces, (mid_ref, sec_ref, w_ref, sem) = refs[:8], refs[8:]

    @pl.when(pl.program_id(0) == 0)
    def _():
        wait_all(start_all(row_copies(place, pieces, w_ref, 8, w_ref.shape[1] // 8), sem))

    out_step(a_ref, w_ref[0], t_ref, bo_ref, g_ref, s_ref, mid_ref, sec_ref)


def out_fast_call(place, attended, tokens, table, pieces):
    rows, d = tokens.shape
    blk = pl.BlockSpec((256, d), lambda i, place: (i, 0))
    return pl.pallas_call(
        out_fast_kernel,
        grid_spec=pltpu.PrefetchScalarGridSpec(
            num_scalar_prefetch=1,
            grid=(rows // 256,),
            in_specs=[blk, blk, row_of(OUT), row_of(GAIN_TWO), row_of(SHIFT_TWO)] + [ANY] * 8,
            out_specs=[blk, blk, pl.BlockSpec((1, d, d), lambda i, place: (0, 0, 0))],
            scratch_shapes=[pltpu.SemaphoreType.DMA],
        ),
        out_shape=[
            jax.ShapeDtypeStruct((rows, d), f32),
            jax.ShapeDtypeStruct((rows, d), bf16),
            jax.ShapeDtypeStruct((1, d, d), bf16),
        ],
        compiler_params=params(1),
        cost_estimate=cost(2 * rows * d * d, rows * d * 10 + 4 * d * d),
        name="project",
    )(place, attended, tokens, table, table, table, *pieces)


def out_call(attended, wo, tokens, table):
    rows, d = tokens.shape
    blk = pl.BlockSpec((256, d), lambda i: (i, 0))
    return pl.pallas_call(
        out_kernel,
        grid=(rows // 256,),
        in_specs=[
            blk, pl.BlockSpec((1, d, d), lambda i: (3, 0, 0)), blk,
            row_of(OUT), row_of(GAIN_TWO), row_of(SHIFT_TWO),
        ],
        out_specs=[blk, blk],
        out_shape=[
            jax.ShapeDtypeStruct((rows, d), f32),
            jax.ShapeDtypeStruct((rows, d), bf16),
        ],
        compiler_params=params(1),
        cost_estimate=cost(2 * rows * d * d, rows * d * 10 + 2 * d * d),
        name="project",
    )(attended, wo, tokens, table, table, table)


def ffn_step(x_ref, g_ref, wu, wd, b, acc_ref, sg_ref, act, hg):
    rows = x_ref.shape[0]
    chunk = 256
    total = jnp.zeros((1, wu.shape[1]), f32)
    for r in range(rows // chunk):
        at = pl.ds(r * chunk, chunk)
        h = nn(x_ref[at, :], wu[...]) + b
        ag = nt(g_ref[at, :], wd[...])
        phi = 0.5 + 0.5 * lax.erf(h * (0.5**0.5))
        a = (h * phi).astype(bf16)
        act[at, :] = a
        dens = jnp.exp(-0.5 * (h * h)) * 0.3989422804014327
        hgv = (ag * (phi + h * dens)).astype(bf16)
        hg[at, :] = hgv
        total += jnp.sum(hgv.astype(f32), axis=0, keepdims=True)
        acc_ref[at, :] += nn(a, wd[...])
        sg_ref[at, :] += nt(hgv, wu[...])
    return total


def ffn_start(start, acc_in, bd_ref, sg_in, acc_ref, sg_ref):
    if start:
        acc_ref[...] = acc_in[...] + bd_ref[0]
        sg_ref[...] = jnp.zeros_like(sg_ref)
    else:
        acc_ref[...] = acc_in[...]
        sg_ref[...] = sg_in[...]


def ffn_kernel(start, x_ref, g_ref, w_ref, b_ref, acc_in, bd_ref, *refs):
    sg_in = None if start else refs[0]
    gw_ref, gb_ref, acc_ref, sg_ref, act, hg = refs[0 if start else 1 :]

    @pl.when(pl.program_id(0) == 0)
    def _():
        ffn_start(start, acc_in, bd_ref, sg_in, acc_ref, sg_ref)

    gb_ref[0] = ffn_step(x_ref, g_ref, w_ref.at[0], w_ref.at[1], b_ref[0], acc_ref, sg_ref, act, hg)
    gw_ref[0] = tn(x_ref[...], hg[...]).astype(bf16)
    gw_ref[1] = tn(act[...], g_ref[...]).astype(bf16)


def ffn_call(lead, second, dgrad, w, table, acc, sg):
    rows, d = second.shape
    n = w.shape[0] // 2
    start = sg is None
    full = pl.BlockSpec((rows, d), lambda j: (0, 0))
    pair = pl.BlockSpec((2, d, d), lambda j: (j, 0, 0))
    return pl.pallas_call(
        partial(ffn_kernel, start),
        grid=(n,),
        in_specs=[
            full, full, pair, pl.BlockSpec((1, 1, d), lambda j: (UP + lead * n + j, 0, 0)),
            full, row_of(DOWN),
        ]
        + ([] if start else [full]),
        out_specs=[pair, pl.BlockSpec((1, 1, d), lambda j: (j, 0, 0)), full, full],
        out_shape=[
            jax.ShapeDtypeStruct((2 * n, d, d), bf16),
            jax.ShapeDtypeStruct((n, 1, d), f32),
            jax.ShapeDtypeStruct((rows, d), f32),
            jax.ShapeDtypeStruct((rows, d), f32),
        ],
        scratch_shapes=[pltpu.VMEM((rows, d), bf16)] * 2,
        compiler_params=params(1),
        cost_estimate=cost(12 * n * rows * d * d, 20 * rows * d + 8 * n * d * d),
        name="feed",
    )(second, dgrad, w, table, acc, table, *([] if start else [sg]))


def ffn_fast_kernel(start, lead, place, x_ref, g_ref, b_ref, acc_in, bd_ref, *refs):
    sg_in, vec_in = (None, None) if start else refs[:2]
    refs = refs[0 if start else 2 :]
    pieces = refs[:8]
    keep, send, vec_ref, acc_ref, sg_ref, w_ref, act, hg, full, sem = refs[8:]
    j = pl.program_id(0)

    @pl.when(j == 0)
    def _():
        copies = start_all(block_copies(place, pieces, w_ref, lead), sem)
        ffn_start(start, acc_in, bd_ref, sg_in, acc_ref, sg_ref)
        vec_ref[...] = jnp.zeros_like(vec_ref) if start else vec_in[...]
        wait_all(copies)

    wu, wd = w_ref.at[2 * j], w_ref.at[2 * j + 1]
    total = ffn_step(x_ref, g_ref, wu, wd, b_ref[0], acc_ref, sg_ref, act, hg)
    vec_ref[pl.ds(2 * lead + j, 1), :] = total
    full[...] = tn(x_ref[...], hg[...]).astype(bf16)
    split_blocks(place, full, keep, send, 0)
    full[...] = tn(act[...], g_ref[...]).astype(bf16)
    split_blocks(place, full, keep, send, 1)


def ffn_fast_call(lead, place, second, dgrad, table, acc, sg, vec, pieces):
    rows, d = second.shape
    start = sg is None
    m = d // 8
    full = pl.BlockSpec((rows, d), lambda j, place: (0, 0))
    half = pl.BlockSpec((2, 4, m, d), lambda j, place: (j, 0, 0, 0))
    rows_of_table = pl.BlockSpec((8, d), lambda j, place: (0, 0))
    return pl.pallas_call(
        partial(ffn_fast_kernel, start, lead),
        grid_spec=pltpu.PrefetchScalarGridSpec(
            num_scalar_prefetch=1,
            grid=(2,),
            in_specs=[
                full, full, pl.BlockSpec((1, 1, d), lambda j, place: (UP + lead * 2 + j, 0, 0)),
                full, row_of(DOWN),
            ]
            + ([] if start else [full, rows_of_table])
            + [ANY] * 8,
            out_specs=[half, half, rows_of_table, full, full],
            scratch_shapes=[pltpu.VMEM((4, d, d), bf16)]
            + [pltpu.VMEM((rows, d), bf16)] * 2
            + [pltpu.VMEM((d, d), bf16), pltpu.SemaphoreType.DMA],
        ),
        out_shape=[
            jax.ShapeDtypeStruct((4, 4, m, d), bf16),
            jax.ShapeDtypeStruct((4, 4, m, d), bf16),
            jax.ShapeDtypeStruct((8, d), f32),
            jax.ShapeDtypeStruct((rows, d), f32),
            jax.ShapeDtypeStruct((rows, d), f32),
        ],
        compiler_params=params(1),
        cost_estimate=cost(24 * rows * d * d, 20 * rows * d + 16 * d * d),
        name="feed",
    )(place, second, dgrad, table, acc, table, *([] if start else [sg, vec]), *pieces)


def norm_back(grad, sc, inv, gain):
    t = grad * gain
    return inv * (
        t - jnp.mean(t, axis=-1, keepdims=True) - sc * jnp.mean(t * sc, axis=-1, keepdims=True)
    )


def mid_kernel(
    place, sg_ref, mid_ref, dy_ref, a_ref, w_ref, g_ref, acc_ref, vec_in,
    mg_ref, ag_ref, vec_ref, lo_ref, wg_ref, *rest,
):
    i = pl.program_id(0)
    wacc = rest[-1]

    @pl.when(i == 0)
    def _():
        wacc[...] = jnp.zeros_like(wacc)
        vec_ref[...] = vec_in[...]

    lo_ref[...] = acc_ref[...].astype(bf16)
    sc, inv = moments(mid_ref[...])
    sg = sg_ref[...]
    dy = dy_ref[...].astype(f32)
    mg = dy + norm_back(sg, sc, inv, g_ref[0])
    mg_ref[...] = mg
    br = mg.astype(bf16)
    vec_ref[4:5, :] += jnp.sum(sg * sc, axis=0, keepdims=True)
    vec_ref[5:6, :] += jnp.sum(sg, axis=0, keepdims=True)
    vec_ref[6:7, :] += jnp.sum(br.astype(f32), axis=0, keepdims=True)
    vec_ref[7:8, :] += jnp.sum(dy, axis=0, keepdims=True)
    ag_ref[...] = nt(br, w_ref[0]).astype(bf16)
    wacc[...] += tn(a_ref[...], br)

    @pl.when(i == pl.num_programs(0) - 1)
    def _():
        if len(rest) == 1:
            wg_ref[0] = wacc[...].astype(bf16)
        else:
            split_blocks(place, wacc, wg_ref, rest[0], 0)


def mid_call(place, sg, mid, dy, attended, wo, table, acc, vec, split):
    rows, d = sg.shape
    blk = pl.BlockSpec((256, d), lambda i, place: (i, 0))
    grad = (1, 4, d // 8, d) if split else (1, d, d)
    last = wo.shape[0] - 1
    return pl.pallas_call(
        mid_kernel,
        grid_spec=pltpu.PrefetchScalarGridSpec(
            num_scalar_prefetch=1,
            grid=(rows // 256,),
            in_specs=[
                blk, blk, blk, blk, pl.BlockSpec((1, d, d), lambda i, place: (last, 0, 0)),
                row_of(GAIN_TWO), blk, pl.BlockSpec((8, d), lambda i, place: (0, 0)),
            ],
            out_specs=[blk, blk, pl.BlockSpec((8, d), lambda i, place: (0, 0)), blk]
            + [pl.BlockSpec(grad, lambda i, place: (0,) * len(grad))] * (2 if split else 1),
            scratch_shapes=[pltpu.VMEM((d, d), f32)],
        ),
        out_shape=[
            jax.ShapeDtypeStruct((rows, d), f32),
            jax.ShapeDtypeStruct((rows, d), bf16),
            jax.ShapeDtypeStruct((8, d), f32),
            jax.ShapeDtypeStruct((rows, d), bf16),
        ]
        + [jax.ShapeDtypeStruct(grad, bf16)] * (2 if split else 1),
        compiler_params=params(1),
        cost_estimate=cost(4 * rows * d * d, rows * d * 22 + 4 * d * d),
        name="middle_back",
    )(place, sg, mid, dy, attended, wo, table, acc, vec)


def wgrad_kernel(x_ref, g_ref, o_ref, b_ref):
    o_ref[0] = tn(x_ref[...], g_ref[0]).astype(bf16)
    b_ref[0] = jnp.sum(g_ref[0].astype(f32), axis=0, keepdims=True)


def wgrad_call(first, grads):
    rows, d = first.shape
    return pl.pallas_call(
        wgrad_kernel,
        grid=(3,),
        in_specs=[
            pl.BlockSpec((rows, d), lambda i: (0, 0)),
            pl.BlockSpec((1, rows, d), lambda i: (i, 0, 0)),
        ],
        out_specs=[
            pl.BlockSpec((1, d, d), lambda i: (i, 0, 0)),
            pl.BlockSpec((1, 1, d), lambda i: (i, 0, 0)),
        ],
        out_shape=[
            jax.ShapeDtypeStruct((3, d, d), bf16),
            jax.ShapeDtypeStruct((3, 1, d), f32),
        ],
        compiler_params=params(1),
        cost_estimate=cost(6 * rows * d * d, 2 * (rows * d * 4 + 3 * d * d)),
        name="weight_back",
    )(first, grads)


def wgrad_fast_kernel(place, x_ref, g_ref, vec_in, keep, send, vec_ref, full):
    i = pl.program_id(0)

    @pl.when(i == 0)
    def _():
        vec_ref[:8, :] = vec_in[...]
        vec_ref[8:, :] = jnp.zeros_like(vec_in)

    full[...] = tn(x_ref[...], g_ref[0])
    vec_ref[pl.ds(8 + i, 1), :] = jnp.sum(g_ref[0].astype(f32), axis=0, keepdims=True)
    split_blocks(place, full, keep, send, 0)


def wgrad_fast_call(place, first, grads, vec):
    rows, d = first.shape
    m = d // 8
    half = pl.BlockSpec((1, 4, m, d), lambda i, place: (i, 0, 0, 0))
    return pl.pallas_call(
        wgrad_fast_kernel,
        grid_spec=pltpu.PrefetchScalarGridSpec(
            num_scalar_prefetch=1,
            grid=(3,),
            in_specs=[
                pl.BlockSpec((rows, d), lambda i, place: (0, 0)),
                pl.BlockSpec((1, rows, d), lambda i, place: (i, 0, 0)),
                pl.BlockSpec((8, d), lambda i, place: (0, 0)),
            ],
            out_specs=[half, half, pl.BlockSpec((16, d), lambda i, place: (0, 0))],
            scratch_shapes=[pltpu.VMEM((d, d), f32)],
        ),
        out_shape=[
            jax.ShapeDtypeStruct((3, 4, m, d), bf16),
            jax.ShapeDtypeStruct((3, 4, m, d), bf16),
            jax.ShapeDtypeStruct((16, d), f32),
        ],
        compiler_params=params(1),
        cost_estimate=cost(6 * rows * d * d, 2 * (rows * d * 4 + 3 * d * d)),
        name="weight_back",
    )(place, first, grads, vec)


def input_kernel(start, g_ref, w_ref, t_ref, mg_ref, gain_ref, *refs):
    o_ref, vec_ref = refs[-2:]

    @pl.when(pl.program_id(0) == 0)
    def _():
        vec_ref[...] = jnp.zeros_like(vec_ref) if start else refs[0][...]

    fg = nt(g_ref[0], w_ref[0]) + nt(g_ref[1], w_ref[1]) + nt(g_ref[2], w_ref[2])
    sc, inv = moments(t_ref[...].astype(f32))
    o_ref[...] = (mg_ref[...] + norm_back(fg, sc, inv, gain_ref[0])).astype(bf16)
    vec_ref[0:1, :] += jnp.sum(fg * sc, axis=0, keepdims=True)
    vec_ref[1:2, :] += jnp.sum(fg, axis=0, keepdims=True)


def input_call(grads, w, tokens, mg, table, skip, steps, before=()):
    rows, d = tokens.shape
    blk = pl.BlockSpec((256, d), lambda i: (skip + i, 0))
    vec = pl.BlockSpec((8, d), lambda i: (0, 0))
    start = not before
    return pl.pallas_call(
        partial(input_kernel, start),
        grid=(steps,),
        in_specs=[
            pl.BlockSpec((3, 256, d), lambda i: (0, skip + i, 0)),
            pl.BlockSpec((3, d, d), lambda i: (0, 0, 0)),
            blk,
            blk,
            row_of(GAIN_ONE),
        ]
        + ([] if start else [vec, ANY]),
        out_specs=[blk, vec],
        out_shape=[
            jax.ShapeDtypeStruct((rows, d), bf16),
            jax.ShapeDtypeStruct((8, d), f32),
        ],
        input_output_aliases={} if start else {6: 0},
        compiler_params=params(1),
        cost_estimate=cost(1536 * steps * d * d, 256 * steps * d * 14 + 6 * d * d),
        name="input_back",
    )(grads, w, tokens, mg, table, *([] if start else [before[1], before[0]]))


CORE = 1
ALONG = (2, 4, 6)
GROUP = (8, 16, 24)


def hop(x, mask):
    return lax.ppermute(x, ("dp", "fsdp"), [(i, i ^ mask) for i in range(32)])


def group_hop(x, second):
    pairs = [(i, i ^ (GROUP[0] if i % 2 == second else GROUP[1])) for i in range(32)]
    return lax.ppermute(x, ("dp", "fsdp"), pairs)


def pick(x, index, axis=0):
    return lax.dynamic_index_in_dim(x, index, axis, keepdims=False)


def after(deps, *xs):
    return lax.optimization_barrier((*xs, *deps))[: len(xs)]


def wide(x):
    return x.astype(f32)


def add_core(keep, got):
    return (wide(keep) + wide(got)).astype(bf16)


def quarter(x, index, axis):
    n = x.shape[axis] // 4
    return lax.dynamic_slice_in_dim(x, index * n, n, axis)


def add_two(a, b):
    return (wide(a) + wide(b)).astype(bf16)


def turn(x, bits):
    for axis, bit in enumerate(bits):
        x = jnp.where(bit == 0, x, jnp.flip(x, axis))
    return x


def add_all(first, others):
    total = wide(first)
    for other in others:
        total = total + wide(other)
    return total.astype(bf16)


def segment_ids(lengths):
    ends = jnp.cumsum(lengths, axis=-1)
    places = jnp.arange(SEQ, dtype=jnp.int32)
    return jnp.sum((places[None, :, None] >= ends[:, None, :]).astype(jnp.int32), axis=-1)


def pack_vectors(pre_gain, pre_shift, bias_query, bias_value, bias_out, mid_gain, mid_shift, bias_up, bias_down):
    none = jnp.zeros_like(bias_query)
    return jnp.concatenate(
        [pre_gain, pre_shift, bias_query, none, bias_value, bias_out, mid_gain, mid_shift, bias_down, bias_up]
    )[None]


def make_table(small):
    shards = small.shape[0]
    n = small.shape[1] * shards // 768
    return small.reshape(shards, n, -1).transpose(1, 0, 2).reshape(n, 1, 768).astype(f32)


def order_hidden(w_up, w_down, shards):
    m, d = w_up.shape[0], w_up.shape[0] * shards
    parts = w_down.shape[0] // m
    up = w_up.reshape(m, shards, parts, m).transpose(2, 0, 1, 3).reshape(parts, m, d)
    return jnp.stack([up, w_down.reshape(parts, m, d)], 1).reshape(2 * parts, m, d)


VEC_ROWS = (0, 1, 16, 18, 10, 8, 9)
DOWN_ROW, UP_ROW = 11, 20


def outputs(layer_out, input_grad, attn, feed, vec, factor, shards):
    m, d = attn[0].shape
    parts = len(feed) // 2
    vec = vec * factor
    up = jnp.stack(feed[0::2]).reshape(parts, m, shards, m).transpose(1, 2, 0, 3)
    return (
        layer_out,
        input_grad,
        *(wide(g) * factor for g in attn),
        wide(up.reshape(m, parts * d)) * factor,
        wide(jnp.concatenate(feed[1::2])) * factor,
        *(vec[i] for i in VEC_ROWS),
        vec[UP_ROW:].reshape(-1),
        vec[DOWN_ROW],
    )


def body_fast(tokens, cotangent, doc_lengths, w_query, w_key, w_value, w_out, w_up, w_down, *vectors):
    rows, d = tokens.shape
    n = d // 8
    dp, at = lax.axis_index("dp"), lax.axis_index("fsdp")
    z, core = at // 2, at % 2
    place = jnp.stack([dp, z, core]).astype(jnp.int32)
    one, two = 1 + core, 2 - core

    quarters = [quarter(w, dp, 0) for w in (w_query, w_key, w_value, w_out)]
    attn_mine = jnp.concatenate(quarters[:3])
    attn_z = [hop(attn_mine, m) for m in ALONG]
    attn_along = jnp.stack(attn_z)
    attn_near = group_hop(attn_along, 0)
    attn_own = jnp.stack([w_query, w_key, w_value])
    attn_own_cross = hop(attn_own, CORE)
    small = pack_vectors(*after([attn_along], *vectors))
    width = small.shape[1]
    low = jnp.pad(small[0], (0, 8 * d - width)).reshape(8, d)
    low = jnp.concatenate([low, hop(low, CORE)])
    attn_far = jnp.stack([attn_along, attn_near])
    (low,) = after([attn_far], low)
    low_across = hop(low, ALONG[1])
    low_beside = hop(jnp.stack([low, low_across]), ALONG[0])
    lows = jnp.stack([low, low_beside[0], low_across, low_beside[1]])
    small = lows.reshape(2, 2, 2, 8 * d)[..., :width]
    table = make_table(turn(small, (z // 2, z % 2, core)).reshape(8, width))
    attn_along_cross = hop(attn_along, CORE)
    attn_far = group_hop(attn_far, 1)
    attn_near_cross = hop(attn_near, CORE)
    attn_far_cross = hop(attn_far, CORE)

    feed_own = order_hidden(w_up, w_down, 8)
    mine_one = jnp.concatenate([pick(feed_own[:4], dp), quarters[3]])
    tokens_late, lengths_late, mine_one = after([attn_along], tokens, doc_lengths, mine_one)
    mine_two = pick(feed_own[4:], dp)
    feed_own = jnp.concatenate([feed_own, w_out[None]])
    across_one = hop(mine_one, ALONG[1])
    mine_late, across_late = after([attn_near], mine_one, across_one)
    beside_one = hop(jnp.stack([mine_late, across_late]), ALONG[0])
    beside_one, mine_two = after([attn_far], beside_one, mine_two)
    along_one = jnp.stack([beside_one[0], across_one, beside_one[1]])
    near_one = group_hop(along_one, 0)
    across_two = hop(mine_two, ALONG[1])

    doc = segment_ids(lengths_late)
    scaled, _ = moments(wide(tokens_late))
    first = (scaled * table[GAIN_ONE] + table[SHIFT_ONE]).astype(bf16)
    qkv, attn_w = qkv_fast_call(
        place, first, table,
        [attn_own, attn_along, attn_near, attn_far]
        + [attn_own_cross, attn_along_cross, attn_near_cross, attn_far_cross],
    )
    feed_own_late, along_one, near_one, mine_two, across_two = after(
        [qkv], feed_own, along_one, near_one, mine_two, across_two
    )
    (qkv,) = after([near_one, across_two], qkv)
    far_one = group_hop(jnp.stack([along_one, near_one]), 1)
    beside_two = hop(jnp.stack([mine_two, across_two]), ALONG[0])
    feed_cross = hop(feed_own_late, CORE)
    pieces_one = [feed_cross, hop(along_one, CORE), hop(near_one, CORE)]
    attended, probs = attn_fwd_call(qkv, doc)
    far_one, beside_two, attended_late = after([attended], far_one, beside_two, attended)
    (attended_late,) = after([far_one, beside_two], attended_late)
    pieces_one = [feed_own, along_one, near_one, far_one, *pieces_one, hop(far_one, CORE)]
    along_two = jnp.stack([beside_two[0], across_two, beside_two[1]])
    near_two = group_hop(along_two, 0)
    middle, second, wo = out_fast_call(place, attended_late, tokens, table, pieces_one)
    along_two, near_two, second = after([middle], along_two, near_two, second)
    (second,) = after([near_two], second)
    far_two = group_hop(jnp.stack([along_two, near_two]), 1)
    pieces_two = [along_two, near_two, far_two]
    pieces_two = [feed_own, *pieces_two, feed_cross, *(hop(x, CORE) for x in pieces_two)]

    def first_hop(parts):
        return group_hop(jnp.stack([parts(dp ^ one), parts(dp ^ 3)]), 0)

    def fold(parts, got):
        return add_two(parts(dp), got[0]), add_two(parts(dp ^ two), got[1])

    def beside(x):
        return jnp.stack([pick(x, z ^ 1), pick(x, z ^ 3)])

    def across(x, got):
        return add_two(pick(x, z), got[0]), add_two(pick(x, z ^ 2), got[1])

    keep_one, send_one, vec, acc, sg = ffn_fast_call(
        0, place, second, cotangent, table, middle, None, None, pieces_one
    )
    (send_one,) = after([far_two], send_one)
    got_one = hop(send_one, CORE)
    parts_one = lambda i: add_two(pick(keep_one, i), pick(got_one, i))
    near_one = first_hop(parts_one)
    (sg,) = after([got_one], sg)
    keep_two, send_two, vec, acc, sg = ffn_fast_call(
        1, place, second, cotangent, table, acc, sg, vec, pieces_two
    )
    got_two = hop(send_two, CORE)
    (sg,) = after([near_one], sg)
    mine_one, far_one = fold(parts_one, near_one)
    (sg,) = after([far_one], sg)
    far_one = group_hop(far_one, 1)
    mid_grad, attended_grad, vec, layer_out, keep_out, send_out = mid_call(
        place, sg, middle, cotangent, attended, wo, table, acc, vec, True
    )
    got_out = hop(send_out, CORE)
    (attended_grad,) = after([far_one, got_two, got_out], attended_grad)
    sum_one = add_two(mine_one, far_one)
    beside_one = hop(beside(sum_one), ALONG[0])

    def parts_two(i):
        out = add_two(quarter(keep_out[0], i, 1), quarter(got_out[0], i, 1))
        return jnp.concatenate([add_two(pick(keep_two, i), pick(got_two, i)), out], 1)

    near_two = first_hop(parts_two)
    grads = attn_bwd_call(qkv, attended_grad, probs)
    (beside_one,) = after([grads], beside_one)
    mine_one, across_one = across(sum_one, beside_one)
    mine_two, far_two = fold(parts_two, near_two)
    (grads,) = after([across_one, far_two], grads)
    across_one = hop(across_one, ALONG[1])
    far_two = group_hop(far_two, 1)
    keep_attn, send_attn, vec = wgrad_fast_call(place, first, grads, vec)
    (send_attn,) = after([across_one, far_two], send_attn)
    got_attn = hop(send_attn, CORE)
    sum_two = add_two(mine_two, far_two)
    beside_two = beside(sum_two)
    (got_attn,) = after([beside_two], got_attn)
    parts_attn = lambda i: add_two(quarter(keep_attn, i, 2), quarter(got_attn, i, 2))
    near_attn = jnp.stack([parts_attn(dp ^ one), parts_attn(dp ^ 3)])
    (grads,) = after([beside_two, near_attn], grads)
    beside_two = hop(beside_two, ALONG[0])
    near_attn = group_hop(near_attn, 0)
    input_grad, in_vec = input_call(grads, attn_w, tokens, mid_grad, table, 0, rows // 256)
    near_attn, beside_two = after([in_vec], near_attn, beside_two)
    mine_attn, far_attn = fold(parts_attn, near_attn)
    mine_two, across_two = across(sum_two, beside_two)
    mine_one, across_one, in_vec, vec = after([far_attn], mine_one, across_one, in_vec, vec)
    far_attn = group_hop(far_attn, 1)
    across_two = hop(across_two, ALONG[1])

    in_vec = in_vec[:2] + hop(in_vec[:2], CORE)
    vec = vec.reshape(16, 4, 2, n).transpose(2, 1, 0, 3)
    vec = pick(vec, core) + hop(pick(vec, 1 - core), CORE)
    vec = vec.reshape(4, 16 * n // d, d).astype(bf16)
    low = jnp.concatenate(
        [vec, jnp.broadcast_to(in_vec.astype(bf16)[None], (4, 2, d)), jnp.zeros((4, 4, d), bf16)], 1
    )
    final_feed = jnp.concatenate([add_two(mine_one, across_one), add_two(mine_two, across_two)])
    feed_near = group_hop(final_feed, 0)
    far_attn, low = after((), far_attn, low)
    attn_sum = add_two(mine_attn, far_attn)
    many = 3 * attn_sum.shape[2]
    rest = attn_sum.transpose(1, 0, 2, 3).reshape(4, many, d)
    rest = jnp.concatenate([rest, low], 1)
    beside_rest = beside(rest)
    final_feed, feed_near = after([beside_rest], final_feed, feed_near)
    beside_rest = hop(beside_rest, ALONG[0])
    feed_far = group_hop(jnp.stack([final_feed, feed_near]), 1)
    mine_rest, across_rest = across(rest, beside_rest)
    final_rest = add_two(mine_rest, hop(across_rest, ALONG[1]))
    (final_rest,) = after([feed_far], final_rest)
    final_rest = jnp.stack([final_rest] + [hop(final_rest, m) for m in GROUP])
    vec = jnp.sum(wide(final_rest[:, many : many + 4]), axis=0)
    in_vec = lax.dynamic_slice_in_dim(vec[2:], at * n, n, 1)
    vec = vec[:2].reshape(16, n)
    none = jnp.zeros((6, n), f32)
    vec = jnp.concatenate([in_vec, none, vec[4:8], none[:4], vec[8:12], vec[:4]])
    final_feed = jnp.stack([final_feed, feed_near, feed_far[0], feed_far[1]])
    order = lambda b: jnp.where(b == one, 1, jnp.where(b == two, 2, b))
    final_attn = [pick(final_rest, dp ^ b)[:many].reshape(3, many // 3, d) for b in range(4)]
    final_feed = [pick(final_feed, order(dp ^ b)) for b in range(4)]
    attn = [jnp.concatenate([x[i] for x in final_attn]) for i in range(3)]
    attn.append(jnp.concatenate([x[2 * n :] for x in final_feed]))
    feed = [x[:n] for x in final_feed] + [x[n : 2 * n] for x in final_feed]
    factor = (32 * rows) ** (-0.5)
    return outputs(layer_out, input_grad, attn, feed, vec, factor, 8)


def gather(local):
    return lax.all_gather(local, "fsdp", axis=1, tiled=True)


def reduce(grad):
    part = lax.psum_scatter(wide(grad), "fsdp", scatter_dimension=1, tiled=True)
    total = lax.psum(part.astype(bf16), "dp")
    return [total[b] for b in range(grad.shape[0])]


def body_plain(tokens, cotangent, doc_lengths, w_query, w_key, w_value, w_out, w_up, w_down, *vectors):
    rows = tokens.shape[0]
    shards, groups = lax.axis_size("fsdp"), lax.axis_size("dp")
    table = make_table(lax.all_gather(pack_vectors(*vectors), "fsdp", axis=0, tiled=True))
    attn_w = gather(jnp.stack([w_query, w_key, w_value, w_out]))
    feed_own = order_hidden(w_up, w_down, shards)
    doc = segment_ids(doc_lengths)
    scaled, _ = moments(wide(tokens))
    first = (scaled * table[GAIN_ONE] + table[SHIFT_ONE]).astype(bf16)
    qkv = qkv_call(first, attn_w, table)
    attended, probs = attn_fwd_call(qkv, doc)
    middle, second = out_call(attended, attn_w, tokens, table)
    acc, sg = middle, None
    feed = []
    up_bias = []
    for lead in range(feed_own.shape[0] // 4):
        w = gather(feed_own[4 * lead : 4 * lead + 4])
        grad, bias_grad, acc, sg = ffn_call(lead, second, cotangent, w, table, acc, sg)
        feed += reduce(grad)
        up_bias.append(bias_grad)
    mid_grad, attended_grad, mid_vec, layer_out, out_grad = mid_call(
        jnp.zeros((3,), jnp.int32), sg, middle, cotangent, attended, attn_w, table, acc,
        jnp.zeros((8, tokens.shape[1]), f32), False,
    )
    grads = attn_bwd_call(qkv, attended_grad, probs)
    proj_grad, proj_bias = wgrad_call(first, grads)
    input_grad, in_vec = input_call(grads, attn_w, tokens, mid_grad, table, 0, tokens.shape[0] // 256)
    attn = reduce(jnp.concatenate([proj_grad, out_grad]))
    none = jnp.zeros((1,) + proj_bias.shape[2:], f32)
    mid_vec = jnp.roll(mid_vec, 4, 0)
    vec = jnp.concatenate([in_vec, mid_vec, proj_bias[:, 0], none] + [x[:, 0] for x in up_bias])
    vec = vec.reshape(vec.shape[0], shards, -1).transpose(1, 0, 2)
    vec = lax.psum(lax.psum_scatter(vec, "fsdp", scatter_dimension=0, tiled=True), "dp")[0]
    factor = (groups * shards * rows) ** (-0.5)
    return outputs(layer_out, input_grad, attn, feed, vec, factor, shards)


def solution(mesh):
    both = P(("dp", "fsdp"), None)
    matrix, vector = P("fsdp", None), P("fsdp")
    fast = mesh.shape["dp"] == 4 and mesh.shape["fsdp"] == 8
    return jax.shard_map(
        body_fast if fast else body_plain,
        mesh=mesh,
        in_specs=(both,) * 3 + (matrix,) * 6 + (vector,) * 9,
        out_specs=(both,) * 2 + (matrix,) * 6 + (vector,) * 9,
        check_vma=False,
    )
```

```python
from functools import partial

import jax
import jax.numpy as jnp
from jax import lax
from jax.experimental import pallas as pl
from jax.experimental.pallas import tpu as pltpu
from jax.sharding import PartitionSpec as P

H = 12
HD = 64
SEQ = 512
MOST = 160
BQ = 256
BAND = 416
GAIN_ONE, SHIFT_ONE, QUERY, KEY, VALUE, OUT, GAIN_TWO, SHIFT_TWO, DOWN, UP = range(10)
epsilon = 1e-05
bf16 = jnp.bfloat16
f32 = jnp.float32


def nn(a, b):
    return jnp.dot(a, b, preferred_element_type=f32)


def nt(a, b):
    return lax.dot_general(a, b, (((1,), (1,)), ((), ())), preferred_element_type=f32)


def tn(a, b):
    return lax.dot_general(a, b, (((0,), (0,)), ((), ())), preferred_element_type=f32)


def params(n, mb=56):
    return pltpu.CompilerParams(
        dimension_semantics=("arbitrary",) * n, vmem_limit_bytes=mb * 1024 * 1024
    )


def cost(flops, nbytes, trans=0):
    return pl.CostEstimate(
        flops=int(flops * 50), bytes_accessed=int(nbytes * 50), transcendentals=int(trans)
    )


def moments(v):
    mean = jnp.mean(v, axis=-1, keepdims=True)
    c = v - mean
    inv = lax.rsqrt(jnp.mean(c * c, axis=-1, keepdims=True) + epsilon)
    return c * inv, inv


def shares(place, sides):
    d, z, c = place[0], place[1], place[2]
    for p, (along, near, far) in enumerate(sides):
        core = c ^ p
        parts = ((d, along), (d ^ (1 + core), near), (d ^ (2 - core), far.at[0]), (d ^ 3, far.at[1]))
        for member, view in parts:
            for k in range(3):
                yield member, 2 * (z ^ (k + 1)) + core, view.at[k]


def by_sides(refs):
    return (refs[0], refs[4]), (refs[1:4], refs[5:8])


def start_all(pairs, sem):
    copies = [pltpu.make_async_copy(a, b, sem) for a, b in pairs]
    for copy in copies:
        copy.start()
    return copies


def wait_all(copies):
    for copy in copies:
        copy.wait()


def block_copies(place, refs, out, lead):
    rows = out.shape[1] // 8
    owns, sides = by_sides(refs)
    pairs = []
    for p, own in enumerate(owns):
        s = 2 * place[1] + (place[2] ^ p)
        pairs += [(own.at[4 * lead + b], out.at[b, pl.ds(s * rows, rows), :]) for b in range(4)]
    for member, s, view in shares(place, sides):
        pairs.append((view.at[pl.ds(0, rows), :], out.at[member, pl.ds(s * rows, rows), :]))
    return pairs


def row_copies(place, refs, out, source, skip):
    rows = out.shape[1] // 8
    few = rows // 4
    owns, sides = by_sides(refs)
    pairs = []
    for p, own in enumerate(owns):
        s = 2 * place[1] + (place[2] ^ p)
        for b in range(out.shape[0]):
            pairs.append((own.at[source + b], out.at[b, pl.ds(s * rows, rows), :]))
    for member, s, view in shares(place, sides):
        for b in range(out.shape[0]):
            to = pl.multiple_of(s * rows + member * few, 8)
            pairs.append((view.at[pl.ds(skip + b * few, few), :], out.at[b, pl.ds(to, few), :]))
    return pairs


def split_blocks(place, full, keep, send, b):
    rows = full.shape[0] // 8
    for k in range(4):
        keep[b, k] = full[pl.ds((2 * k + place[2]) * rows, rows), :].astype(bf16)
        send[b, k] = full[pl.ds((2 * k + 1 - place[2]) * rows, rows), :].astype(bf16)


ANY = pl.BlockSpec(memory_space=pl.ANY)


def qkv_kernel(x_ref, w_ref, b_ref, o_ref):
    b = b_ref[0]
    for r in range(x_ref.shape[0] // 256):
        rows = pl.ds(r * 256, 256)
        o_ref[0, rows, :] = (nn(x_ref[rows, :], w_ref[0]) + b).astype(bf16)


def qkv_call(first, w, table):
    rows, d = first.shape
    return pl.pallas_call(
        qkv_kernel,
        grid=(3,),
        in_specs=[
            pl.BlockSpec((rows, d), lambda i: (0, 0)),
            pl.BlockSpec((1, d, d), lambda i: (i, 0, 0)),
            pl.BlockSpec((1, 1, d), lambda i: (QUERY + i, 0, 0)),
        ],
        out_specs=pl.BlockSpec((1, rows, d), lambda i: (i, 0, 0)),
        out_shape=jax.ShapeDtypeStruct((3, rows, d), bf16),
        compiler_params=params(1),
        cost_estimate=cost(6 * rows * d * d, 2 * (rows * d * 4 + 3 * d * d)),
        name="qkv",
    )(first, w, table)


def qkv_fast_kernel(place, x_ref, b_ref, *refs):
    pieces, (o_ref, w_ref, sem) = refs[:8], refs[8:]
    i = pl.program_id(0)

    @pl.when(i == 0)
    def _():
        wait_all(start_all(row_copies(place, pieces, w_ref, 0, 0), sem))

    b = b_ref[0]
    for r in range(x_ref.shape[0] // 256):
        rows = pl.ds(r * 256, 256)
        o_ref[0, rows, :] = (nn(x_ref[rows, :], w_ref[i]) + b).astype(bf16)


def qkv_fast_call(place, first, table, pieces):
    rows, d = first.shape
    return pl.pallas_call(
        qkv_fast_kernel,
        grid_spec=pltpu.PrefetchScalarGridSpec(
            num_scalar_prefetch=1,
            grid=(3,),
            in_specs=[
                pl.BlockSpec((rows, d), lambda i, place: (0, 0)),
                pl.BlockSpec((1, 1, d), lambda i, place: (QUERY + i, 0, 0)),
            ]
            + [ANY] * 8,
            out_specs=[
                pl.BlockSpec((1, rows, d), lambda i, place: (i, 0, 0)),
                pl.BlockSpec((3, d, d), lambda i, place: (0, 0, 0)),
            ],
            scratch_shapes=[pltpu.SemaphoreType.DMA],
        ),
        out_shape=[
            jax.ShapeDtypeStruct((3, rows, d), bf16),
            jax.ShapeDtypeStruct((3, d, d), bf16),
        ],
        compiler_params=params(1),
        cost_estimate=cost(6 * rows * d * d, 2 * (rows * d * 4 + 8 * d * d)),
        name="qkv",
    )(place, first, table, *pieces)


def spans(b):
    return b * BQ, b * (SEQ - BAND)


def attn_fwd_kernel(q_ref, k_ref, v_ref, dr_ref, dc_ref, o_ref, p_ref, bias):
    @pl.when(pl.program_id(1) == 0)
    def _():
        for b in range(2):
            q0, k0 = spans(b)
            same = dc_ref[0, k0 : k0 + BAND, :] == dr_ref[0, :, q0 : q0 + BQ]
            bias[b] = jnp.where(same, 0.0, -3e38)

    low = lax.broadcasted_iota(jnp.int32, (1, 128), 1) < HD
    for b in range(2):
        q0, k0 = spans(b)
        qb = q_ref[0, q0 : q0 + BQ, :] * bf16(HD**-0.5)
        kb = k_ref[0, k0 : k0 + BAND, :]
        vb = v_ref[0, k0 : k0 + BAND, :]
        acc = None
        for hh in range(2):
            mine = low if hh == 0 else jnp.logical_not(low)
            s = nt(kb, jnp.where(mine, qb, bf16(0))) + bias[b]
            e = jnp.exp(s - jnp.max(s, axis=0, keepdims=True))
            p = (e * (1.0 / jnp.sum(e, axis=0, keepdims=True))).astype(bf16)
            p_ref[hh, b] = p
            part = tn(jnp.where(mine, vb, bf16(0)), p)
            acc = part if acc is None else acc + part
        o_ref[q0 : q0 + BQ, :] = acc.T.astype(bf16)


def attn_fwd_call(qkv, doc):
    rows = qkv.shape[1]
    d = qkv.shape[2]
    seqs = rows // SEQ
    hp = d // 128

    def part(i):
        return pl.BlockSpec((1, SEQ, 128), lambda s, h: (i, s, h))

    return pl.pallas_call(
        attn_fwd_kernel,
        grid=(seqs, hp),
        in_specs=[
            part(0),
            part(1),
            part(2),
            pl.BlockSpec((1, 1, SEQ), lambda s, h: (s, 0, 0)),
            pl.BlockSpec((1, SEQ, 1), lambda s, h: (s, 0, 0)),
        ],
        out_specs=[
            pl.BlockSpec((SEQ, 128), lambda s, h: (s, h)),
            pl.BlockSpec((2, 2, BAND, BQ), lambda s, h: (s * hp + h, 0, 0, 0)),
        ],
        out_shape=[
            jax.ShapeDtypeStruct((rows, d), bf16),
            jax.ShapeDtypeStruct((seqs * H, 2, BAND, BQ), bf16),
        ],
        scratch_shapes=[pltpu.VMEM((2, BAND, BQ), f32)],
        compiler_params=params(2),
        cost_estimate=cost(
            seqs * H * 2 * BAND * BQ * 2 * 256, 2 * 4 * rows * d + 4 * seqs * H * BAND * BQ
        ),
        name="attend",
    )(qkv, qkv, qkv, doc[:, None, :], doc[:, :, None])


def attn_bwd_kernel(q_ref, k_ref, v_ref, do_ref, p_ref, o_ref):
    low = lax.broadcasted_iota(jnp.int32, (1, 128), 1) < HD
    scale = bf16(HD**-0.5)
    over = SEQ - BAND
    tails = []
    for b in range(2):
        q0, k0 = spans(b)
        qb = q_ref[0, q0 : q0 + BQ, :] * scale
        dob = do_ref[q0 : q0 + BQ, :]
        kb = k_ref[0, k0 : k0 + BAND, :] * scale
        vb = v_ref[0, k0 : k0 + BAND, :]
        dq = dk = dv = None
        for hh in range(2):
            mine = low if hh == 0 else jnp.logical_not(low)
            p = p_ref[hh, b]
            dom = jnp.where(mine, dob, bf16(0))
            dp = nt(vb, dom)
            pf = p.astype(f32)
            inner = jnp.sum(pf * dp, axis=0, keepdims=True)
            ds = (pf * (dp - inner)).astype(bf16)
            a = nn(p, dom)
            c = nn(ds, jnp.where(mine, qb, bf16(0)))
            g = tn(jnp.where(mine, kb, bf16(0)), ds)
            dv = a if dv is None else dv + a
            dk = c if dk is None else dk + c
            dq = g if dq is None else dq + g
        o_ref[0, q0 : q0 + BQ, :] = dq.T.astype(bf16)
        tails.append((dk, dv))
    for i, (first_part, second_part) in enumerate(zip(*tails)):
        o_ref[i + 1, :over, :] = first_part[:over].astype(bf16)
        o_ref[i + 1, over:BAND, :] = (first_part[over:] + second_part[: BAND - over]).astype(bf16)
        o_ref[i + 1, BAND:, :] = second_part[BAND - over :].astype(bf16)


def attn_bwd_call(qkv, dattn, probs):
    rows = qkv.shape[1]
    d = qkv.shape[2]
    seqs = rows // SEQ
    hp = d // 128

    def part(i):
        return pl.BlockSpec((1, SEQ, 128), lambda s, h: (i, s, h))

    return pl.pallas_call(
        attn_bwd_kernel,
        grid=(seqs, hp),
        in_specs=[
            part(0),
            part(1),
            part(2),
            pl.BlockSpec((SEQ, 128), lambda s, h: (s, h)),
            pl.BlockSpec((2, 2, BAND, BQ), lambda s, h: (s * hp + h, 0, 0, 0)),
        ],
        out_specs=pl.BlockSpec((3, SEQ, 128), lambda s, h: (0, s, h)),
        out_shape=jax.ShapeDtypeStruct((3, rows, d), bf16),
        compiler_params=params(2),
        cost_estimate=cost(
            seqs * H * 2 * BAND * BQ * 2 * 256 * 2, 2 * 7 * rows * d + 4 * seqs * H * BAND * BQ
        ),
        name="attend_back",
    )(qkv, qkv, qkv, dattn, probs)


def row_of(i):
    return pl.BlockSpec((1, 1, 768), lambda *_: (i, 0, 0))


def out_step(a_ref, w, t_ref, bo_ref, g_ref, s_ref, mid_ref, sec_ref):
    mid = t_ref[...].astype(f32) + nn(a_ref[...], w) + bo_ref[0]
    mid_ref[...] = mid
    sc, _ = moments(mid)
    sec_ref[...] = (sc * g_ref[0] + s_ref[0]).astype(bf16)


def out_kernel(a_ref, w_ref, t_ref, bo_ref, g_ref, s_ref, mid_ref, sec_ref):
    out_step(a_ref, w_ref[0], t_ref, bo_ref, g_ref, s_ref, mid_ref, sec_ref)


def out_fast_kernel(place, a_ref, t_ref, bo_ref, g_ref, s_ref, *refs):
    pieces, (mid_ref, sec_ref, w_ref, sem) = refs[:8], refs[8:]

    @pl.when(pl.program_id(0) == 0)
    def _():
        wait_all(start_all(row_copies(place, pieces, w_ref, 8, w_ref.shape[1] // 8), sem))

    out_step(a_ref, w_ref[0], t_ref, bo_ref, g_ref, s_ref, mid_ref, sec_ref)


def out_fast_call(place, attended, tokens, table, pieces):
    rows, d = tokens.shape
    blk = pl.BlockSpec((256, d), lambda i, place: (i, 0))
    return pl.pallas_call(
        out_fast_kernel,
        grid_spec=pltpu.PrefetchScalarGridSpec(
            num_scalar_prefetch=1,
            grid=(rows // 256,),
            in_specs=[blk, blk, row_of(OUT), row_of(GAIN_TWO), row_of(SHIFT_TWO)] + [ANY] * 8,
            out_specs=[blk, blk, pl.BlockSpec((1, d, d), lambda i, place: (0, 0, 0))],
            scratch_shapes=[pltpu.SemaphoreType.DMA],
        ),
        out_shape=[
            jax.ShapeDtypeStruct((rows, d), f32),
            jax.ShapeDtypeStruct((rows, d), bf16),
            jax.ShapeDtypeStruct((1, d, d), bf16),
        ],
        compiler_params=params(1),
        cost_estimate=cost(2 * rows * d * d, rows * d * 10 + 4 * d * d),
        name="project",
    )(place, attended, tokens, table, table, table, *pieces)


def out_call(attended, wo, tokens, table):
    rows, d = tokens.shape
    blk = pl.BlockSpec((256, d), lambda i: (i, 0))
    return pl.pallas_call(
        out_kernel,
        grid=(rows // 256,),
        in_specs=[
            blk, pl.BlockSpec((1, d, d), lambda i: (3, 0, 0)), blk,
            row_of(OUT), row_of(GAIN_TWO), row_of(SHIFT_TWO),
        ],
        out_specs=[blk, blk],
        out_shape=[
            jax.ShapeDtypeStruct((rows, d), f32),
            jax.ShapeDtypeStruct((rows, d), bf16),
        ],
        compiler_params=params(1),
        cost_estimate=cost(2 * rows * d * d, rows * d * 10 + 2 * d * d),
        name="project",
    )(attended, wo, tokens, table, table, table)


def ffn_step(x_ref, g_ref, wu, wd, b, acc_ref, sg_ref, act, hg):
    rows = x_ref.shape[0]
    chunk = 256
    total = jnp.zeros((1, wu.shape[1]), f32)
    def step(r, total):
        at = pl.ds(pl.multiple_of(r * chunk, chunk), chunk)
        h = nn(x_ref[at, :], wu[...]) + b
        ag = nt(g_ref[at, :], wd[...])
        phi = 0.5 + 0.5 * lax.erf(h * (0.5**0.5))
        a = (h * phi).astype(bf16)
        act[at, :] = a
        dens = jnp.exp(-0.5 * (h * h)) * 0.3989422804014327
        hgv = (ag * (phi + h * dens)).astype(bf16)
        hg[at, :] = hgv
        acc_ref[at, :] += nn(a, wd[...])
        sg_ref[at, :] += nt(hgv, wu[...])
        return total + jnp.sum(hgv.astype(f32), axis=0, keepdims=True)

    return lax.fori_loop(0, rows // chunk, step, total)


def ffn_start(start, acc_in, bd_ref, sg_in, acc_ref, sg_ref):
    if start:
        acc_ref[...] = acc_in[...] + bd_ref[0]
        sg_ref[...] = jnp.zeros_like(sg_ref)
    else:
        acc_ref[...] = acc_in[...]
        sg_ref[...] = sg_in[...]


def ffn_kernel(start, x_ref, g_ref, w_ref, b_ref, acc_in, bd_ref, *refs):
    sg_in = None if start else refs[0]
    gw_ref, gb_ref, acc_ref, sg_ref, act, hg = refs[0 if start else 1 :]

    @pl.when(pl.program_id(0) == 0)
    def _():
        ffn_start(start, acc_in, bd_ref, sg_in, acc_ref, sg_ref)

    gb_ref[0] = ffn_step(x_ref, g_ref, w_ref.at[0], w_ref.at[1], b_ref[0], acc_ref, sg_ref, act, hg)
    gw_ref[0] = tn(x_ref[...], hg[...]).astype(bf16)
    gw_ref[1] = tn(act[...], g_ref[...]).astype(bf16)


def ffn_call(lead, second, dgrad, w, table, acc, sg):
    rows, d = second.shape
    n = w.shape[0] // 2
    start = sg is None
    full = pl.BlockSpec((rows, d), lambda j: (0, 0))
    pair = pl.BlockSpec((2, d, d), lambda j: (j, 0, 0))
    return pl.pallas_call(
        partial(ffn_kernel, start),
        grid=(n,),
        in_specs=[
            full, full, pair, pl.BlockSpec((1, 1, d), lambda j: (UP + lead * n + j, 0, 0)),
            full, row_of(DOWN),
        ]
        + ([] if start else [full]),
        out_specs=[pair, pl.BlockSpec((1, 1, d), lambda j: (j, 0, 0)), full, full],
        out_shape=[
            jax.ShapeDtypeStruct((2 * n, d, d), bf16),
            jax.ShapeDtypeStruct((n, 1, d), f32),
            jax.ShapeDtypeStruct((rows, d), f32),
            jax.ShapeDtypeStruct((rows, d), f32),
        ],
        scratch_shapes=[pltpu.VMEM((rows, d), bf16)] * 2,
        compiler_params=params(1),
        cost_estimate=cost(12 * n * rows * d * d, 20 * rows * d + 8 * n * d * d),
        name="feed",
    )(second, dgrad, w, table, acc, table, *([] if start else [sg]))


def ffn_fast_kernel(start, lead, place, x_ref, g_ref, b_ref, acc_in, bd_ref, *refs):
    sg_in, vec_in = (None, None) if start else refs[:2]
    refs = refs[0 if start else 2 :]
    pieces = refs[:8]
    keep, send, vec_ref, acc_ref, sg_ref, w_ref, act, hg, full, sem = refs[8:]
    j = pl.program_id(0)

    @pl.when(j == 0)
    def _():
        copies = start_all(block_copies(place, pieces, w_ref, lead), sem)
        ffn_start(start, acc_in, bd_ref, sg_in, acc_ref, sg_ref)
        vec_ref[...] = jnp.zeros_like(vec_ref) if start else vec_in[...]
        wait_all(copies)

    wu, wd = w_ref.at[2 * j], w_ref.at[2 * j + 1]
    total = ffn_step(x_ref, g_ref, wu, wd, b_ref[0], acc_ref, sg_ref, act, hg)
    vec_ref[pl.ds(2 * lead + j, 1), :] = total
    full[...] = tn(x_ref[...], hg[...]).astype(bf16)
    split_blocks(place, full, keep, send, 0)
    full[...] = tn(act[...], g_ref[...]).astype(bf16)
    split_blocks(place, full, keep, send, 1)


def ffn_fast_call(lead, place, second, dgrad, table, acc, sg, vec, pieces):
    rows, d = second.shape
    start = sg is None
    m = d // 8
    full = pl.BlockSpec((rows, d), lambda j, place: (0, 0))
    half = pl.BlockSpec((2, 4, m, d), lambda j, place: (j, 0, 0, 0))
    rows_of_table = pl.BlockSpec((8, d), lambda j, place: (0, 0))
    return pl.pallas_call(
        partial(ffn_fast_kernel, start, lead),
        grid_spec=pltpu.PrefetchScalarGridSpec(
            num_scalar_prefetch=1,
            grid=(2,),
            in_specs=[
                full, full, pl.BlockSpec((1, 1, d), lambda j, place: (UP + lead * 2 + j, 0, 0)),
                full, row_of(DOWN),
            ]
            + ([] if start else [full, rows_of_table])
            + [ANY] * 8,
            out_specs=[half, half, rows_of_table, full, full],
            scratch_shapes=[pltpu.VMEM((4, d, d), bf16)]
            + [pltpu.VMEM((rows, d), bf16)] * 2
            + [pltpu.VMEM((d, d), bf16), pltpu.SemaphoreType.DMA],
        ),
        out_shape=[
            jax.ShapeDtypeStruct((4, 4, m, d), bf16),
            jax.ShapeDtypeStruct((4, 4, m, d), bf16),
            jax.ShapeDtypeStruct((8, d), f32),
            jax.ShapeDtypeStruct((rows, d), f32),
            jax.ShapeDtypeStruct((rows, d), f32),
        ],
        compiler_params=params(1),
        cost_estimate=cost(24 * rows * d * d, 20 * rows * d + 16 * d * d),
        name="feed",
    )(place, second, dgrad, table, acc, table, *([] if start else [sg, vec]), *pieces)


def norm_back(grad, sc, inv, gain):
    t = grad * gain
    return inv * (
        t - jnp.mean(t, axis=-1, keepdims=True) - sc * jnp.mean(t * sc, axis=-1, keepdims=True)
    )


def mid_kernel(
    place, sg_ref, mid_ref, dy_ref, a_ref, w_ref, g_ref, acc_ref, vec_in,
    mg_ref, ag_ref, vec_ref, lo_ref, wg_ref, *rest,
):
    i = pl.program_id(0)
    wacc = rest[-1]

    @pl.when(i == 0)
    def _():
        wacc[...] = jnp.zeros_like(wacc)
        vec_ref[...] = vec_in[...]

    lo_ref[...] = acc_ref[...].astype(bf16)
    sc, inv = moments(mid_ref[...])
    sg = sg_ref[...]
    dy = dy_ref[...].astype(f32)
    mg = dy + norm_back(sg, sc, inv, g_ref[0])
    mg_ref[...] = mg
    br = mg.astype(bf16)
    vec_ref[4:5, :] += jnp.sum(sg * sc, axis=0, keepdims=True)
    vec_ref[5:6, :] += jnp.sum(sg, axis=0, keepdims=True)
    vec_ref[6:7, :] += jnp.sum(br.astype(f32), axis=0, keepdims=True)
    vec_ref[7:8, :] += jnp.sum(dy, axis=0, keepdims=True)
    ag_ref[...] = nt(br, w_ref[0]).astype(bf16)
    wacc[...] += tn(a_ref[...], br)

    @pl.when(i == pl.num_programs(0) - 1)
    def _():
        if len(rest) == 1:
            wg_ref[0] = wacc[...].astype(bf16)
        else:
            split_blocks(place, wacc, wg_ref, rest[0], 0)


def mid_call(place, sg, mid, dy, attended, wo, table, acc, vec, split):
    rows, d = sg.shape
    blk = pl.BlockSpec((256, d), lambda i, place: (i, 0))
    grad = (1, 4, d // 8, d) if split else (1, d, d)
    last = wo.shape[0] - 1
    return pl.pallas_call(
        mid_kernel,
        grid_spec=pltpu.PrefetchScalarGridSpec(
            num_scalar_prefetch=1,
            grid=(rows // 256,),
            in_specs=[
                blk, blk, blk, blk, pl.BlockSpec((1, d, d), lambda i, place: (last, 0, 0)),
                row_of(GAIN_TWO), blk, pl.BlockSpec((8, d), lambda i, place: (0, 0)),
            ],
            out_specs=[blk, blk, pl.BlockSpec((8, d), lambda i, place: (0, 0)), blk]
            + [pl.BlockSpec(grad, lambda i, place: (0,) * len(grad))] * (2 if split else 1),
            scratch_shapes=[pltpu.VMEM((d, d), f32)],
        ),
        out_shape=[
            jax.ShapeDtypeStruct((rows, d), f32),
            jax.ShapeDtypeStruct((rows, d), bf16),
            jax.ShapeDtypeStruct((8, d), f32),
            jax.ShapeDtypeStruct((rows, d), bf16),
        ]
        + [jax.ShapeDtypeStruct(grad, bf16)] * (2 if split else 1),
        compiler_params=params(1),
        cost_estimate=cost(4 * rows * d * d, rows * d * 22 + 4 * d * d),
        name="middle_back",
    )(place, sg, mid, dy, attended, wo, table, acc, vec)


def wgrad_kernel(x_ref, g_ref, o_ref, b_ref):
    o_ref[0] = tn(x_ref[...], g_ref[0]).astype(bf16)
    b_ref[0] = jnp.sum(g_ref[0].astype(f32), axis=0, keepdims=True)


def wgrad_call(first, grads):
    rows, d = first.shape
    return pl.pallas_call(
        wgrad_kernel,
        grid=(3,),
        in_specs=[
            pl.BlockSpec((rows, d), lambda i: (0, 0)),
            pl.BlockSpec((1, rows, d), lambda i: (i, 0, 0)),
        ],
        out_specs=[
            pl.BlockSpec((1, d, d), lambda i: (i, 0, 0)),
            pl.BlockSpec((1, 1, d), lambda i: (i, 0, 0)),
        ],
        out_shape=[
            jax.ShapeDtypeStruct((3, d, d), bf16),
            jax.ShapeDtypeStruct((3, 1, d), f32),
        ],
        compiler_params=params(1),
        cost_estimate=cost(6 * rows * d * d, 2 * (rows * d * 4 + 3 * d * d)),
        name="weight_back",
    )(first, grads)


def wgrad_fast_kernel(place, x_ref, g_ref, vec_in, keep, send, vec_ref, full):
    i = pl.program_id(0)

    @pl.when(i == 0)
    def _():
        vec_ref[:8, :] = vec_in[...]
        vec_ref[8:, :] = jnp.zeros_like(vec_in)

    full[...] = tn(x_ref[...], g_ref[0])
    vec_ref[pl.ds(8 + i, 1), :] = jnp.sum(g_ref[0].astype(f32), axis=0, keepdims=True)
    split_blocks(place, full, keep, send, 0)


def wgrad_fast_call(place, first, grads, vec):
    rows, d = first.shape
    m = d // 8
    half = pl.BlockSpec((1, 4, m, d), lambda i, place: (i, 0, 0, 0))
    return pl.pallas_call(
        wgrad_fast_kernel,
        grid_spec=pltpu.PrefetchScalarGridSpec(
            num_scalar_prefetch=1,
            grid=(3,),
            in_specs=[
                pl.BlockSpec((rows, d), lambda i, place: (0, 0)),
                pl.BlockSpec((1, rows, d), lambda i, place: (i, 0, 0)),
                pl.BlockSpec((8, d), lambda i, place: (0, 0)),
            ],
            out_specs=[half, half, pl.BlockSpec((16, d), lambda i, place: (0, 0))],
            scratch_shapes=[pltpu.VMEM((d, d), f32)],
        ),
        out_shape=[
            jax.ShapeDtypeStruct((3, 4, m, d), bf16),
            jax.ShapeDtypeStruct((3, 4, m, d), bf16),
            jax.ShapeDtypeStruct((16, d), f32),
        ],
        compiler_params=params(1),
        cost_estimate=cost(6 * rows * d * d, 2 * (rows * d * 4 + 3 * d * d)),
        name="weight_back",
    )(place, first, grads, vec)


def input_kernel(start, g_ref, w_ref, t_ref, mg_ref, gain_ref, *refs):
    o_ref, vec_ref = refs[-2:]

    @pl.when(pl.program_id(0) == 0)
    def _():
        vec_ref[...] = jnp.zeros_like(vec_ref) if start else refs[0][...]

    fg = nt(g_ref[0], w_ref[0]) + nt(g_ref[1], w_ref[1]) + nt(g_ref[2], w_ref[2])
    sc, inv = moments(t_ref[...].astype(f32))
    o_ref[...] = (mg_ref[...] + norm_back(fg, sc, inv, gain_ref[0])).astype(bf16)
    vec_ref[0:1, :] += jnp.sum(fg * sc, axis=0, keepdims=True)
    vec_ref[1:2, :] += jnp.sum(fg, axis=0, keepdims=True)


def input_call(grads, w, tokens, mg, table, skip, steps, before=()):
    rows, d = tokens.shape
    blk = pl.BlockSpec((256, d), lambda i: (skip + i, 0))
    vec = pl.BlockSpec((8, d), lambda i: (0, 0))
    start = not before
    return pl.pallas_call(
        partial(input_kernel, start),
        grid=(steps,),
        in_specs=[
            pl.BlockSpec((3, 256, d), lambda i: (0, skip + i, 0)),
            pl.BlockSpec((3, d, d), lambda i: (0, 0, 0)),
            blk,
            blk,
            row_of(GAIN_ONE),
        ]
        + ([] if start else [vec, ANY]),
        out_specs=[blk, vec],
        out_shape=[
            jax.ShapeDtypeStruct((rows, d), bf16),
            jax.ShapeDtypeStruct((8, d), f32),
        ],
        input_output_aliases={} if start else {6: 0},
        compiler_params=params(1),
        cost_estimate=cost(1536 * steps * d * d, 256 * steps * d * 14 + 6 * d * d),
        name="input_back",
    )(grads, w, tokens, mg, table, *([] if start else [before[1], before[0]]))


CORE = 1
ALONG = (2, 4, 6)
GROUP = (8, 16, 24)


def hop(x, mask):
    return lax.ppermute(x, ("dp", "fsdp"), [(i, i ^ mask) for i in range(32)])


def group_hop(x, second):
    pairs = [(i, i ^ (GROUP[0] if i % 2 == second else GROUP[1])) for i in range(32)]
    return lax.ppermute(x, ("dp", "fsdp"), pairs)


def pick(x, index, axis=0):
    return lax.dynamic_index_in_dim(x, index, axis, keepdims=False)


def after(deps, *xs):
    return lax.optimization_barrier((*xs, *deps))[: len(xs)]


def wide(x):
    return x.astype(f32)


def add_core(keep, got):
    return (wide(keep) + wide(got)).astype(bf16)


def quarter(x, index, axis):
    n = x.shape[axis] // 4
    return lax.dynamic_slice_in_dim(x, index * n, n, axis)


def add_two(a, b):
    return (wide(a) + wide(b)).astype(bf16)


def turn(x, bits):
    for axis, bit in enumerate(bits):
        x = jnp.where(bit == 0, x, jnp.flip(x, axis))
    return x


def add_all(first, others):
    total = wide(first)
    for other in others:
        total = total + wide(other)
    return total.astype(bf16)


def segment_ids(lengths):
    ends = jnp.cumsum(lengths, axis=-1)
    places = jnp.arange(SEQ, dtype=jnp.int32)
    return jnp.sum((places[None, :, None] >= ends[:, None, :]).astype(jnp.int32), axis=-1)


def pack_vectors(pre_gain, pre_shift, bias_query, bias_value, bias_out, mid_gain, mid_shift, bias_up, bias_down):
    none = jnp.zeros_like(bias_query)
    return jnp.concatenate(
        [pre_gain, pre_shift, bias_query, none, bias_value, bias_out, mid_gain, mid_shift, bias_down, bias_up]
    )[None]


def make_table(small):
    shards = small.shape[0]
    n = small.shape[1] * shards // 768
    return small.reshape(shards, n, -1).transpose(1, 0, 2).reshape(n, 1, 768).astype(f32)


def order_hidden(w_up, w_down, shards):
    m, d = w_up.shape[0], w_up.shape[0] * shards
    parts = w_down.shape[0] // m
    up = w_up.reshape(m, shards, parts, m).transpose(2, 0, 1, 3).reshape(parts, m, d)
    return jnp.stack([up, w_down.reshape(parts, m, d)], 1).reshape(2 * parts, m, d)


VEC_ROWS = (0, 1, 16, 18, 10, 8, 9)
DOWN_ROW, UP_ROW = 11, 20


def outputs(layer_out, input_grad, attn, feed, vec, factor, shards):
    m, d = attn[0].shape
    parts = len(feed) // 2
    vec = vec * factor
    up = jnp.stack(feed[0::2]).reshape(parts, m, shards, m).transpose(1, 2, 0, 3)
    return (
        layer_out,
        input_grad,
        *(wide(g) * factor for g in attn),
        wide(up.reshape(m, parts * d)) * factor,
        wide(jnp.concatenate(feed[1::2])) * factor,
        *(vec[i] for i in VEC_ROWS),
        vec[UP_ROW:].reshape(-1),
        vec[DOWN_ROW],
    )


def body_fast(tokens, cotangent, doc_lengths, w_query, w_key, w_value, w_out, w_up, w_down, *vectors):
    rows, d = tokens.shape
    n = d // 8
    dp, at = lax.axis_index("dp"), lax.axis_index("fsdp")
    z, core = at // 2, at % 2
    place = jnp.stack([dp, z, core]).astype(jnp.int32)
    one, two = 1 + core, 2 - core

    quarters = [quarter(w, dp, 0) for w in (w_query, w_key, w_value, w_out)]
    attn_mine = jnp.concatenate(quarters[:3])
    attn_z = [hop(attn_mine, m) for m in ALONG]
    attn_along = jnp.stack(attn_z)
    attn_near = group_hop(attn_along, 0)
    attn_own = jnp.stack([w_query, w_key, w_value])
    attn_own_cross = hop(attn_own, CORE)
    small = pack_vectors(*after([attn_along], *vectors))
    width = small.shape[1]
    low = jnp.pad(small[0], (0, 8 * d - width)).reshape(8, d)
    low = jnp.concatenate([low, hop(low, CORE)])
    attn_far = jnp.stack([attn_along, attn_near])
    (low,) = after([attn_far], low)
    low_across = hop(low, ALONG[1])
    low_beside = hop(jnp.stack([low, low_across]), ALONG[0])
    lows = jnp.stack([low, low_beside[0], low_across, low_beside[1]])
    small = lows.reshape(2, 2, 2, 8 * d)[..., :width]
    table = make_table(turn(small, (z // 2, z % 2, core)).reshape(8, width))
    attn_along_cross = hop(attn_along, CORE)
    attn_far = group_hop(attn_far, 1)
    attn_near_cross = hop(attn_near, CORE)
    attn_far_cross = hop(attn_far, CORE)

    feed_own = order_hidden(w_up, w_down, 8)
    mine_one = jnp.concatenate([pick(feed_own[:4], dp), quarters[3]])
    tokens_late, lengths_late, mine_one = after([attn_along], tokens, doc_lengths, mine_one)
    mine_two = pick(feed_own[4:], dp)
    feed_own = jnp.concatenate([feed_own, w_out[None]])
    across_one = hop(mine_one, ALONG[1])
    mine_late, across_late = after([attn_near], mine_one, across_one)
    beside_one = hop(jnp.stack([mine_late, across_late]), ALONG[0])
    beside_one, mine_two = after([attn_far], beside_one, mine_two)
    along_one = jnp.stack([beside_one[0], across_one, beside_one[1]])
    near_one = group_hop(along_one, 0)
    across_two = hop(mine_two, ALONG[1])

    doc = segment_ids(lengths_late)
    scaled, _ = moments(wide(tokens_late))
    first = (scaled * table[GAIN_ONE] + table[SHIFT_ONE]).astype(bf16)
    qkv, attn_w = qkv_fast_call(
        place, first, table,
        [attn_own, attn_along, attn_near, attn_far]
        + [attn_own_cross, attn_along_cross, attn_near_cross, attn_far_cross],
    )
    feed_own_late, along_one, near_one, mine_two, across_two = after(
        [qkv], feed_own, along_one, near_one, mine_two, across_two
    )
    (qkv,) = after([near_one, across_two], qkv)
    far_one = group_hop(jnp.stack([along_one, near_one]), 1)
    beside_two = hop(jnp.stack([mine_two, across_two]), ALONG[0])
    feed_cross = hop(feed_own_late, CORE)
    pieces_one = [feed_cross, hop(along_one, CORE), hop(near_one, CORE)]
    attended, probs = attn_fwd_call(qkv, doc)
    far_one, beside_two, attended_late = after([attended], far_one, beside_two, attended)
    (attended_late,) = after([far_one, beside_two], attended_late)
    pieces_one = [feed_own, along_one, near_one, far_one, *pieces_one, hop(far_one, CORE)]
    along_two = jnp.stack([beside_two[0], across_two, beside_two[1]])
    near_two = group_hop(along_two, 0)
    middle, second, wo = out_fast_call(place, attended_late, tokens, table, pieces_one)
    along_two, near_two, second = after([middle], along_two, near_two, second)
    (second,) = after([near_two], second)
    far_two = group_hop(jnp.stack([along_two, near_two]), 1)
    pieces_two = [along_two, near_two, far_two]
    pieces_two = [feed_own, *pieces_two, feed_cross, *(hop(x, CORE) for x in pieces_two)]

    def first_hop(parts):
        return group_hop(jnp.stack([parts(dp ^ one), parts(dp ^ 3)]), 0)

    def fold(parts, got):
        return add_two(parts(dp), got[0]), add_two(parts(dp ^ two), got[1])

    def beside(x):
        return jnp.stack([pick(x, z ^ 1), pick(x, z ^ 3)])

    def across(x, got):
        return add_two(pick(x, z), got[0]), add_two(pick(x, z ^ 2), got[1])

    keep_one, send_one, vec, acc, sg = ffn_fast_call(
        0, place, second, cotangent, table, middle, None, None, pieces_one
    )
    (send_one,) = after([far_two], send_one)
    got_one = hop(send_one, CORE)
    parts_one = lambda i: add_two(pick(keep_one, i), pick(got_one, i))
    near_one = first_hop(parts_one)
    (sg,) = after([got_one], sg)
    keep_two, send_two, vec, acc, sg = ffn_fast_call(
        1, place, second, cotangent, table, acc, sg, vec, pieces_two
    )
    got_two = hop(send_two, CORE)
    (sg,) = after([near_one], sg)
    mine_one, far_one = fold(parts_one, near_one)
    (sg,) = after([far_one], sg)
    far_one = group_hop(far_one, 1)
    mid_grad, attended_grad, vec, layer_out, keep_out, send_out = mid_call(
        place, sg, middle, cotangent, attended, wo, table, acc, vec, True
    )
    got_out = hop(send_out, CORE)
    (attended_grad,) = after([far_one, got_two, got_out], attended_grad)
    sum_one = add_two(mine_one, far_one)
    beside_one = hop(beside(sum_one), ALONG[0])

    def parts_two(i):
        out = add_two(quarter(keep_out[0], i, 1), quarter(got_out[0], i, 1))
        return jnp.concatenate([add_two(pick(keep_two, i), pick(got_two, i)), out], 1)

    near_two = first_hop(parts_two)
    grads = attn_bwd_call(qkv, attended_grad, probs)
    (beside_one,) = after([grads], beside_one)
    mine_one, across_one = across(sum_one, beside_one)
    mine_two, far_two = fold(parts_two, near_two)
    (grads,) = after([across_one, far_two], grads)
    across_one = hop(across_one, ALONG[1])
    far_two = group_hop(far_two, 1)
    keep_attn, send_attn, vec = wgrad_fast_call(place, first, grads, vec)
    (send_attn,) = after([across_one, far_two], send_attn)
    got_attn = hop(send_attn, CORE)
    sum_two = add_two(mine_two, far_two)
    beside_two = beside(sum_two)
    (got_attn,) = after([beside_two], got_attn)
    parts_attn = lambda i: add_two(quarter(keep_attn, i, 2), quarter(got_attn, i, 2))
    near_attn = jnp.stack([parts_attn(dp ^ one), parts_attn(dp ^ 3)])
    (grads,) = after([beside_two, near_attn], grads)
    beside_two = hop(beside_two, ALONG[0])
    near_attn = group_hop(near_attn, 0)
    input_grad, in_vec = input_call(grads, attn_w, tokens, mid_grad, table, 0, rows // 256)
    near_attn, beside_two = after([in_vec], near_attn, beside_two)
    mine_attn, far_attn = fold(parts_attn, near_attn)
    mine_two, across_two = across(sum_two, beside_two)
    mine_one, across_one, in_vec, vec = after([far_attn], mine_one, across_one, in_vec, vec)
    far_attn = group_hop(far_attn, 1)
    across_two = hop(across_two, ALONG[1])

    in_vec = in_vec[:2] + hop(in_vec[:2], CORE)
    vec = vec.reshape(16, 4, 2, n).transpose(2, 1, 0, 3)
    vec = pick(vec, core) + hop(pick(vec, 1 - core), CORE)
    vec = vec.reshape(4, 16 * n // d, d).astype(bf16)
    low = jnp.concatenate(
        [vec, jnp.broadcast_to(in_vec.astype(bf16)[None], (4, 2, d)), jnp.zeros((4, 4, d), bf16)], 1
    )
    far_attn, low = after((), far_attn, low)
    attn_sum = add_two(mine_attn, far_attn)
    many = 3 * attn_sum.shape[2]
    rest = attn_sum.transpose(1, 0, 2, 3).reshape(4, many, d)
    rest = jnp.concatenate([rest, low], 1)
    beside_rest = beside(rest)
    (across_two,) = after([beside_rest], across_two)
    beside_rest = hop(beside_rest, ALONG[0])
    final_feed = jnp.concatenate([add_two(mine_one, across_one), add_two(mine_two, across_two)])
    feed_near = group_hop(final_feed, 0)
    mine_rest, across_rest = across(rest, beside_rest)
    final_feed, feed_near = after([across_rest], final_feed, feed_near)
    feed_far = group_hop(jnp.stack([final_feed, feed_near]), 1)
    final_rest = add_two(mine_rest, hop(across_rest, ALONG[1]))
    (final_rest,) = after([feed_far], final_rest)
    final_rest = jnp.stack([final_rest] + [hop(final_rest, m) for m in GROUP])
    vec = jnp.sum(wide(final_rest[:, many : many + 4]), axis=0)
    in_vec = lax.dynamic_slice_in_dim(vec[2:], at * n, n, 1)
    vec = vec[:2].reshape(16, n)
    none = jnp.zeros((6, n), f32)
    vec = jnp.concatenate([in_vec, none, vec[4:8], none[:4], vec[8:12], vec[:4]])
    final_feed = jnp.stack([final_feed, feed_near, feed_far[0], feed_far[1]])
    order = lambda b: jnp.where(b == one, 1, jnp.where(b == two, 2, b))
    final_attn = [pick(final_rest, dp ^ b)[:many].reshape(3, many // 3, d) for b in range(4)]
    final_feed = [pick(final_feed, order(dp ^ b)) for b in range(4)]
    attn = [jnp.concatenate([x[i] for x in final_attn]) for i in range(3)]
    attn.append(jnp.concatenate([x[2 * n :] for x in final_feed]))
    feed = [x[:n] for x in final_feed] + [x[n : 2 * n] for x in final_feed]
    factor = (32 * rows) ** (-0.5)
    return outputs(layer_out, input_grad, attn, feed, vec, factor, 8)


def gather(local):
    return lax.all_gather(local, "fsdp", axis=1, tiled=True)


def reduce(grad):
    part = lax.psum_scatter(wide(grad), "fsdp", scatter_dimension=1, tiled=True)
    total = lax.psum(part.astype(bf16), "dp")
    return [total[b] for b in range(grad.shape[0])]


def body_plain(tokens, cotangent, doc_lengths, w_query, w_key, w_value, w_out, w_up, w_down, *vectors):
    rows = tokens.shape[0]
    shards, groups = lax.axis_size("fsdp"), lax.axis_size("dp")
    table = make_table(lax.all_gather(pack_vectors(*vectors), "fsdp", axis=0, tiled=True))
    attn_w = gather(jnp.stack([w_query, w_key, w_value, w_out]))
    feed_own = order_hidden(w_up, w_down, shards)
    doc = segment_ids(doc_lengths)
    scaled, _ = moments(wide(tokens))
    first = (scaled * table[GAIN_ONE] + table[SHIFT_ONE]).astype(bf16)
    qkv = qkv_call(first, attn_w, table)
    attended, probs = attn_fwd_call(qkv, doc)
    middle, second = out_call(attended, attn_w, tokens, table)
    acc, sg = middle, None
    feed = []
    up_bias = []
    for lead in range(feed_own.shape[0] // 4):
        w = gather(feed_own[4 * lead : 4 * lead + 4])
        grad, bias_grad, acc, sg = ffn_call(lead, second, cotangent, w, table, acc, sg)
        feed += reduce(grad)
        up_bias.append(bias_grad)
    mid_grad, attended_grad, mid_vec, layer_out, out_grad = mid_call(
        jnp.zeros((3,), jnp.int32), sg, middle, cotangent, attended, attn_w, table, acc,
        jnp.zeros((8, tokens.shape[1]), f32), False,
    )
    grads = attn_bwd_call(qkv, attended_grad, probs)
    proj_grad, proj_bias = wgrad_call(first, grads)
    input_grad, in_vec = input_call(grads, attn_w, tokens, mid_grad, table, 0, tokens.shape[0] // 256)
    attn = reduce(jnp.concatenate([proj_grad, out_grad]))
    none = jnp.zeros((1,) + proj_bias.shape[2:], f32)
    mid_vec = jnp.roll(mid_vec, 4, 0)
    vec = jnp.concatenate([in_vec, mid_vec, proj_bias[:, 0], none] + [x[:, 0] for x in up_bias])
    vec = vec.reshape(vec.shape[0], shards, -1).transpose(1, 0, 2)
    vec = lax.psum(lax.psum_scatter(vec, "fsdp", scatter_dimension=0, tiled=True), "dp")[0]
    factor = (groups * shards * rows) ** (-0.5)
    return outputs(layer_out, input_grad, attn, feed, vec, factor, shards)


def solution(mesh):
    both = P(("dp", "fsdp"), None)
    matrix, vector = P("fsdp", None), P("fsdp")
    fast = mesh.shape["dp"] == 4 and mesh.shape["fsdp"] == 8
    return jax.shard_map(
        body_fast if fast else body_plain,
        mesh=mesh,
        in_specs=(both,) * 3 + (matrix,) * 6 + (vector,) * 9,
        out_specs=(both,) * 2 + (matrix,) * 6 + (vector,) * 9,
        check_vma=False,
    )
```

```python
from functools import partial

import jax
import jax.numpy as jnp
from jax import lax
from jax.experimental import pallas as pl
from jax.experimental.pallas import tpu as pltpu
from jax.sharding import PartitionSpec as P

H = 12
HD = 64
SEQ = 512
MOST = 160
BQ = 256
BAND = 416
GAIN_ONE, SHIFT_ONE, QUERY, KEY, VALUE, OUT, GAIN_TWO, SHIFT_TWO, DOWN, UP = range(10)
epsilon = 1e-05
bf16 = jnp.bfloat16
f32 = jnp.float32


def nn(a, b):
    return jnp.dot(a, b, preferred_element_type=f32)


def nt(a, b):
    return lax.dot_general(a, b, (((1,), (1,)), ((), ())), preferred_element_type=f32)


def tn(a, b):
    return lax.dot_general(a, b, (((0,), (0,)), ((), ())), preferred_element_type=f32)


def params(n, mb=56):
    return pltpu.CompilerParams(
        dimension_semantics=("arbitrary",) * n, vmem_limit_bytes=mb * 1024 * 1024
    )


def cost(flops, nbytes, trans=0):
    return pl.CostEstimate(
        flops=int(flops * 50), bytes_accessed=int(nbytes * 50), transcendentals=int(trans)
    )


def moments(v):
    mean = jnp.mean(v, axis=-1, keepdims=True)
    c = v - mean
    inv = lax.rsqrt(jnp.mean(c * c, axis=-1, keepdims=True) + epsilon)
    return c * inv, inv


def shares(place, sides):
    d, z, c = place[0], place[1], place[2]
    for p, (along, near, far) in enumerate(sides):
        core = c ^ p
        parts = ((d, along), (d ^ (1 + core), near), (d ^ (2 - core), far.at[0]), (d ^ 3, far.at[1]))
        for member, view in parts:
            for k in range(3):
                yield member, 2 * (z ^ (k + 1)) + core, view.at[k]


def by_sides(refs):
    return (refs[0], refs[4]), (refs[1:4], refs[5:8])


def start_all(pairs, sem):
    copies = [pltpu.make_async_copy(a, b, sem) for a, b in pairs]
    for copy in copies:
        copy.start()
    return copies


def wait_all(copies):
    for copy in copies:
        copy.wait()


def block_copies(place, refs, out, lead):
    rows = out.shape[1] // 8
    owns, sides = by_sides(refs)
    pairs = []
    for p, own in enumerate(owns):
        s = 2 * place[1] + (place[2] ^ p)
        pairs += [(own.at[4 * lead + b], out.at[b, pl.ds(s * rows, rows), :]) for b in range(4)]
    for member, s, view in shares(place, sides):
        pairs.append((view.at[pl.ds(0, rows), :], out.at[member, pl.ds(s * rows, rows), :]))
    return pairs


def row_copies(place, refs, out, source, skip):
    rows = out.shape[1] // 8
    few = rows // 4
    owns, sides = by_sides(refs)
    pairs = []
    for p, own in enumerate(owns):
        s = 2 * place[1] + (place[2] ^ p)
        for b in range(out.shape[0]):
            pairs.append((own.at[source + b], out.at[b, pl.ds(s * rows, rows), :]))
    for member, s, view in shares(place, sides):
        for b in range(out.shape[0]):
            to = pl.multiple_of(s * rows + member * few, 8)
            pairs.append((view.at[pl.ds(skip + b * few, few), :], out.at[b, pl.ds(to, few), :]))
    return pairs


def split_blocks(place, full, keep, send, b):
    rows = full.shape[0] // 8
    for k in range(4):
        keep[b, k] = full[pl.ds((2 * k + place[2]) * rows, rows), :].astype(bf16)
        send[b, k] = full[pl.ds((2 * k + 1 - place[2]) * rows, rows), :].astype(bf16)


ANY = pl.BlockSpec(memory_space=pl.ANY)


def qkv_kernel(x_ref, w_ref, b_ref, o_ref):
    b = b_ref[0]
    for r in range(x_ref.shape[0] // 256):
        rows = pl.ds(r * 256, 256)
        o_ref[0, rows, :] = (nn(x_ref[rows, :], w_ref[0]) + b).astype(bf16)


def qkv_call(first, w, table):
    rows, d = first.shape
    return pl.pallas_call(
        qkv_kernel,
        grid=(3,),
        in_specs=[
            pl.BlockSpec((rows, d), lambda i: (0, 0)),
            pl.BlockSpec((1, d, d), lambda i: (i, 0, 0)),
            pl.BlockSpec((1, 1, d), lambda i: (QUERY + i, 0, 0)),
        ],
        out_specs=pl.BlockSpec((1, rows, d), lambda i: (i, 0, 0)),
        out_shape=jax.ShapeDtypeStruct((3, rows, d), bf16),
        compiler_params=params(1),
        cost_estimate=cost(6 * rows * d * d, 2 * (rows * d * 4 + 3 * d * d)),
        name="qkv",
    )(first, w, table)


def qkv_fast_kernel(place, x_ref, b_ref, *refs):
    pieces, (o_ref, w_ref, sem) = refs[:8], refs[8:]
    i = pl.program_id(0)

    @pl.when(i == 0)
    def _():
        wait_all(start_all(row_copies(place, pieces, w_ref, 0, 0), sem))

    b = b_ref[0]
    for r in range(x_ref.shape[0] // 256):
        rows = pl.ds(r * 256, 256)
        o_ref[0, rows, :] = (nn(x_ref[rows, :], w_ref[i]) + b).astype(bf16)


def qkv_fast_call(place, first, table, pieces):
    rows, d = first.shape
    return pl.pallas_call(
        qkv_fast_kernel,
        grid_spec=pltpu.PrefetchScalarGridSpec(
            num_scalar_prefetch=1,
            grid=(3,),
            in_specs=[
                pl.BlockSpec((rows, d), lambda i, place: (0, 0)),
                pl.BlockSpec((1, 1, d), lambda i, place: (QUERY + i, 0, 0)),
            ]
            + [ANY] * 8,
            out_specs=[
                pl.BlockSpec((1, rows, d), lambda i, place: (i, 0, 0)),
                pl.BlockSpec((3, d, d), lambda i, place: (0, 0, 0)),
            ],
            scratch_shapes=[pltpu.SemaphoreType.DMA],
        ),
        out_shape=[
            jax.ShapeDtypeStruct((3, rows, d), bf16),
            jax.ShapeDtypeStruct((3, d, d), bf16),
        ],
        compiler_params=params(1),
        cost_estimate=cost(6 * rows * d * d, 2 * (rows * d * 4 + 8 * d * d)),
        name="qkv",
    )(place, first, table, *pieces)


def spans(b):
    return b * BQ, b * (SEQ - BAND)


def attn_fwd_kernel(q_ref, k_ref, v_ref, dr_ref, dc_ref, o_ref, p_ref, bias):
    @pl.when(pl.program_id(1) == 0)
    def _():
        for b in range(2):
            q0, k0 = spans(b)
            same = dc_ref[0, k0 : k0 + BAND, :] == dr_ref[0, :, q0 : q0 + BQ]
            bias[b] = jnp.where(same, 0.0, -3e38)

    low = lax.broadcasted_iota(jnp.int32, (1, 128), 1) < HD
    for b in range(2):
        q0, k0 = spans(b)
        qb = q_ref[0, q0 : q0 + BQ, :] * bf16(HD**-0.5)
        kb = k_ref[0, k0 : k0 + BAND, :]
        vb = v_ref[0, k0 : k0 + BAND, :]
        acc = None
        for hh in range(2):
            mine = low if hh == 0 else jnp.logical_not(low)
            s = nt(kb, jnp.where(mine, qb, bf16(0))) + bias[b]
            e = jnp.exp(s - jnp.max(s, axis=0, keepdims=True))
            p = (e * (1.0 / jnp.sum(e, axis=0, keepdims=True))).astype(bf16)
            p_ref[hh, b] = p
            part = tn(jnp.where(mine, vb, bf16(0)), p)
            acc = part if acc is None else acc + part
        o_ref[q0 : q0 + BQ, :] = acc.T.astype(bf16)


def attn_fwd_call(qkv, doc):
    rows = qkv.shape[1]
    d = qkv.shape[2]
    seqs = rows // SEQ
    hp = d // 128

    def part(i):
        return pl.BlockSpec((1, SEQ, 128), lambda s, h: (i, s, h))

    return pl.pallas_call(
        attn_fwd_kernel,
        grid=(seqs, hp),
        in_specs=[
            part(0),
            part(1),
            part(2),
            pl.BlockSpec((1, 1, SEQ), lambda s, h: (s, 0, 0)),
            pl.BlockSpec((1, SEQ, 1), lambda s, h: (s, 0, 0)),
        ],
        out_specs=[
            pl.BlockSpec((SEQ, 128), lambda s, h: (s, h)),
            pl.BlockSpec((2, 2, BAND, BQ), lambda s, h: (s * hp + h, 0, 0, 0)),
        ],
        out_shape=[
            jax.ShapeDtypeStruct((rows, d), bf16),
            jax.ShapeDtypeStruct((seqs * H, 2, BAND, BQ), bf16),
        ],
        scratch_shapes=[pltpu.VMEM((2, BAND, BQ), f32)],
        compiler_params=params(2),
        cost_estimate=cost(
            seqs * H * 2 * BAND * BQ * 2 * 256, 2 * 4 * rows * d + 4 * seqs * H * BAND * BQ
        ),
        name="attend",
    )(qkv, qkv, qkv, doc[:, None, :], doc[:, :, None])


def attn_bwd_kernel(q_ref, k_ref, v_ref, do_ref, p_ref, o_ref):
    low = lax.broadcasted_iota(jnp.int32, (1, 128), 1) < HD
    scale = bf16(HD**-0.5)
    over = SEQ - BAND
    tails = []
    for b in range(2):
        q0, k0 = spans(b)
        qb = q_ref[0, q0 : q0 + BQ, :] * scale
        dob = do_ref[q0 : q0 + BQ, :]
        kb = k_ref[0, k0 : k0 + BAND, :] * scale
        vb = v_ref[0, k0 : k0 + BAND, :]
        dq = dk = dv = None
        for hh in range(2):
            mine = low if hh == 0 else jnp.logical_not(low)
            p = p_ref[hh, b]
            dom = jnp.where(mine, dob, bf16(0))
            dp = nt(vb, dom)
            pf = p.astype(f32)
            inner = jnp.sum(pf * dp, axis=0, keepdims=True)
            ds = (pf * (dp - inner)).astype(bf16)
            a = nn(p, dom)
            c = nn(ds, jnp.where(mine, qb, bf16(0)))
            g = tn(jnp.where(mine, kb, bf16(0)), ds)
            dv = a if dv is None else dv + a
            dk = c if dk is None else dk + c
            dq = g if dq is None else dq + g
        o_ref[0, q0 : q0 + BQ, :] = dq.T.astype(bf16)
        tails.append((dk, dv))
    for i, (first_part, second_part) in enumerate(zip(*tails)):
        o_ref[i + 1, :over, :] = first_part[:over].astype(bf16)
        o_ref[i + 1, over:BAND, :] = (first_part[over:] + second_part[: BAND - over]).astype(bf16)
        o_ref[i + 1, BAND:, :] = second_part[BAND - over :].astype(bf16)


def attn_bwd_call(qkv, dattn, probs):
    rows = qkv.shape[1]
    d = qkv.shape[2]
    seqs = rows // SEQ
    hp = d // 128

    def part(i):
        return pl.BlockSpec((1, SEQ, 128), lambda s, h: (i, s, h))

    return pl.pallas_call(
        attn_bwd_kernel,
        grid=(seqs, hp),
        in_specs=[
            part(0),
            part(1),
            part(2),
            pl.BlockSpec((SEQ, 128), lambda s, h: (s, h)),
            pl.BlockSpec((2, 2, BAND, BQ), lambda s, h: (s * hp + h, 0, 0, 0)),
        ],
        out_specs=pl.BlockSpec((3, SEQ, 128), lambda s, h: (0, s, h)),
        out_shape=jax.ShapeDtypeStruct((3, rows, d), bf16),
        compiler_params=params(2),
        cost_estimate=cost(
            seqs * H * 2 * BAND * BQ * 2 * 256 * 2, 2 * 7 * rows * d + 4 * seqs * H * BAND * BQ
        ),
        name="attend_back",
    )(qkv, qkv, qkv, dattn, probs)


def row_of(i):
    return pl.BlockSpec((1, 1, 768), lambda *_: (i, 0, 0))


def out_step(a_ref, w, t_ref, bo_ref, g_ref, s_ref, mid_ref, sec_ref):
    mid = t_ref[...].astype(f32) + nn(a_ref[...], w) + bo_ref[0]
    mid_ref[...] = mid
    sc, _ = moments(mid)
    sec_ref[...] = (sc * g_ref[0] + s_ref[0]).astype(bf16)


def out_kernel(a_ref, w_ref, t_ref, bo_ref, g_ref, s_ref, mid_ref, sec_ref):
    out_step(a_ref, w_ref[0], t_ref, bo_ref, g_ref, s_ref, mid_ref, sec_ref)


def out_fast_kernel(place, a_ref, t_ref, bo_ref, g_ref, s_ref, *refs):
    pieces, (mid_ref, sec_ref, w_ref, sem) = refs[:8], refs[8:]

    @pl.when(pl.program_id(0) == 0)
    def _():
        wait_all(start_all(row_copies(place, pieces, w_ref, 8, w_ref.shape[1] // 8), sem))

    out_step(a_ref, w_ref[0], t_ref, bo_ref, g_ref, s_ref, mid_ref, sec_ref)


def out_fast_call(place, attended, tokens, table, pieces):
    rows, d = tokens.shape
    blk = pl.BlockSpec((256, d), lambda i, place: (i, 0))
    return pl.pallas_call(
        out_fast_kernel,
        grid_spec=pltpu.PrefetchScalarGridSpec(
            num_scalar_prefetch=1,
            grid=(rows // 256,),
            in_specs=[blk, blk, row_of(OUT), row_of(GAIN_TWO), row_of(SHIFT_TWO)] + [ANY] * 8,
            out_specs=[blk, blk, pl.BlockSpec((1, d, d), lambda i, place: (0, 0, 0))],
            scratch_shapes=[pltpu.SemaphoreType.DMA],
        ),
        out_shape=[
            jax.ShapeDtypeStruct((rows, d), f32),
            jax.ShapeDtypeStruct((rows, d), bf16),
            jax.ShapeDtypeStruct((1, d, d), bf16),
        ],
        compiler_params=params(1),
        cost_estimate=cost(2 * rows * d * d, rows * d * 10 + 4 * d * d),
        name="project",
    )(place, attended, tokens, table, table, table, *pieces)


def out_call(attended, wo, tokens, table):
    rows, d = tokens.shape
    blk = pl.BlockSpec((256, d), lambda i: (i, 0))
    return pl.pallas_call(
        out_kernel,
        grid=(rows // 256,),
        in_specs=[
            blk, pl.BlockSpec((1, d, d), lambda i: (3, 0, 0)), blk,
            row_of(OUT), row_of(GAIN_TWO), row_of(SHIFT_TWO),
        ],
        out_specs=[blk, blk],
        out_shape=[
            jax.ShapeDtypeStruct((rows, d), f32),
            jax.ShapeDtypeStruct((rows, d), bf16),
        ],
        compiler_params=params(1),
        cost_estimate=cost(2 * rows * d * d, rows * d * 10 + 2 * d * d),
        name="project",
    )(attended, wo, tokens, table, table, table)


def ffn_step(x_ref, g_ref, wu, wd, b, acc_ref, sg_ref, act, hg):
    rows = x_ref.shape[0]
    chunk = 256
    total = jnp.zeros((1, wu.shape[1]), f32)
    def step(r, total):
        at = pl.ds(pl.multiple_of(r * chunk, chunk), chunk)
        h = nn(x_ref[at, :], wu[...]) + b
        ag = nt(g_ref[at, :], wd[...])
        phi = 0.5 + 0.5 * lax.erf(h * (0.5**0.5))
        a = (h * phi).astype(bf16)
        act[at, :] = a
        dens = jnp.exp(-0.5 * (h * h)) * 0.3989422804014327
        hgv = (ag * (phi + h * dens)).astype(bf16)
        hg[at, :] = hgv
        acc_ref[at, :] += nn(a, wd[...])
        sg_ref[at, :] += nt(hgv, wu[...])
        return total + jnp.sum(hgv.astype(f32), axis=0, keepdims=True)

    return lax.fori_loop(0, rows // chunk, step, total)


def ffn_start(start, acc_in, bd_ref, sg_in, acc_ref, sg_ref):
    if start:
        acc_ref[...] = acc_in[...] + bd_ref[0]
        sg_ref[...] = jnp.zeros_like(sg_ref)
    else:
        acc_ref[...] = acc_in[...]
        sg_ref[...] = sg_in[...]


def ffn_kernel(start, x_ref, g_ref, w_ref, b_ref, acc_in, bd_ref, *refs):
    sg_in = None if start else refs[0]
    gw_ref, gb_ref, acc_ref, sg_ref, act, hg = refs[0 if start else 1 :]

    @pl.when(pl.program_id(0) == 0)
    def _():
        ffn_start(start, acc_in, bd_ref, sg_in, acc_ref, sg_ref)

    gb_ref[0] = ffn_step(x_ref, g_ref, w_ref.at[0], w_ref.at[1], b_ref[0], acc_ref, sg_ref, act, hg)
    gw_ref[0] = tn(x_ref[...], hg[...]).astype(bf16)
    gw_ref[1] = tn(act[...], g_ref[...]).astype(bf16)


def ffn_call(lead, second, dgrad, w, table, acc, sg):
    rows, d = second.shape
    n = w.shape[0] // 2
    start = sg is None
    full = pl.BlockSpec((rows, d), lambda j: (0, 0))
    pair = pl.BlockSpec((2, d, d), lambda j: (j, 0, 0))
    return pl.pallas_call(
        partial(ffn_kernel, start),
        grid=(n,),
        in_specs=[
            full, full, pair, pl.BlockSpec((1, 1, d), lambda j: (UP + lead * n + j, 0, 0)),
            full, row_of(DOWN),
        ]
        + ([] if start else [full]),
        out_specs=[pair, pl.BlockSpec((1, 1, d), lambda j: (j, 0, 0)), full, full],
        out_shape=[
            jax.ShapeDtypeStruct((2 * n, d, d), bf16),
            jax.ShapeDtypeStruct((n, 1, d), f32),
            jax.ShapeDtypeStruct((rows, d), f32),
            jax.ShapeDtypeStruct((rows, d), f32),
        ],
        scratch_shapes=[pltpu.VMEM((rows, d), bf16)] * 2,
        compiler_params=params(1),
        cost_estimate=cost(12 * n * rows * d * d, 20 * rows * d + 8 * n * d * d),
        name="feed",
    )(second, dgrad, w, table, acc, table, *([] if start else [sg]))


def ffn_fast_kernel(start, lead, place, x_ref, g_ref, b_ref, acc_in, bd_ref, *refs):
    sg_in, vec_in = (None, None) if start else refs[:2]
    refs = refs[0 if start else 2 :]
    pieces = refs[:8]
    keep, send, vec_ref, acc_ref, sg_ref, w_ref, act, hg, full, sem = refs[8:]
    j = pl.program_id(0)

    @pl.when(j == 0)
    def _():
        copies = start_all(block_copies(place, pieces, w_ref, lead), sem)
        ffn_start(start, acc_in, bd_ref, sg_in, acc_ref, sg_ref)
        vec_ref[...] = jnp.zeros_like(vec_ref) if start else vec_in[...]
        wait_all(copies)

    wu, wd = w_ref.at[2 * j], w_ref.at[2 * j + 1]
    total = ffn_step(x_ref, g_ref, wu, wd, b_ref[0], acc_ref, sg_ref, act, hg)
    vec_ref[pl.ds(2 * lead + j, 1), :] = total
    full[...] = tn(x_ref[...], hg[...]).astype(bf16)
    split_blocks(place, full, keep, send, 0)
    full[...] = tn(act[...], g_ref[...]).astype(bf16)
    split_blocks(place, full, keep, send, 1)


def ffn_fast_call(lead, place, second, dgrad, table, acc, sg, vec, pieces):
    rows, d = second.shape
    start = sg is None
    m = d // 8
    full = pl.BlockSpec((rows, d), lambda j, place: (0, 0))
    half = pl.BlockSpec((2, 4, m, d), lambda j, place: (j, 0, 0, 0))
    rows_of_table = pl.BlockSpec((8, d), lambda j, place: (0, 0))
    return pl.pallas_call(
        partial(ffn_fast_kernel, start, lead),
        grid_spec=pltpu.PrefetchScalarGridSpec(
            num_scalar_prefetch=1,
            grid=(2,),
            in_specs=[
                full, full, pl.BlockSpec((1, 1, d), lambda j, place: (UP + lead * 2 + j, 0, 0)),
                full, row_of(DOWN),
            ]
            + ([] if start else [full, rows_of_table])
            + [ANY] * 8,
            out_specs=[half, half, rows_of_table, full, full],
            scratch_shapes=[pltpu.VMEM((4, d, d), bf16)]
            + [pltpu.VMEM((rows, d), bf16)] * 2
            + [pltpu.VMEM((d, d), bf16), pltpu.SemaphoreType.DMA],
        ),
        out_shape=[
            jax.ShapeDtypeStruct((4, 4, m, d), bf16),
            jax.ShapeDtypeStruct((4, 4, m, d), bf16),
            jax.ShapeDtypeStruct((8, d), f32),
            jax.ShapeDtypeStruct((rows, d), f32),
            jax.ShapeDtypeStruct((rows, d), f32),
        ],
        compiler_params=params(1),
        cost_estimate=cost(24 * rows * d * d, 20 * rows * d + 16 * d * d),
        name="feed",
    )(place, second, dgrad, table, acc, table, *([] if start else [sg, vec]), *pieces)


def norm_back(grad, sc, inv, gain):
    t = grad * gain
    return inv * (
        t - jnp.mean(t, axis=-1, keepdims=True) - sc * jnp.mean(t * sc, axis=-1, keepdims=True)
    )


def mid_kernel(
    place, sg_ref, mid_ref, dy_ref, a_ref, w_ref, g_ref, acc_ref, vec_in,
    mg_ref, ag_ref, vec_ref, lo_ref, wg_ref, *rest,
):
    i = pl.program_id(0)
    wacc = rest[-1]

    @pl.when(i == 0)
    def _():
        wacc[...] = jnp.zeros_like(wacc)
        vec_ref[...] = vec_in[...]

    lo_ref[...] = acc_ref[...].astype(bf16)
    sc, inv = moments(mid_ref[...])
    sg = sg_ref[...]
    dy = dy_ref[...].astype(f32)
    mg = dy + norm_back(sg, sc, inv, g_ref[0])
    mg_ref[...] = mg
    br = mg.astype(bf16)
    vec_ref[4:5, :] += jnp.sum(sg * sc, axis=0, keepdims=True)
    vec_ref[5:6, :] += jnp.sum(sg, axis=0, keepdims=True)
    vec_ref[6:7, :] += jnp.sum(br.astype(f32), axis=0, keepdims=True)
    vec_ref[7:8, :] += jnp.sum(dy, axis=0, keepdims=True)
    ag_ref[...] = nt(br, w_ref[0]).astype(bf16)
    wacc[...] += tn(a_ref[...], br)

    @pl.when(i == pl.num_programs(0) - 1)
    def _():
        if len(rest) == 1:
            wg_ref[0] = wacc[...].astype(bf16)
        else:
            split_blocks(place, wacc, wg_ref, rest[0], 0)


def mid_call(place, sg, mid, dy, attended, wo, table, acc, vec, split):
    rows, d = sg.shape
    blk = pl.BlockSpec((256, d), lambda i, place: (i, 0))
    grad = (1, 4, d // 8, d) if split else (1, d, d)
    last = wo.shape[0] - 1
    return pl.pallas_call(
        mid_kernel,
        grid_spec=pltpu.PrefetchScalarGridSpec(
            num_scalar_prefetch=1,
            grid=(rows // 256,),
            in_specs=[
                blk, blk, blk, blk, pl.BlockSpec((1, d, d), lambda i, place: (last, 0, 0)),
                row_of(GAIN_TWO), blk, pl.BlockSpec((8, d), lambda i, place: (0, 0)),
            ],
            out_specs=[blk, blk, pl.BlockSpec((8, d), lambda i, place: (0, 0)), blk]
            + [pl.BlockSpec(grad, lambda i, place: (0,) * len(grad))] * (2 if split else 1),
            scratch_shapes=[pltpu.VMEM((d, d), f32)],
        ),
        out_shape=[
            jax.ShapeDtypeStruct((rows, d), f32),
            jax.ShapeDtypeStruct((rows, d), bf16),
            jax.ShapeDtypeStruct((8, d), f32),
            jax.ShapeDtypeStruct((rows, d), bf16),
        ]
        + [jax.ShapeDtypeStruct(grad, bf16)] * (2 if split else 1),
        compiler_params=params(1),
        cost_estimate=cost(4 * rows * d * d, rows * d * 22 + 4 * d * d),
        name="middle_back",
    )(place, sg, mid, dy, attended, wo, table, acc, vec)


def wgrad_kernel(x_ref, g_ref, o_ref, b_ref):
    o_ref[0] = tn(x_ref[...], g_ref[0]).astype(bf16)
    b_ref[0] = jnp.sum(g_ref[0].astype(f32), axis=0, keepdims=True)


def wgrad_call(first, grads):
    rows, d = first.shape
    return pl.pallas_call(
        wgrad_kernel,
        grid=(3,),
        in_specs=[
            pl.BlockSpec((rows, d), lambda i: (0, 0)),
            pl.BlockSpec((1, rows, d), lambda i: (i, 0, 0)),
        ],
        out_specs=[
            pl.BlockSpec((1, d, d), lambda i: (i, 0, 0)),
            pl.BlockSpec((1, 1, d), lambda i: (i, 0, 0)),
        ],
        out_shape=[
            jax.ShapeDtypeStruct((3, d, d), bf16),
            jax.ShapeDtypeStruct((3, 1, d), f32),
        ],
        compiler_params=params(1),
        cost_estimate=cost(6 * rows * d * d, 2 * (rows * d * 4 + 3 * d * d)),
        name="weight_back",
    )(first, grads)


def wgrad_fast_kernel(place, x_ref, g_ref, vec_in, keep, send, vec_ref, full):
    i = pl.program_id(0)

    @pl.when(i == 0)
    def _():
        vec_ref[:8, :] = vec_in[...]
        vec_ref[8:, :] = jnp.zeros_like(vec_in)

    full[...] = tn(x_ref[...], g_ref[0])
    vec_ref[pl.ds(8 + i, 1), :] = jnp.sum(g_ref[0].astype(f32), axis=0, keepdims=True)
    split_blocks(place, full, keep, send, 0)


def wgrad_fast_call(place, first, grads, vec):
    rows, d = first.shape
    m = d // 8
    half = pl.BlockSpec((1, 4, m, d), lambda i, place: (i, 0, 0, 0))
    return pl.pallas_call(
        wgrad_fast_kernel,
        grid_spec=pltpu.PrefetchScalarGridSpec(
            num_scalar_prefetch=1,
            grid=(3,),
            in_specs=[
                pl.BlockSpec((rows, d), lambda i, place: (0, 0)),
                pl.BlockSpec((1, rows, d), lambda i, place: (i, 0, 0)),
                pl.BlockSpec((8, d), lambda i, place: (0, 0)),
            ],
            out_specs=[half, half, pl.BlockSpec((16, d), lambda i, place: (0, 0))],
            scratch_shapes=[pltpu.VMEM((d, d), f32)],
        ),
        out_shape=[
            jax.ShapeDtypeStruct((3, 4, m, d), bf16),
            jax.ShapeDtypeStruct((3, 4, m, d), bf16),
            jax.ShapeDtypeStruct((16, d), f32),
        ],
        compiler_params=params(1),
        cost_estimate=cost(6 * rows * d * d, 2 * (rows * d * 4 + 3 * d * d)),
        name="weight_back",
    )(place, first, grads, vec)


def input_kernel(start, g_ref, w_ref, t_ref, mg_ref, gain_ref, *refs):
    o_ref, vec_ref = refs[-2:]

    @pl.when(pl.program_id(0) == 0)
    def _():
        vec_ref[...] = jnp.zeros_like(vec_ref) if start else refs[0][...]

    fg = nt(g_ref[0], w_ref[0]) + nt(g_ref[1], w_ref[1]) + nt(g_ref[2], w_ref[2])
    sc, inv = moments(t_ref[...].astype(f32))
    o_ref[...] = (mg_ref[...] + norm_back(fg, sc, inv, gain_ref[0])).astype(bf16)
    vec_ref[0:1, :] += jnp.sum(fg * sc, axis=0, keepdims=True)
    vec_ref[1:2, :] += jnp.sum(fg, axis=0, keepdims=True)


def input_call(grads, w, tokens, mg, table, skip, steps, before=()):
    rows, d = tokens.shape
    blk = pl.BlockSpec((256, d), lambda i: (skip + i, 0))
    vec = pl.BlockSpec((8, d), lambda i: (0, 0))
    start = not before
    return pl.pallas_call(
        partial(input_kernel, start),
        grid=(steps,),
        in_specs=[
            pl.BlockSpec((3, 256, d), lambda i: (0, skip + i, 0)),
            pl.BlockSpec((3, d, d), lambda i: (0, 0, 0)),
            blk,
            blk,
            row_of(GAIN_ONE),
        ]
        + ([] if start else [vec, ANY]),
        out_specs=[blk, vec],
        out_shape=[
            jax.ShapeDtypeStruct((rows, d), bf16),
            jax.ShapeDtypeStruct((8, d), f32),
        ],
        input_output_aliases={} if start else {6: 0},
        compiler_params=params(1),
        cost_estimate=cost(1536 * steps * d * d, 256 * steps * d * 14 + 6 * d * d),
        name="input_back",
    )(grads, w, tokens, mg, table, *([] if start else [before[1], before[0]]))


def finish_kernel(factor, order, x_ref, up_ref, down_ref, out_ref):
    n = up_ref.shape[0]
    few = n // 4
    for b in range(4):
        x = x_ref[order[b]].astype(f32) * factor
        out_ref[b * few : (b + 1) * few, :] = x[2 * n :]
        for half in range(2):
            block, p = x[half * n : (half + 1) * n], 2 * half + b // 2
            if b % 2:
                down_ref[p * n : (p + 1) * n, :] = block
            else:
                for s in range(8):
                    to = s * 4 * n + p * n
                    up_ref[:, to : to + n] = block[:, s * n : (s + 1) * n]


def finish_call(order, final, factor):
    n, d = final.shape[1] * 4 // 9, final.shape[2]
    full = lambda *shape: pl.BlockSpec(shape, lambda i, order: (0,) * len(shape))
    return pl.pallas_call(
        partial(finish_kernel, factor),
        grid_spec=pltpu.PrefetchScalarGridSpec(
            num_scalar_prefetch=1,
            grid=(1,),
            in_specs=[full(*final.shape)],
            out_specs=[full(n, 4 * d), full(4 * n, d), full(n, d)],
        ),
        out_shape=[
            jax.ShapeDtypeStruct((n, 4 * d), f32),
            jax.ShapeDtypeStruct((4 * n, d), f32),
            jax.ShapeDtypeStruct((n, d), f32),
        ],
        compiler_params=params(1),
        name="finish",
    )(order, final)


CORE = 1
ALONG = (2, 4, 6)
GROUP = (8, 16, 24)


def hop(x, mask):
    return lax.ppermute(x, ("dp", "fsdp"), [(i, i ^ mask) for i in range(32)])


def group_hop(x, second):
    pairs = [(i, i ^ (GROUP[0] if i % 2 == second else GROUP[1])) for i in range(32)]
    return lax.ppermute(x, ("dp", "fsdp"), pairs)


def pick(x, index, axis=0):
    return lax.dynamic_index_in_dim(x, index, axis, keepdims=False)


def after(deps, *xs):
    return lax.optimization_barrier((*xs, *deps))[: len(xs)]


def wide(x):
    return x.astype(f32)


def add_core(keep, got):
    return (wide(keep) + wide(got)).astype(bf16)


def quarter(x, index, axis):
    n = x.shape[axis] // 4
    return lax.dynamic_slice_in_dim(x, index * n, n, axis)


def add_two(a, b):
    return (wide(a) + wide(b)).astype(bf16)


def turn(x, bits):
    for axis, bit in enumerate(bits):
        x = jnp.where(bit == 0, x, jnp.flip(x, axis))
    return x


def add_all(first, others):
    total = wide(first)
    for other in others:
        total = total + wide(other)
    return total.astype(bf16)


def segment_ids(lengths):
    ends = jnp.cumsum(lengths, axis=-1)
    places = jnp.arange(SEQ, dtype=jnp.int32)
    return jnp.sum((places[None, :, None] >= ends[:, None, :]).astype(jnp.int32), axis=-1)


def pack_vectors(pre_gain, pre_shift, bias_query, bias_value, bias_out, mid_gain, mid_shift, bias_up, bias_down):
    none = jnp.zeros_like(bias_query)
    return jnp.concatenate(
        [pre_gain, pre_shift, bias_query, none, bias_value, bias_out, mid_gain, mid_shift, bias_down, bias_up]
    )[None]


def make_table(small):
    shards = small.shape[0]
    n = small.shape[1] * shards // 768
    return small.reshape(shards, n, -1).transpose(1, 0, 2).reshape(n, 1, 768).astype(f32)


def order_hidden(w_up, w_down, shards):
    m, d = w_up.shape[0], w_up.shape[0] * shards
    parts = w_down.shape[0] // m
    up = w_up.reshape(m, shards, parts, m).transpose(2, 0, 1, 3).reshape(parts, m, d)
    return jnp.stack([up, w_down.reshape(parts, m, d)], 1).reshape(2 * parts, m, d)


VEC_ROWS = (0, 1, 16, 18, 10, 8, 9)
DOWN_ROW, UP_ROW = 11, 20


def outputs(layer_out, input_grad, attn, feed, vec, factor, shards):
    m, d = attn[0].shape
    parts = len(feed) // 2
    vec = vec * factor
    up = jnp.stack(feed[0::2]).reshape(parts, m, shards, m).transpose(1, 2, 0, 3)
    return (
        layer_out,
        input_grad,
        *(wide(g) * factor for g in attn),
        wide(up.reshape(m, parts * d)) * factor,
        wide(jnp.concatenate(feed[1::2])) * factor,
        *(vec[i] for i in VEC_ROWS),
        vec[UP_ROW:].reshape(-1),
        vec[DOWN_ROW],
    )


def body_fast(tokens, cotangent, doc_lengths, w_query, w_key, w_value, w_out, w_up, w_down, *vectors):
    rows, d = tokens.shape
    n = d // 8
    dp, at = lax.axis_index("dp"), lax.axis_index("fsdp")
    z, core = at // 2, at % 2
    place = jnp.stack([dp, z, core]).astype(jnp.int32)
    one, two = 1 + core, 2 - core

    quarters = [quarter(w, dp, 0) for w in (w_query, w_key, w_value, w_out)]
    attn_mine = jnp.concatenate(quarters[:3])
    attn_z = [hop(attn_mine, m) for m in ALONG]
    attn_along = jnp.stack(attn_z)
    attn_near = group_hop(attn_along, 0)
    attn_own = jnp.stack([w_query, w_key, w_value])
    attn_own_cross = hop(attn_own, CORE)
    small = pack_vectors(*after([attn_along], *vectors))
    width = small.shape[1]
    low = jnp.pad(small[0], (0, 8 * d - width)).reshape(8, d)
    low = jnp.concatenate([low, hop(low, CORE)])
    attn_far = jnp.stack([attn_along, attn_near])
    (low,) = after([attn_far], low)
    low_across = hop(low, ALONG[1])
    low_beside = hop(jnp.stack([low, low_across]), ALONG[0])
    lows = jnp.stack([low, low_beside[0], low_across, low_beside[1]])
    small = lows.reshape(2, 2, 2, 8 * d)[..., :width]
    table = make_table(turn(small, (z // 2, z % 2, core)).reshape(8, width))
    attn_along_cross = hop(attn_along, CORE)
    attn_far = group_hop(attn_far, 1)
    attn_near_cross = hop(attn_near, CORE)
    attn_far_cross = hop(attn_far, CORE)

    feed_own = order_hidden(w_up, w_down, 8)
    mine_one = jnp.concatenate([pick(feed_own[:4], dp), quarters[3]])
    tokens_late, lengths_late, mine_one = after([attn_along], tokens, doc_lengths, mine_one)
    mine_two = pick(feed_own[4:], dp)
    feed_own = jnp.concatenate([feed_own, w_out[None]])
    across_one = hop(mine_one, ALONG[1])
    mine_late, across_late = after([attn_near], mine_one, across_one)
    beside_one = hop(jnp.stack([mine_late, across_late]), ALONG[0])
    beside_one, mine_two = after([attn_far], beside_one, mine_two)
    along_one = jnp.stack([beside_one[0], across_one, beside_one[1]])
    near_one = group_hop(along_one, 0)
    across_two = hop(mine_two, ALONG[1])

    doc = segment_ids(lengths_late)
    scaled, _ = moments(wide(tokens_late))
    first = (scaled * table[GAIN_ONE] + table[SHIFT_ONE]).astype(bf16)
    qkv, attn_w = qkv_fast_call(
        place, first, table,
        [attn_own, attn_along, attn_near, attn_far]
        + [attn_own_cross, attn_along_cross, attn_near_cross, attn_far_cross],
    )
    feed_own_late, along_one, near_one, mine_two, across_two = after(
        [qkv], feed_own, along_one, near_one, mine_two, across_two
    )
    (qkv,) = after([near_one, across_two], qkv)
    far_one = group_hop(jnp.stack([along_one, near_one]), 1)
    beside_two = hop(jnp.stack([mine_two, across_two]), ALONG[0])
    feed_cross = hop(feed_own_late, CORE)
    pieces_one = [feed_cross, hop(along_one, CORE), hop(near_one, CORE)]
    attended, probs = attn_fwd_call(qkv, doc)
    far_one, beside_two, attended_late = after([attended], far_one, beside_two, attended)
    (attended_late,) = after([far_one, beside_two], attended_late)
    pieces_one = [feed_own, along_one, near_one, far_one, *pieces_one, hop(far_one, CORE)]
    along_two = jnp.stack([beside_two[0], across_two, beside_two[1]])
    near_two = group_hop(along_two, 0)
    middle, second, wo = out_fast_call(place, attended_late, tokens, table, pieces_one)
    along_two, near_two, second = after([middle], along_two, near_two, second)
    (second,) = after([near_two], second)
    far_two = group_hop(jnp.stack([along_two, near_two]), 1)
    pieces_two = [along_two, near_two, far_two]
    pieces_two = [feed_own, *pieces_two, feed_cross, *(hop(x, CORE) for x in pieces_two)]

    def first_hop(parts):
        return group_hop(jnp.stack([parts(dp ^ one), parts(dp ^ 3)]), 0)

    def fold(parts, got):
        return add_two(parts(dp), got[0]), add_two(parts(dp ^ two), got[1])

    def beside(x):
        return jnp.stack([pick(x, z ^ 1), pick(x, z ^ 3)])

    def across(x, got):
        return add_two(pick(x, z), got[0]), add_two(pick(x, z ^ 2), got[1])

    keep_one, send_one, vec, acc, sg = ffn_fast_call(
        0, place, second, cotangent, table, middle, None, None, pieces_one
    )
    (send_one,) = after([far_two], send_one)
    got_one = hop(send_one, CORE)
    parts_one = lambda i: add_two(pick(keep_one, i), pick(got_one, i))
    near_one = first_hop(parts_one)
    (sg,) = after([got_one], sg)
    keep_two, send_two, vec, acc, sg = ffn_fast_call(
        1, place, second, cotangent, table, acc, sg, vec, pieces_two
    )
    got_two = hop(send_two, CORE)
    (sg,) = after([near_one], sg)
    mine_one, far_one = fold(parts_one, near_one)
    (sg,) = after([far_one], sg)
    far_one = group_hop(far_one, 1)
    mid_grad, attended_grad, vec, layer_out, keep_out, send_out = mid_call(
        place, sg, middle, cotangent, attended, wo, table, acc, vec, True
    )
    got_out = hop(send_out, CORE)
    (attended_grad,) = after([far_one, got_two, got_out], attended_grad)
    sum_one = add_two(mine_one, far_one)
    beside_one = hop(beside(sum_one), ALONG[0])

    def parts_two(i):
        out = add_two(quarter(keep_out[0], i, 1), quarter(got_out[0], i, 1))
        return jnp.concatenate([add_two(pick(keep_two, i), pick(got_two, i)), out], 1)

    near_two = first_hop(parts_two)
    grads = attn_bwd_call(qkv, attended_grad, probs)
    (beside_one,) = after([grads], beside_one)
    mine_one, across_one = across(sum_one, beside_one)
    mine_two, far_two = fold(parts_two, near_two)
    (grads,) = after([across_one, far_two], grads)
    across_one = hop(across_one, ALONG[1])
    far_two = group_hop(far_two, 1)
    keep_attn, send_attn, vec = wgrad_fast_call(place, first, grads, vec)
    (send_attn,) = after([across_one, far_two], send_attn)
    got_attn = hop(send_attn, CORE)
    sum_two = add_two(mine_two, far_two)
    beside_two = beside(sum_two)
    (got_attn,) = after([beside_two], got_attn)
    parts_attn = lambda i: add_two(quarter(keep_attn, i, 2), quarter(got_attn, i, 2))
    near_attn = jnp.stack([parts_attn(dp ^ one), parts_attn(dp ^ 3)])
    (grads,) = after([beside_two, near_attn], grads)
    beside_two = hop(beside_two, ALONG[0])
    near_attn = group_hop(near_attn, 0)
    input_grad, in_vec = input_call(grads, attn_w, tokens, mid_grad, table, 0, rows // 256)
    near_attn, beside_two = after([in_vec], near_attn, beside_two)
    mine_attn, far_attn = fold(parts_attn, near_attn)
    mine_two, across_two = across(sum_two, beside_two)
    mine_one, across_one, in_vec, vec = after([far_attn], mine_one, across_one, in_vec, vec)
    far_attn = group_hop(far_attn, 1)
    across_two = hop(across_two, ALONG[1])

    in_vec = in_vec[:2] + hop(in_vec[:2], CORE)
    vec = vec.reshape(16, 4, 2, n).transpose(2, 1, 0, 3)
    vec = pick(vec, core) + hop(pick(vec, 1 - core), CORE)
    vec = vec.reshape(4, 16 * n // d, d).astype(bf16)
    low = jnp.concatenate(
        [vec, jnp.broadcast_to(in_vec.astype(bf16)[None], (4, 2, d)), jnp.zeros((4, 4, d), bf16)], 1
    )
    far_attn, low = after((), far_attn, low)
    attn_sum = add_two(mine_attn, far_attn)
    many = 3 * attn_sum.shape[2]
    rest = attn_sum.transpose(1, 0, 2, 3).reshape(4, many, d)
    rest = jnp.concatenate([rest, low], 1)
    beside_rest = beside(rest)
    (across_two,) = after([beside_rest], across_two)
    beside_rest = hop(beside_rest, ALONG[0])
    final_feed = jnp.concatenate([add_two(mine_one, across_one), add_two(mine_two, across_two)])
    feed_near = group_hop(final_feed, 0)
    mine_rest, across_rest = across(rest, beside_rest)
    final_feed, feed_near = after([across_rest], final_feed, feed_near)
    feed_far = group_hop(jnp.stack([final_feed, feed_near]), 1)
    final_rest = add_two(mine_rest, hop(across_rest, ALONG[1]))
    (final_rest,) = after([feed_far], final_rest)
    final_rest = jnp.stack([final_rest] + [hop(final_rest, m) for m in GROUP])
    vec = jnp.sum(wide(final_rest[:, many : many + 4]), axis=0)
    in_vec = lax.dynamic_slice_in_dim(vec[2:], at * n, n, 1)
    vec = vec[:2].reshape(16, n)
    none = jnp.zeros((6, n), f32)
    vec = jnp.concatenate([in_vec, none, vec[4:8], none[:4], vec[8:12], vec[:4]])
    final_feed = jnp.stack([final_feed, feed_near, feed_far[0], feed_far[1]])
    order = lambda b: jnp.where(b == one, 1, jnp.where(b == two, 2, b))
    final_attn = [pick(final_rest, dp ^ b)[:many].reshape(3, many // 3, d) for b in range(4)]
    factor = (32 * rows) ** (-0.5)
    members = jnp.stack([order(dp ^ b) for b in range(4)]).astype(jnp.int32)
    up, down, out = finish_call(members, final_feed, factor)
    vec = vec * factor
    return (
        layer_out,
        input_grad,
        *(wide(jnp.concatenate([x[i] for x in final_attn])) * factor for i in range(3)),
        out,
        up,
        down,
        *(vec[i] for i in VEC_ROWS),
        vec[UP_ROW:].reshape(-1),
        vec[DOWN_ROW],
    )


def gather(local):
    return lax.all_gather(local, "fsdp", axis=1, tiled=True)


def reduce(grad):
    part = lax.psum_scatter(wide(grad), "fsdp", scatter_dimension=1, tiled=True)
    total = lax.psum(part.astype(bf16), "dp")
    return [total[b] for b in range(grad.shape[0])]


def body_plain(tokens, cotangent, doc_lengths, w_query, w_key, w_value, w_out, w_up, w_down, *vectors):
    rows = tokens.shape[0]
    shards, groups = lax.axis_size("fsdp"), lax.axis_size("dp")
    table = make_table(lax.all_gather(pack_vectors(*vectors), "fsdp", axis=0, tiled=True))
    attn_w = gather(jnp.stack([w_query, w_key, w_value, w_out]))
    feed_own = order_hidden(w_up, w_down, shards)
    doc = segment_ids(doc_lengths)
    scaled, _ = moments(wide(tokens))
    first = (scaled * table[GAIN_ONE] + table[SHIFT_ONE]).astype(bf16)
    qkv = qkv_call(first, attn_w, table)
    attended, probs = attn_fwd_call(qkv, doc)
    middle, second = out_call(attended, attn_w, tokens, table)
    acc, sg = middle, None
    feed = []
    up_bias = []
    for lead in range(feed_own.shape[0] // 4):
        w = gather(feed_own[4 * lead : 4 * lead + 4])
        grad, bias_grad, acc, sg = ffn_call(lead, second, cotangent, w, table, acc, sg)
        feed += reduce(grad)
        up_bias.append(bias_grad)
    mid_grad, attended_grad, mid_vec, layer_out, out_grad = mid_call(
        jnp.zeros((3,), jnp.int32), sg, middle, cotangent, attended, attn_w, table, acc,
        jnp.zeros((8, tokens.shape[1]), f32), False,
    )
    grads = attn_bwd_call(qkv, attended_grad, probs)
    proj_grad, proj_bias = wgrad_call(first, grads)
    input_grad, in_vec = input_call(grads, attn_w, tokens, mid_grad, table, 0, tokens.shape[0] // 256)
    attn = reduce(jnp.concatenate([proj_grad, out_grad]))
    none = jnp.zeros((1,) + proj_bias.shape[2:], f32)
    mid_vec = jnp.roll(mid_vec, 4, 0)
    vec = jnp.concatenate([in_vec, mid_vec, proj_bias[:, 0], none] + [x[:, 0] for x in up_bias])
    vec = vec.reshape(vec.shape[0], shards, -1).transpose(1, 0, 2)
    vec = lax.psum(lax.psum_scatter(vec, "fsdp", scatter_dimension=0, tiled=True), "dp")[0]
    factor = (groups * shards * rows) ** (-0.5)
    return outputs(layer_out, input_grad, attn, feed, vec, factor, shards)


def solution(mesh):
    both = P(("dp", "fsdp"), None)
    matrix, vector = P("fsdp", None), P("fsdp")
    fast = mesh.shape["dp"] == 4 and mesh.shape["fsdp"] == 8
    return jax.shard_map(
        body_fast if fast else body_plain,
        mesh=mesh,
        in_specs=(both,) * 3 + (matrix,) * 6 + (vector,) * 9,
        out_specs=(both,) * 2 + (matrix,) * 6 + (vector,) * 9,
        check_vma=False,
    )
```
